128 devices in a mesh: ctx: 16 (over x_hi, y, core), tp: 8 (over z, x_lo).
Axes of the slice: x: 4 (x_hi: 2, x_lo: 2; x = x_hi * 2 + x_lo), y: 4, z: 4, core: 2. Of those that a mesh axis runs over, the one named last changes fastest.
Arguments:
- residual_in: bfloat16 [2, 4096, 4096], P(None, 'ctx', 'tp'), may hold values from -6 to 6
- mr_qkv: bfloat16 [2, 4096, 3, 4096], P(None, 'ctx', None, 'tp'), may hold values from -6 to 6
- mr_short_w: float32 [3, 3, 4096], P(None, None, 'tp'), may hold values from -3.5 to 3.5
- mr_filter: bfloat16 [128, 4096], P(None, 'tp'), may hold values from -0.5 to 0.5
- mr_skip: float32 [4096], P('tp'), may hold values from -4 to 4
- mr_out_w: bfloat16 [4096, 4096], P('tp', 'ctx'), may hold values from -0.09375 to 0.09375
- lr_gain: float32 [4096], replicated, may hold values from 0.1 to 1.9
- lr_in_w: bfloat16 [4096, 3, 4096], P(None, None, 'tp'), may hold values from -0.09375 to 0.09375
- lr_short_w: float32 [3, 3, 4096], P(None, None, 'tp'), may hold values from -3.5 to 3.5
- lr_rate: float32 [16, 4096], P(None, 'tp'), may hold values from 0 to 1, as said below
- lr_res: float32 [16, 4096], P(None, 'tp'), may hold values from -3 to 3
- lr_skip: float32 [4096], P('tp'), may hold values from -4 to 4
- lr_out_w: bfloat16 [4096, 4096], P('tp', 'ctx'), may hold values from -0.09375 to 0.09375
Outputs:
- residual_out: bfloat16 [2, 4096, 4096], P(None, 'ctx', 'tp')
The draws below stay inside these ranges and needn't reach their ends.
Inputs may be any that keep to these rules, and one draw needn't show every extreme that they name: `lr_rate`: each rate lies between 0.1 / 4096 and 1 / 20.
All inputs are finite; a program needn't handle non-finite values.
Results may differ from the reference program's by a relative error of at most 0.034.
Values may be sent and summed in bfloat16 or wider, within the bound.
A program may use at most 192 MiB of HBM per device.

```python
import math
import jax
import jax.numpy as jnp
from jax import lax

D = 4096
MR_TAPS = 128
STATE = 16
SHORT = 3
SEQS = 2
LENGTH = 4096
N_TP = 8


def draw_lr_rate(key, part):
    lowest = math.log(0.1 / LENGTH)
    return jnp.exp(jax.random.uniform(key, (STATE, D), jnp.float32, lowest, math.log(1.0 / 30.0))).astype(jnp.float32)


def level_of(rng, dims, cuts, smallest, largest):
    def one(position, parts):
        heights = jax.random.uniform(jax.random.fold_in(jax.random.fold_in(rng, 6), position), (parts,), jnp.float32, smallest / len(cuts), largest / len(cuts))
        return jnp.repeat(jnp.exp(heights), dims[position] // parts).reshape((-1,) + (1,) * (len(dims) - position - 1))

    level = one(*cuts[0])
    for cut in cuts[1:]:
        level = level * one(*cut)
    return level


def noise(own_key, dims, scale, bound, cuts=(), held_as=jnp.bfloat16):
    gain = level_of(own_key, dims, cuts, -0.22, 0.18) if cuts else 1.0
    values = jax.random.normal(own_key, dims, jnp.float32) * scale * gain
    return jnp.minimum(jnp.maximum(values, -bound), bound).astype(held_as)


def setup_inputs(seed: int = 0) -> dict:
    arg_keys = jax.random.split(jax.random.key(seed), 14)
    return {
        "residual_in": noise(arg_keys[0], (SEQS, LENGTH, D), 1.0, 6.0, ((1, 16), (2, 8))),
        "mr_qkv": noise(arg_keys[1], (SEQS, LENGTH, 3, D), 1.0, 6.0, ((1, 16), (3, 8))),
        "mr_short_w": noise(arg_keys[2], (SHORT, 3, D), SHORT ** -0.5, 3.5, ((2, 8),), jnp.float32),
        "mr_filter": noise(arg_keys[3], (MR_TAPS, D), MR_TAPS ** -0.5, 0.5, ((1, 8),)),
        "mr_skip": noise(arg_keys[4], (D,), 1.0, 4.0, ((0, 8),), jnp.float32),
        "mr_out_w": noise(arg_keys[5], (D, D), D ** -0.5, 0.09375, ((0, 8), (1, 16))),
        "lr_gain": jnp.clip(1.0 + 0.18 * jax.random.normal(arg_keys[6], (D,), jnp.float32), 0.1, 1.9),
        "lr_in_w": noise(arg_keys[7], (D, 3, D), D ** -0.5, 0.09375, ((2, 8),)),
        "lr_short_w": noise(arg_keys[8], (SHORT, 3, D), SHORT ** -0.5, 3.5, ((2, 8),), jnp.float32),
        "lr_rate": draw_lr_rate(jax.random.fold_in(arg_keys[13], 71), 0),
        "lr_res": noise(arg_keys[10], (STATE, D), 0.5, 3.0, ((1, 8),), jnp.float32),
        "lr_skip": noise(arg_keys[11], (D,), 1.0, 4.0, ((0, 8),), jnp.float32),
        "lr_out_w": noise(arg_keys[12], (D, D), D ** -0.5, 0.09375, ((0, 8), (1, 16))),
    }


def causal_short(inputs, weights):
    prior = weights.shape[0] - 1
    padded = jnp.pad(inputs, ((0, 0), (prior, 0), (0, 0), (0, 0)))
    total = jnp.zeros(inputs.shape, jnp.float32)
    for lag in range(weights.shape[0]):
        total = total + weights[lag] * padded[:, prior - lag:prior - lag + LENGTH].astype(jnp.float32)
    return total

def long_taps(values, taps):
    padded = jnp.pad(values.astype(jnp.float32), ((0, 0), (MR_TAPS - 1, 0), (0, 0)))

    def accumulate(index, total):
        offset = (MR_TAPS - 1 - index).astype(jnp.int32)
        window = lax.dynamic_slice_in_dim(padded, offset, LENGTH, 1)
        return total + taps[index].astype(jnp.float32) * window
    return lax.fori_loop(0, MR_TAPS, accumulate, jnp.zeros(values.shape, jnp.float32))

def modal(values, rate, residue):
    decay = jnp.exp(-rate)
    weight = residue * jnp.sqrt(1.0 - jnp.exp(-2.0 * rate))

    def advance(state, row):
        state = decay * state + row[:, None, :]
        return (state, lax.optimization_barrier(jnp.sum(weight * state, axis=1)))
    start = jnp.zeros((SEQS, STATE, D), jnp.float32)
    _, result = lax.scan(advance, start, jnp.moveaxis(values, 1, 0))
    return jnp.moveaxis(result, 0, 1)

def split_sum(mixed, weight):
    group = D // N_TP
    flat = mixed.reshape(SEQS * LENGTH, D)
    total = jnp.zeros((SEQS * LENGTH, D), jnp.float32)
    for index in range(N_TP):
        partial_sum = jnp.dot(flat[:, index * group:(index + 1) * group], weight[index * group:(index + 1) * group], preferred_element_type=jnp.float32)
        total = total + partial_sum.astype(jnp.bfloat16).astype(jnp.float32)
    return total.reshape(SEQS, LENGTH, D)

def reference(residual_in, mr_qkv, mr_short_w, mr_filter, mr_skip, mr_out_w, lr_gain, lr_in_w, lr_short_w, lr_rate, lr_res, lr_skip, lr_out_w):
    mr_mixed = causal_short(mr_qkv, mr_short_w)
    mr_u = (mr_mixed[:, :, 1] * mr_mixed[:, :, 2]).astype(jnp.bfloat16)
    mr_conv = long_taps(mr_u, mr_filter)
    mr_z = (mr_mixed[:, :, 0] * (mr_conv + mr_skip * mr_u.astype(jnp.float32))).astype(jnp.bfloat16)
    residual_mid = (residual_in.astype(jnp.float32) + split_sum(mr_z, mr_out_w)).astype(jnp.bfloat16)
    widened = residual_mid.astype(jnp.float32)
    meansq = lax.optimization_barrier(jnp.mean(widened * widened, axis=-1, keepdims=True))
    normed = (widened * lax.rsqrt(meansq + 1e-06) * lr_gain).astype(jnp.bfloat16)
    lr_qkv = jnp.dot(normed.reshape(SEQS * LENGTH, D), lr_in_w.reshape(D, 3 * D), preferred_element_type=jnp.float32)
    lr_qkv = lr_qkv.astype(jnp.bfloat16).reshape(SEQS, LENGTH, 3, D)
    lr_mixed = causal_short(lr_qkv, lr_short_w)
    lr_u = lr_mixed[:, :, 1] * lr_mixed[:, :, 2]
    lr_conv = modal(lr_u, lr_rate, lr_res)
    lr_z = (lr_mixed[:, :, 0] * (lr_conv + lr_skip * lr_u)).astype(jnp.bfloat16)
    return (residual_mid.astype(jnp.float32) + split_sum(lr_z, lr_out_w)).astype(jnp.bfloat16)
```

```python
import jax
import jax.numpy as jnp
from jax import lax
from jax.experimental import pallas as pl
from jax.experimental.pallas import tpu as pltpu
from jax.sharding import PartitionSpec as P

MESH = pl.DeviceIdType.MESH
F32 = jnp.float32
BF16 = jnp.bfloat16

SEGS = 8
STEPS = 64
ROWS = SEGS * STEPS
WIDTH = 512
TAPS = 128
POLES = 16
LANES = 128


def kernel(
    res_h, qkv_h, sw1, filt, skip1, wo1_h, gain, win_h, sw2, rate, resid, skip2, wo2_h,
    out_h,
    qkv_v, xtail, x32, q32, uext, fb, pk_s, pk_r, zo, zn, w, win, ps, pr, pacc, mid, scaled, acc, ssq,
    ltail_s, ltail, est, st_s, st_r, hin, obf, resv,
    loc, hs, hr, wsnd, fsnd, wrecv, zs, zr, pss, prs, ags, agr, sts, strv,
):
    c = lax.axis_index("ctx")
    t = lax.axis_index("tp")
    core = c % 2
    m = c // 2
    y = m % 4
    z = t // 2
    xl = t % 2
    sib = c + 1 - 2 * core
    xn = t + 1 - 2 * xl

    def ztp(dz, x):
        return ((z + dz) % 4) * 2 + x

    def remote(src, dst, ssem, rsem, ctx, tp):
        return pltpu.make_async_remote_copy(
            src_ref=src,
            dst_ref=dst,
            send_sem=ssem,
            recv_sem=rsem,
            device_id={"ctx": ctx, "tp": tp},
            device_id_type=MESH,
        )

    def arrived(ref, sem):
        pltpu.make_async_copy(ref, ref, sem).wait()

    load_qkv = pltpu.make_async_copy(qkv_h, qkv_v, loc.at[0])
    load_qkv.start()
    load_res = pltpu.make_async_copy(res_h, resv, loc.at[1])
    load_res.start()

    barrier = pltpu.get_barrier_semaphore()

    def greet(ctx, tp):
        pl.semaphore_signal(barrier, inc=1, device_id={"ctx": ctx, "tp": tp}, device_id_type=MESH)

    for d in range(1, 16):
        greet((c + d) % 16, t)
    greet(c, xn)
    for d in range(1, 4):
        greet(c, ztp(d, xl))
    for q in range(4):
        greet(2 * (2 * q + xl) + core, xn)
    pl.semaphore_wait(barrier, 19 + 8 * ((y + xl) % 2))

    tail_copy = remote(qkv_h.at[:, :, 248:256, :], xtail, hs.at[0], hr.at[0], (c + 1) % 16, t)
    tail_copy.start()

    slot_mine = xl * 4 + m // 2
    same = (y + xl) % 2 == 0

    def weight_copies(stage, source):
        home = pltpu.make_async_copy(source, w.at[stage, slot_mine, core], wrecv.at[stage, slot_mine, core])
        far = [
            remote(
                source,
                w.at[stage, slot_mine, core],
                wsnd.at[stage, d],
                wrecv.at[stage, slot_mine, core],
                2 * ((m + d) % 8) + core,
                2 * z + y % 2,
            )
            for d in range(8)
        ]
        return home, far

    def weight_start(stage, source):
        home, far = weight_copies(stage, source)
        for d in (4, 2, 6, 1, 3, 5, 7):
            far[d].start()

        @pl.when(same)
        def _():
            home.start()

        @pl.when(jnp.logical_not(same))
        def _():
            far[0].start()

    def weight_forward(stage, index):
        arrived(w.at[stage, index, core], wrecv.at[stage, index, core])
        remote(
            w.at[stage, index, core],
            w.at[stage, index, core],
            fsnd.at[stage, index],
            wrecv.at[stage, index, core],
            sib,
            t,
        ).start()

    def weight_sibling(stage, index):
        arrived(w.at[stage, index, 1 - core], wrecv.at[stage, index, 1 - core])

    def weight_drain(stage, source):
        _, far = weight_copies(stage, source)
        for d in range(1, 8):
            far[d].wait_send()

        @pl.when(jnp.logical_not(same))
        def _():
            far[0].wait_send()

        for index in range(8):
            remote(
                w.at[stage, index, core],
                w.at[stage, index, core],
                fsnd.at[stage, index],
                wrecv.at[stage, index, core],
                sib,
                t,
            ).wait_send()

    weight_start(0, wo1_h)
    load_win = pltpu.make_async_copy(win_h, win, loc.at[2])

    seg = lax.broadcasted_iota(jnp.int32, (SEGS, WIDTH), 0)
    seg1 = lax.broadcasted_iota(jnp.int32, (SEGS, LANES), 0)
    first = seg % 4 == 0
    live = jnp.where(c > 0, 1.0, 0.0).astype(F32)

    def rows(j, count=1):
        start = j * SEGS
        return pl.ds(start if isinstance(start, int) else pl.multiple_of(start, SEGS), count * SEGS)

    def lanes(lt):
        return pl.ds(pl.multiple_of(lt * LANES, LANES), LANES)

    @pl.loop(0, TAPS // 8)
    def _(i):
        taps = filt[pl.ds(pl.multiple_of(i * 8, 8), 8), :].astype(F32)
        for k in range(8):
            fb[rows(i * 8 + k), :] = jnp.broadcast_to(taps[k : k + 1, :], (SEGS, WIDTH))

    load_qkv.wait()
    for s in range(2):
        for p in range(3):

            @pl.loop(0, 16)
            def _(i, s=s, p=p):
                here = pl.ds(pl.multiple_of(i * 16, 16), 16)
                there = pl.ds(pl.multiple_of(s * 256 + i * 16, 16), 16)
                values = qkv_v[s, p, here, :].astype(F32)
                for k in range(WIDTH // LANES):
                    x32[p, k, there, :] = values[:, LANES * k : LANES * (k + 1)]

    def tap(ref, lag, p):
        return jnp.broadcast_to(ref[3 * lag + p : 3 * lag + p + 1, :], (SEGS, WIDTH))

    def strided3(p, j):
        return jnp.concatenate(
            [x32[p, k, pl.ds(j, SEGS, stride=STEPS), :] for k in range(WIDTH // LANES)], axis=1
        )

    def medium(j, now, before, before2):
        mixed = [tap(sw1, 0, p) * now[p] + tap(sw1, 1, p) * before[p] + tap(sw1, 2, p) * before2[p] for p in range(3)]
        q32[rows(j), :] = mixed[0]
        uext[rows(j + 128), :] = (mixed[1] * mixed[2]).astype(BF16).astype(F32)

    last = [strided3(p, 63) for p in range(3)]
    last2 = [strided3(p, 62) for p in range(3)]
    x0 = [strided3(p, 0) for p in range(3)]
    x1 = [strided3(p, 1) for p in range(3)]
    own1 = [jnp.where(first, 0.0, pltpu.roll(v, 1, 0)) for v in last]
    own2 = [jnp.where(first, 0.0, pltpu.roll(v, 1, 0)) for v in last2]
    medium(0, x0, own1, own2)
    medium(1, x1, x0, own1)

    @pl.loop(2, STEPS)
    def _(j):
        medium(
            j,
            [strided3(p, j) for p in range(3)],
            [strided3(p, j - 1) for p in range(3)],
            [strided3(p, j - 2) for p in range(3)],
        )

    @pl.loop(0, STEPS // 4)
    def _(i):
        packed = []
        for k in range(2):
            even = uext[rows(128 + 4 * i + 2 * k), :]
            odd = uext[rows(129 + 4 * i + 2 * k), :]
            packed.append(jnp.where(seg % 4 >= 2, even, pltpu.roll(odd, 6, 0)))
        pk_s[pl.ds(pl.multiple_of(i * 16, 16), 16), :] = jnp.concatenate(packed, axis=0).astype(BF16)

    u_copy = remote(pk_s, pk_r, hs.at[1], hr.at[1], (c + 1) % 16, t)
    u_copy.start()

    arrived(xtail, hr.at[0])

    def halo(p, row):
        top = xtail[0, p].astype(F32)[row : row + 1, :] * live
        bottom = xtail[1, p].astype(F32)[row : row + 1, :] * live
        return jnp.where(seg < 4, jnp.broadcast_to(top, (SEGS, WIDTH)), jnp.broadcast_to(bottom, (SEGS, WIDTH)))

    full1 = [jnp.where(first, halo(p, 7), own1[p]) for p in range(3)]
    full2 = [jnp.where(first, halo(p, 6), own2[p]) for p in range(3)]
    medium(0, x0, full1, full2)
    medium(1, x1, x0, full1)

    load_win.start()
    arrived(pk_r, hr.at[1])

    @pl.loop(0, STEPS // 2)
    def _(i):
        both = pk_r[pl.ds(pl.multiple_of((i // 2) * 16, 16), 16), :].astype(F32) * live
        got = jnp.where(i % 2 == 0, both[:SEGS], both[SEGS:])
        even = uext[rows(128 + 2 * i), :]
        odd = uext[rows(129 + 2 * i), :]
        uext[rows(64 + 2 * i), :] = jnp.where(first, pltpu.roll(got, 5, 0), pltpu.roll(even, 1, 0))
        uext[rows(65 + 2 * i), :] = jnp.where(first, pltpu.roll(got, 7, 0), pltpu.roll(odd, 1, 0))
        uext[rows(2 * i), :] = jnp.where(seg % 4 < 2, pltpu.roll(got, 6, 0), pltpu.roll(even, 2, 0))
        uext[rows(1 + 2 * i), :] = jnp.where(seg % 4 < 2, got, pltpu.roll(odd, 2, 0))

    def z_copy(stage, kh):
        return remote(zo.at[stage, kh], zn.at[stage, kh], zs.at[stage, kh], zr.at[stage, kh], c, xn)

    def p_copy(stage, d):
        return remote(
            ps.at[stage, d - 1], pr.at[stage, d - 1], pss.at[stage, d - 1], prs.at[stage, d - 1], c, ztp(d, xl)
        )

    def project(stage):
        for kh in range(2):
            arrived(zn.at[stage, kh], zr.at[stage, kh])
        for d in (2, 1, 3, 0):
            dest = (z + d) % 4
            for source in range(2):
                weight_sibling(stage, source * 4 + dest)

            @pl.loop(0, 2)
            def _(half, d=d, dest=dest):
                mine = xl * 4 + dest
                other = (1 - xl) * 4 + dest
                total = jnp.zeros((ROWS, 256), F32)
                for kh in range(2):
                    ks = pl.ds(256 * kh, 256)
                    total += jnp.dot(zo[stage, kh], w[stage, mine, half, ks, :], preferred_element_type=F32)
                    total += jnp.dot(zn[stage, kh], w[stage, other, half, ks, :], preferred_element_type=F32)
                cols = pl.ds(pl.multiple_of(half * 256, 256), 256)
                if d == 0:
                    pacc[:, cols] = total
                else:
                    ps[stage, d - 1, :, cols] = total.astype(BF16)

            if d:
                p_copy(stage, d).start()
        for d in (1, 3, 2):
            arrived(pr.at[stage, d - 1], prs.at[stage, d - 1])

    def project_drain(stage):
        for kh in range(2):
            z_copy(stage, kh).wait_send()
        for d in range(1, 4):
            p_copy(stage, d).wait_send()

    def arrivals(stage, i):
        here = pl.ds(pl.multiple_of(i * 16, 16), 16)
        total = pacc[here, :]
        for k in range(3):
            total += pr[stage, k, here, :].astype(F32)
        return total

    for kh in range(2):

        @pl.loop(0, 8)
        def _(block, kh=kh):
            lane = lanes(kh * 2 + block // 4)
            j0 = (block % 4) * 16

            def taps8(ib, totals):
                base = 128 + j0 - 8 * ib - 7
                window = uext[pl.ds(pl.multiple_of(base * SEGS, SEGS), 23 * SEGS), lane]
                weights = fb[pl.ds(pl.multiple_of(ib * 64, 64), 64), lane]
                totals = list(totals)
                for b in range(8):
                    f = weights[b * SEGS : (b + 1) * SEGS]
                    for a in range(16):
                        k = a + 7 - b
                        totals[a] = totals[a] + f * window[k * SEGS : (k + 1) * SEGS]
                return tuple(totals)

            totals = lax.fori_loop(0, 16, taps8, tuple(jnp.zeros((SEGS, LANES), F32) for _ in range(16)))
            skip = jnp.broadcast_to(skip1[:, lane], (SEGS, LANES))
            out_lane = lanes(block // 4)
            for a in range(0, 16, 2):
                pair = []
                for k in (a, a + 1):
                    u = uext[rows(128 + j0 + k), lane]
                    pair.append(q32[rows(j0 + k), lane] * (totals[k] + skip * u))
                zo[0, kh, pl.ds(pl.multiple_of((j0 + a) * SEGS, 16), 16), out_lane] = jnp.concatenate(
                    pair, axis=0
                ).astype(BF16)

        z_copy(0, kh).start()

    for d in (2, 1, 3, 0):
        for source in range(2):
            weight_forward(0, source * 4 + (z + d) % 4)
    project(0)
    weight_start(1, wo2_h)

    load_res.wait()

    @pl.loop(0, 32)
    def _(i):
        s = i // 16
        r = (i % 16) * 16
        values = resv[s, pl.ds(pl.multiple_of(r, 16), 16), :].astype(F32)
        for k in range(WIDTH // LANES):
            x32[0, k, pl.ds(pl.multiple_of(i * 16, 16), 16), :] = values[:, LANES * k : LANES * (k + 1)]

    @pl.loop(0, 32)
    def _(i):
        before = jnp.concatenate([strided3(0, 2 * i), strided3(0, 2 * i + 1)], axis=0)
        value = (before + arrivals(0, i)).astype(BF16)
        mid[t, i // 8, pl.ds(pl.multiple_of((i % 8) * 16, 16), 16), :] = value

    sent = []

    def send(slot, quarter, tp):
        k = len(sent)
        copy = remote(
            mid.at[slot, quarter], mid.at[slot, quarter], ags.at[k], agr.at[slot, quarter], c, tp
        )
        copy.start()
        sent.append(copy)

    def have(slot, *quarters):
        for quarter in quarters:
            arrived(mid.at[slot, quarter], agr.at[slot, quarter])

    load_win.wait()

    def absorb(slot, fresh=False):
        scale = gain[pl.ds(slot, 1), :]

        @pl.loop(0, 16)
        def _(i):
            here = pl.ds(pl.multiple_of((i % 4) * 32, 32), 32)
            values = mid[slot, i // 4, here, :].astype(F32)
            square = values * values
            part = square[:, 0:128] + square[:, 128:256] + square[:, 256:384] + square[:, 384:512]
            there = pl.ds(pl.multiple_of(i * 32, 32), 32)
            ssq[there, :] = part if fresh else ssq[there, :] + part
            scaled[there, :] = (values * scale).astype(BF16)

        @pl.loop(0, 6)
        def _(i):
            cols = pl.ds(pl.multiple_of((i % 2) * 256, 256), 256)
            depth = pl.ds(pl.multiple_of(slot * WIDTH, WIDTH), WIDTH)
            product = jnp.dot(scaled[...], win[i // 2, depth, cols], preferred_element_type=F32)
            acc[i // 2, :, cols] = product if fresh else acc[i // 2, :, cols] + product

    zp, zm, zz = ztp(1, xl), ztp(3, xl), ztp(2, xl)
    xp, xm, xz = ztp(1, 1 - xl), ztp(3, 1 - xl), ztp(2, 1 - xl)
    for quarter in range(4):
        send(t, quarter, xn)
        send(t, quarter, zp)
        send(t, quarter, zm)
    absorb(t, fresh=True)
    have(xn, 0, 1)
    for quarter in range(2):
        send(xn, quarter, zp)
        send(xn, quarter, zm)
    have(zm, 0, 1, 2, 3)
    send(zm, 0, zp)
    send(zm, 2, zp)
    send(zm, 2, xn)
    send(zm, 3, xn)
    have(zp, 0, 1, 2, 3)
    send(zp, 1, zm)
    send(zp, 3, zm)
    send(zp, 2, xn)
    send(zp, 3, xn)
    absorb(zm)
    absorb(zp)
    have(xm, 0, 1)
    send(xm, 0, zp)
    have(xp, 0, 1)
    send(xp, 1, zm)
    have(zz, 0, 1, 2, 3)
    send(zz, 2, xn)
    send(zz, 3, xn)
    have(xn, 2, 3)
    absorb(xn)
    absorb(zz)
    have(xm, 2, 3)
    absorb(xm)
    have(xp, 2, 3)
    absorb(xp)
    have(xz, 0, 1, 2, 3)
    absorb(xz)

    for d in (2, 1, 3, 0):
        for source in range(2):
            weight_forward(1, source * 4 + (z + d) % 4)

    def finish(i):
        here = pl.ds(i * 16 if isinstance(i, int) else pl.multiple_of(i * 16, 16), 16)
        meansq = jnp.sum(ssq[here, :], axis=1, keepdims=True) * (1.0 / 4096.0)
        factor = lax.rsqrt(meansq + 1e-6)
        values = [(acc[p, here, :] * factor).astype(BF16) for p in range(3)]
        for p in range(3):
            acc[p, here, :] = values[p].astype(F32)
        return values

    tails = finish(31)
    for p in range(3):
        ltail_s[p] = tails[p]
    l_copy = remote(ltail_s, ltail, hs.at[2], hr.at[2], (c + 1) % 16, t)
    l_copy.start()

    @pl.loop(0, 31)
    def _(i):
        finish(i)

    def longer(j, now, before, before2):
        mixed = [tap(sw2, 0, p) * now[p] + tap(sw2, 1, p) * before[p] + tap(sw2, 2, p) * before2[p] for p in range(3)]
        q32[rows(j), :] = mixed[0]
        uext[rows(j), :] = mixed[1] * mixed[2]

    @pl.loop(2, STEPS)
    def _(j):
        longer(
            j,
            [acc[p, rows(j), :] for p in range(3)],
            [acc[p, rows(j - 1), :] for p in range(3)],
            [acc[p, rows(j - 2), :] for p in range(3)],
        )

    arrived(ltail, hr.at[2])
    edge1, edge2 = [], []
    for p in range(3):
        got = ltail[p].astype(F32) * live
        edge2.append(jnp.where(first, pltpu.roll(got[:SEGS], 5, 0), pltpu.roll(acc[p, rows(62), :], 1, 0)))
        edge1.append(jnp.where(first, pltpu.roll(got[SEGS:], 5, 0), pltpu.roll(acc[p, rows(63), :], 1, 0)))
    y0 = [acc[p, rows(0), :] for p in range(3)]
    y1 = [acc[p, rows(1), :] for p in range(3)]
    longer(0, y0, edge1, edge2)
    longer(1, y1, y0, edge1)

    def row_of(ref, n, lane):
        return jnp.broadcast_to(ref[n : n + 1, lane], (SEGS, LANES))

    @pl.loop(0, WIDTH // LANES)
    def _(lt):
        lane = lanes(lt)
        decay = [jnp.exp(-row_of(rate, n, lane)) for n in range(POLES)]

        def step(j, states):
            u = uext[rows(j), lane]
            return tuple(decay[n] * states[n] + u for n in range(POLES))

        states = lax.fori_loop(0, STEPS, step, tuple(jnp.zeros((SEGS, LANES), F32) for _ in range(POLES)))
        for n in range(POLES):
            est[rows(n), lane] = states[n]

    place = seg1 % 4

    @pl.loop(0, WIDTH // LANES)
    def _(lt):
        lane = lanes(lt)
        for g in range(2):
            packed = []
            for h in range(2):
                total = jnp.zeros((SEGS, LANES), F32)
                for r in range(4):
                    n = g * 8 + h * 4 + r
                    span = jnp.exp(-float(STEPS) * row_of(rate, n, lane))
                    value = est[rows(n), lane]
                    value = value + span * jnp.where(place >= 1, pltpu.roll(value, 1, 0), 0.0)
                    value = value + span * span * jnp.where(place >= 2, pltpu.roll(value, 2, 0), 0.0)
                    est[rows(n), lane] = jnp.where(place >= 1, pltpu.roll(value, 1, 0), 0.0)
                    end = value if r == 3 else pltpu.roll(value, (r - 3) % 8, 0)
                    total = jnp.where(place == r, end, total)
                packed.append(total)
            st_s[pl.ds(g * 16, 16), lane] = jnp.concatenate(packed, axis=0).astype(BF16)

    def state_copy(d):
        return remote(st_s, st_r.at[d - 1], sts.at[d - 1], strv.at[d - 1], c + d, t)

    for d in range(15, 0, -1):

        @pl.when(c + d < 16)
        def _(d=d):
            state_copy(d).start()

    packs = []
    for g in range(4):
        total = jnp.zeros((SEGS, WIDTH), F32)
        for r in range(4):
            n = g * 4 + r
            total = jnp.where(seg % 4 == r, jnp.broadcast_to(rate[n : n + 1, :], (SEGS, WIDTH)), total)
        packs.append(total)
    pack = jnp.concatenate(packs, axis=0)
    hin[...] = jnp.zeros((4 * SEGS, WIDTH), F32)
    for d in range(1, 16):

        @pl.when(c - d >= 0)
        def _(d=d):
            arrived(st_r.at[d - 1], strv.at[d - 1])
            hin[...] += jnp.exp(pack * (-256.0 * (d - 1))) * st_r[d - 1].astype(F32)

    for kh in range(2):

        @pl.loop(0, 2)
        def _(half, kh=kh):
            lane = lanes(kh * 2 + half)
            decay, weight, states = [], [], []
            for n in range(POLES):
                r = row_of(rate, n, lane)
                decay.append(jnp.exp(-r))
                weight.append(row_of(resid, n, lane) * jnp.sqrt(1.0 - jnp.exp(-2.0 * r)))
                k = (n // 4) * SEGS + n % 4
                enter = jnp.where(
                    seg1 < 4,
                    jnp.broadcast_to(hin[k : k + 1, lane], (SEGS, LANES)),
                    jnp.broadcast_to(hin[k + 4 : k + 5, lane], (SEGS, LANES)),
                )
                states.append(est[rows(n), lane] + jnp.exp(r * (place.astype(F32) * (-float(STEPS)))) * enter)
            skip = jnp.broadcast_to(skip2[:, lane], (SEGS, LANES))
            out_lane = lanes(half)

            def step(i, states):
                pair = []
                for k in range(2):
                    u = uext[rows(2 * i + k), lane]
                    states = [decay[n] * states[n] + u for n in range(POLES)]
                    terms = [weight[n] * states[n] for n in range(POLES)]
                    while len(terms) > 1:
                        terms = [terms[a] + terms[a + 1] for a in range(0, len(terms), 2)]
                    pair.append(q32[rows(2 * i + k), lane] * (terms[0] + skip * u))
                zo[1, kh, pl.ds(pl.multiple_of(i * 16, 16), 16), out_lane] = jnp.concatenate(pair, axis=0).astype(BF16)
                return tuple(states)

            lax.fori_loop(0, STEPS // 2, step, tuple(states))

        z_copy(1, kh).start()

    project(1)

    @pl.loop(0, 32)
    def _(i):
        base = mid[t, i // 8, pl.ds(pl.multiple_of((i % 8) * 16, 16), 16), :].astype(F32)
        value = base + arrivals(1, i)
        for k in range(WIDTH // LANES):
            part = value[:, LANES * k : LANES * (k + 1)]
            x32[1, k, pl.ds(2 * i, SEGS, stride=STEPS), :] = part[:SEGS]
            x32[1, k, pl.ds(2 * i + 1, SEGS, stride=STEPS), :] = part[SEGS:]

    @pl.loop(0, 32)
    def _(i):
        s = i // 16
        r = (i % 16) * 16
        here = pl.ds(pl.multiple_of(i * 16, 16), 16)
        value = jnp.concatenate([x32[1, k, here, :] for k in range(WIDTH // LANES)], axis=1)
        obf[s, pl.ds(pl.multiple_of(r, 16), 16), :] = value.astype(BF16)

    store = pltpu.make_async_copy(obf, out_h, loc.at[3])
    store.start()

    tail_copy.wait_send()
    u_copy.wait_send()
    l_copy.wait_send()
    weight_drain(0, wo1_h)
    weight_drain(1, wo2_h)
    project_drain(0)
    project_drain(1)
    for copy in sent:
        copy.wait_send()
    for d in range(1, 16):

        @pl.when(c + d < 16)
        def _(d=d):
            state_copy(d).wait_send()

    store.wait()


def local(
    residual_in, mr_qkv, mr_short_w, mr_filter, mr_skip, mr_out_w, lr_gain,
    lr_in_w, lr_short_w, lr_rate, lr_res, lr_skip, lr_out_w,
):
    vmem = pl.BlockSpec(memory_space=pltpu.VMEM)
    hbm = pl.BlockSpec(memory_space=pl.ANY)
    dma = pltpu.SemaphoreType.DMA
    scratch = [
        pltpu.VMEM((2, 3, 256, WIDTH), BF16),
        pltpu.VMEM((2, 3, 8, WIDTH), BF16),
        pltpu.VMEM((3, WIDTH // LANES, ROWS, LANES), F32),
        pltpu.VMEM((ROWS, WIDTH), F32),
        pltpu.VMEM((192 * SEGS, WIDTH), F32),
        pltpu.VMEM((TAPS * SEGS, WIDTH), F32),
        pltpu.VMEM((256, WIDTH), BF16),
        pltpu.VMEM((256, WIDTH), BF16),
        pltpu.VMEM((2, 2, ROWS, 256), BF16),
        pltpu.VMEM((2, 2, ROWS, 256), BF16),
        pltpu.VMEM((2, 8, 2, WIDTH, 256), BF16),
        pltpu.VMEM((3, 4096, WIDTH), BF16),
        pltpu.VMEM((2, 3, ROWS, WIDTH), BF16),
        pltpu.VMEM((2, 3, ROWS, WIDTH), BF16),
        pltpu.VMEM((ROWS, WIDTH), F32),
        pltpu.VMEM((8, 4, 128, WIDTH), BF16),
        pltpu.VMEM((ROWS, WIDTH), BF16),
        pltpu.VMEM((3, ROWS, WIDTH), F32),
        pltpu.VMEM((ROWS, LANES), F32),
        pltpu.VMEM((3, 16, WIDTH), BF16),
        pltpu.VMEM((3, 16, WIDTH), BF16),
        pltpu.VMEM((POLES * SEGS, WIDTH), F32),
        pltpu.VMEM((4 * SEGS, WIDTH), BF16),
        pltpu.VMEM((15, 4 * SEGS, WIDTH), BF16),
        pltpu.VMEM((4 * SEGS, WIDTH), F32),
        pltpu.VMEM((2, 256, WIDTH), BF16),
        pltpu.VMEM((2, 256, WIDTH), BF16),
        dma((4,)),
        dma((3,)),
        dma((3,)),
        dma((2, 8)),
        dma((2, 8)),
        dma((2, 8, 2)),
        dma((2, 2)),
        dma((2, 2)),
        dma((2, 3)),
        dma((2, 3)),
        dma((32,)),
        dma((8, 4)),
        dma((15,)),
        dma((15,)),
    ]
    return pl.pallas_call(
        kernel,
        out_shape=jax.ShapeDtypeStruct((2, 256, WIDTH), BF16),
        in_specs=[hbm, hbm, vmem, vmem, vmem, hbm, vmem, hbm, vmem, vmem, vmem, vmem, hbm],
        out_specs=hbm,
        scratch_shapes=scratch,
        compiler_params=pltpu.CompilerParams(
            collective_id=0, has_side_effects=True, vmem_limit_bytes=62 * 1024 * 1024
        ),
    )(
        residual_in,
        jnp.transpose(mr_qkv, (0, 2, 1, 3)),
        mr_short_w.reshape(9, WIDTH),
        mr_filter,
        mr_skip.reshape(1, WIDTH),
        mr_out_w,
        lr_gain.reshape(8, WIDTH),
        jnp.transpose(lr_in_w, (1, 0, 2)),
        lr_short_w.reshape(9, WIDTH),
        lr_rate,
        lr_res,
        lr_skip.reshape(1, WIDTH),
        lr_out_w,
    )


def solution(mesh):
    in_specs = (
        P(None, "ctx", "tp"),
        P(None, "ctx", None, "tp"),
        P(None, None, "tp"),
        P(None, "tp"),
        P("tp"),
        P("tp", "ctx"),
        P(),
        P(None, None, "tp"),
        P(None, None, "tp"),
        P(None, "tp"),
        P(None, "tp"),
        P("tp"),
        P("tp", "ctx"),
    )
    return jax.shard_map(local, mesh=mesh, in_specs=in_specs, out_specs=P(None, "ctx", "tp"), check_vma=False)
```

```python
import jax
import jax.numpy as jnp
from jax import lax
from jax.experimental import pallas as pl
from jax.experimental.pallas import tpu as pltpu
from jax.sharding import PartitionSpec as P

MESH = pl.DeviceIdType.MESH
F32 = jnp.float32
BF16 = jnp.bfloat16

SEGS = 8
STEPS = 64
ROWS = SEGS * STEPS
WIDTH = 512
TAPS = 128
POLES = 16
LANES = 128


def kernel(
    res_h, qkv_h, sw1, filt, skip1, wo1_h, gain, win_h, sw2, rate, resid, skip2, wo2_h,
    out_h,
    qkv_v, xtail, x32, q32, uext, fb, pk_s, pk_r, zo, zn, w, win, ps, pr, pacc, mid, scaled, acc, ssq,
    ltail_s, ltail, est, st_s, st_r, hin, obf, resv,
    loc, hs, hr, wsnd, fsnd, bsnd, wrecv, zs, zr, pss, prs, ags, agr, sts, strv,
):
    c = lax.axis_index("ctx")
    t = lax.axis_index("tp")
    core = c % 2
    m = c // 2
    y = m % 4
    xh = m // 4
    z = t // 2
    xl = t % 2
    sib = c + 1 - 2 * core
    xn = t + 1 - 2 * xl

    def ztp(dz, x):
        return ((z + dz) % 4) * 2 + x

    def remote(src, dst, ssem, rsem, ctx, tp):
        return pltpu.make_async_remote_copy(
            src_ref=src,
            dst_ref=dst,
            send_sem=ssem,
            recv_sem=rsem,
            device_id={"ctx": ctx, "tp": tp},
            device_id_type=MESH,
        )

    def arrived(ref, sem):
        pltpu.make_async_copy(ref, ref, sem).wait()

    load_qkv = pltpu.make_async_copy(qkv_h, qkv_v, loc.at[0])
    load_qkv.start()
    load_res = pltpu.make_async_copy(res_h, resv, loc.at[1])
    load_res.start()

    barrier = pltpu.get_barrier_semaphore()

    def greet(ctx, tp):
        pl.semaphore_signal(barrier, inc=1, device_id={"ctx": ctx, "tp": tp}, device_id_type=MESH)

    for d in range(1, 16):
        greet((c + d) % 16, t)
    greet(c, xn)
    greet((c + 8) % 16, xn)
    greet(c, ztp(1, xl))
    greet(c, ztp(3, xl))
    pl.semaphore_wait(barrier, 19)

    tail_copy = remote(qkv_h.at[:, :, 248:256, :], xtail, hs.at[0], hr.at[0], (c + 1) % 16, t)
    tail_copy.start()

    holder = (y + xl) % 2 == 0
    relay = (y + xl) % 2 == 1
    ups = ((y + 1) % 4, (y + 3) % 4)

    def place_of(k, row):
        xs = (xl, 1 - xl, 1 - xl, xl)[k]
        xhs = (xh, xh, 1 - xh, 1 - xh)[k]
        return xs * 4 + xhs * 2 + row // 2

    def ctx_of(h, row):
        return (h * 4 + row) * 2 + core

    def weight_first(stage, source):
        mine = place_of(0, y)
        target = w.at[stage, mine, core]
        arrival = wrecv.at[stage, mine, core]
        home = pltpu.make_async_copy(source, target, arrival)
        along = [
            remote(source, target, wsnd.at[stage, 0], arrival, ctx_of(xh, ups[0]), t),
            remote(source, target, wsnd.at[stage, 1], arrival, ctx_of(xh, ups[1]), t),
            remote(source, target, wsnd.at[stage, 2], arrival, ctx_of(1 - xh, y), t),
        ]
        across = [
            remote(source, target, wsnd.at[stage, 0], arrival, c, xn),
            remote(source, target, wsnd.at[stage, 1], arrival, ctx_of(1 - xh, y), xn),
        ]
        return home, along, across

    def weight_start(stage, source):
        home, along, across = weight_first(stage, source)

        @pl.when(holder)
        def _():
            home.start()
            for copy in along:
                copy.start()

        @pl.when(relay)
        def _():
            for copy in across:
                copy.start()

    def weight_pass(stage, index, sem, ctx):
        block = w.at[stage, index, core]
        return remote(block, block, sem, wrecv.at[stage, index, core], ctx, t)

    def weight_got(stage, index):
        arrived(w.at[stage, index, core], wrecv.at[stage, index, core])

    def weight_moves(stage, k):
        here, up, down, far = place_of(k, y), place_of(k, ups[0]), place_of(k, ups[1]), place_of(k, (y + 2) % 4)

        def sibling(index, n):
            return weight_pass(stage, index, bsnd.at[stage, n], sib)

        held = [sibling(here, k)]
        if k:
            held += [weight_pass(stage, here, fsnd.at[stage, n, k], ctx_of(xh, ups[n])) for n in range(2)]
        late = [sibling(far, 4 + k)]
        below = [sibling(down, k)]
        above = [sibling(up, 4 + k)]
        if k % 2 == 0:
            below.append(weight_pass(stage, down, fsnd.at[stage, 0, k], ctx_of(xh, ups[0])))
        else:
            above.append(weight_pass(stage, up, fsnd.at[stage, 0, k], ctx_of(xh, ups[1])))
        return (here, held), (far, late), (down, below), (up, above)

    def weight_step(stage, k):
        first_, _, below, above = weight_moves(stage, k)

        @pl.when(holder)
        def _():
            weight_got(stage, first_[0])
            for copy in reversed(first_[1]):
                copy.start()

        @pl.when(relay)
        def _():
            for index, copies in (below, above):
                weight_got(stage, index)
                for copy in reversed(copies):
                    copy.start()

    def weight_last(stage):
        @pl.when(holder)
        def _():
            for k in range(4):
                _, (index, copies), _, _ = weight_moves(stage, k)
                weight_got(stage, index)
                copies[0].start()

    def weight_sibling(stage, index):
        arrived(w.at[stage, index, 1 - core], wrecv.at[stage, index, 1 - core])

    def weight_drain(stage, source):
        _, along, across = weight_first(stage, source)

        @pl.when(holder)
        def _():
            for copy in along:
                copy.wait_send()
            for k in range(4):
                first_, late, _, _ = weight_moves(stage, k)
                for copy in first_[1] + late[1]:
                    copy.wait_send()

        @pl.when(relay)
        def _():
            for copy in across:
                copy.wait_send()
            for k in range(4):
                _, _, below, above = weight_moves(stage, k)
                for copy in below[1] + above[1]:
                    copy.wait_send()

    weight_start(0, wo1_h)
    load_win = pltpu.make_async_copy(win_h, win, loc.at[2])

    seg = lax.broadcasted_iota(jnp.int32, (SEGS, WIDTH), 0)
    seg1 = lax.broadcasted_iota(jnp.int32, (SEGS, LANES), 0)
    first = seg % 4 == 0
    live = jnp.where(c > 0, 1.0, 0.0).astype(F32)

    def rows(j, count=1):
        start = j * SEGS
        return pl.ds(start if isinstance(start, int) else pl.multiple_of(start, SEGS), count * SEGS)

    def lanes(lt):
        return pl.ds(pl.multiple_of(lt * LANES, LANES), LANES)

    @pl.loop(0, TAPS // 8)
    def _(i):
        taps = filt[pl.ds(pl.multiple_of(i * 8, 8), 8), :].astype(F32)
        for k in range(8):
            fb[rows(i * 8 + k), :] = jnp.broadcast_to(taps[k : k + 1, :], (SEGS, WIDTH))

    load_qkv.wait()
    for s in range(2):
        for p in range(3):

            @pl.loop(0, 16)
            def _(i, s=s, p=p):
                here = pl.ds(pl.multiple_of(i * 16, 16), 16)
                there = pl.ds(pl.multiple_of(s * 256 + i * 16, 16), 16)
                values = qkv_v[s, p, here, :].astype(F32)
                for k in range(WIDTH // LANES):
                    x32[p, k, there, :] = values[:, LANES * k : LANES * (k + 1)]

    def tap(ref, lag, p):
        return jnp.broadcast_to(ref[lag, p : p + 1, :], (SEGS, WIDTH))

    def strided3(p, j):
        return jnp.concatenate(
            [x32[p, k, pl.ds(j, SEGS, stride=STEPS), :] for k in range(WIDTH // LANES)], axis=1
        )

    def medium(j, now, before, before2):
        mixed = [tap(sw1, 0, p) * now[p] + tap(sw1, 1, p) * before[p] + tap(sw1, 2, p) * before2[p] for p in range(3)]
        q32[rows(j), :] = mixed[0]
        uext[rows(j + 128), :] = (mixed[1] * mixed[2]).astype(BF16).astype(F32)

    last = [strided3(p, 63) for p in range(3)]
    last2 = [strided3(p, 62) for p in range(3)]
    x0 = [strided3(p, 0) for p in range(3)]
    x1 = [strided3(p, 1) for p in range(3)]
    own1 = [jnp.where(first, 0.0, pltpu.roll(v, 1, 0)) for v in last]
    own2 = [jnp.where(first, 0.0, pltpu.roll(v, 1, 0)) for v in last2]
    medium(0, x0, own1, own2)
    medium(1, x1, x0, own1)

    @pl.loop(2, STEPS)
    def _(j):
        medium(
            j,
            [strided3(p, j) for p in range(3)],
            [strided3(p, j - 1) for p in range(3)],
            [strided3(p, j - 2) for p in range(3)],
        )

    @pl.loop(0, STEPS // 4)
    def _(i):
        packed = []
        for k in range(2):
            even = uext[rows(128 + 4 * i + 2 * k), :]
            odd = uext[rows(129 + 4 * i + 2 * k), :]
            packed.append(jnp.where(seg % 4 >= 2, even, pltpu.roll(odd, 6, 0)))
        pk_s[pl.ds(pl.multiple_of(i * 16, 16), 16), :] = jnp.concatenate(packed, axis=0).astype(BF16)

    u_copy = remote(pk_s, pk_r, hs.at[1], hr.at[1], (c + 1) % 16, t)
    u_copy.start()
    weight_step(0, 0)

    arrived(xtail, hr.at[0])

    def halo(p, row):
        top = xtail[0, p].astype(F32)[row : row + 1, :] * live
        bottom = xtail[1, p].astype(F32)[row : row + 1, :] * live
        return jnp.where(seg < 4, jnp.broadcast_to(top, (SEGS, WIDTH)), jnp.broadcast_to(bottom, (SEGS, WIDTH)))

    full1 = [jnp.where(first, halo(p, 7), own1[p]) for p in range(3)]
    full2 = [jnp.where(first, halo(p, 6), own2[p]) for p in range(3)]
    medium(0, x0, full1, full2)
    medium(1, x1, x0, full1)

    load_win.start()
    arrived(pk_r, hr.at[1])

    @pl.loop(0, STEPS // 2)
    def _(i):
        both = pk_r[pl.ds(pl.multiple_of((i // 2) * 16, 16), 16), :].astype(F32) * live
        got = jnp.where(i % 2 == 0, both[:SEGS], both[SEGS:])
        even = uext[rows(128 + 2 * i), :]
        odd = uext[rows(129 + 2 * i), :]
        uext[rows(64 + 2 * i), :] = jnp.where(first, pltpu.roll(got, 5, 0), pltpu.roll(even, 1, 0))
        uext[rows(65 + 2 * i), :] = jnp.where(first, pltpu.roll(got, 7, 0), pltpu.roll(odd, 1, 0))
        uext[rows(2 * i), :] = jnp.where(seg % 4 < 2, pltpu.roll(got, 6, 0), pltpu.roll(even, 2, 0))
        uext[rows(1 + 2 * i), :] = jnp.where(seg % 4 < 2, got, pltpu.roll(odd, 2, 0))

    weight_step(0, 1)

    def z_copy(stage, kh):
        return remote(zo.at[stage, kh], zn.at[stage, kh], zs.at[stage, kh], zr.at[stage, kh], c, xn)

    def p_copy(stage, i):
        return remote(
            ps.at[stage, i], pr.at[stage, i], pss.at[stage, i], prs.at[stage, i], c, ztp(1 if i % 2 == 0 else 3, xl)
        )

    def project(stage):
        for kh in range(2):
            arrived(zn.at[stage, kh], zr.at[stage, kh])

        def term(d, half):
            dest = (z + d) % 4
            total = jnp.zeros((ROWS, 256), F32)
            for kh in range(2):
                ks = pl.ds(256 * kh, 256)
                total += jnp.dot(zo[stage, kh], w[stage, xl * 4 + dest, half, ks, :], preferred_element_type=F32)
                total += jnp.dot(zn[stage, kh], w[stage, (1 - xl) * 4 + dest, half, ks, :], preferred_element_type=F32)
            return total

        for i, d, half in ((0, 2, 0), (1, 2, 1), (2, 1, 1), (3, 3, 0), (4, 1, 0), (5, 3, 1)):
            if i in (0, 2, 3):
                for source in range(2):
                    weight_sibling(stage, source * 4 + (z + d) % 4)
            if i >= 4:
                arrived(pr.at[stage, i - 4], prs.at[stage, i - 4])
                ps[stage, i] = (term(d, half) + pr[stage, i - 4].astype(F32)).astype(BF16)
            else:
                ps[stage, i] = term(d, half).astype(BF16)
            p_copy(stage, i).start()
            if i == 3:
                for source in range(2):
                    weight_sibling(stage, source * 4 + z)
                for own in range(2):
                    pacc[:, 256 * own : 256 * (own + 1)] = term(0, own)

    def project_wait(stage):
        for i in (2, 3, 4, 5):
            arrived(pr.at[stage, i], prs.at[stage, i])

    def project_drain(stage):
        for kh in range(2):
            z_copy(stage, kh).wait_send()
        for i in range(6):
            p_copy(stage, i).wait_send()

    def arrivals(stage, i):
        here = pl.ds(pl.multiple_of(i * 16, 16), 16)
        left = pr[stage, 3, here, :].astype(F32) + pr[stage, 4, here, :].astype(F32)
        right = pr[stage, 2, here, :].astype(F32) + pr[stage, 5, here, :].astype(F32)
        return pacc[here, :] + jnp.concatenate([left, right], axis=1)

    for kh in range(2):

        @pl.loop(0, 8)
        def _(block, kh=kh):
            lane = lanes(kh * 2 + block // 4)
            j0 = (block % 4) * 16

            def taps8(ib, totals):
                base = 128 + j0 - 8 * ib - 7
                window = uext[pl.ds(pl.multiple_of(base * SEGS, SEGS), 23 * SEGS), lane]
                weights = fb[pl.ds(pl.multiple_of(ib * 64, 64), 64), lane]
                totals = list(totals)
                for b in range(8):
                    f = weights[b * SEGS : (b + 1) * SEGS]
                    for a in range(16):
                        k = a + 7 - b
                        totals[a] = totals[a] + f * window[k * SEGS : (k + 1) * SEGS]
                return tuple(totals)

            totals = lax.fori_loop(0, 16, taps8, tuple(jnp.zeros((SEGS, LANES), F32) for _ in range(16)))
            skip = jnp.broadcast_to(skip1[:, lane], (SEGS, LANES))
            out_lane = lanes(block // 4)
            for a in range(0, 16, 2):
                pair = []
                for k in (a, a + 1):
                    u = uext[rows(128 + j0 + k), lane]
                    pair.append(q32[rows(j0 + k), lane] * (totals[k] + skip * u))
                zo[0, kh, pl.ds(pl.multiple_of((j0 + a) * SEGS, 16), 16), out_lane] = jnp.concatenate(
                    pair, axis=0
                ).astype(BF16)

        z_copy(0, kh).start()
        weight_step(0, 2 + kh)

    weight_start(1, wo2_h)
    weight_last(0)
    project(0)
    weight_step(1, 0)
    weight_step(1, 1)
    project_wait(0)

    load_res.wait()

    @pl.loop(0, 32)
    def _(i):
        s = i // 16
        r = (i % 16) * 16
        values = resv[s, pl.ds(pl.multiple_of(r, 16), 16), :].astype(F32)
        for k in range(WIDTH // LANES):
            x32[0, k, pl.ds(pl.multiple_of(i * 16, 16), 16), :] = values[:, LANES * k : LANES * (k + 1)]

    @pl.loop(0, 32)
    def _(i):
        before = jnp.concatenate([strided3(0, 2 * i), strided3(0, 2 * i + 1)], axis=0)
        value = (before + arrivals(0, i)).astype(BF16)
        mid[t, i // 8, pl.ds(pl.multiple_of((i % 8) * 16, 16), 16), :] = value

    sent = []

    def send(slot, quarter, tp):
        k = len(sent)
        copy = remote(
            mid.at[slot, quarter], mid.at[slot, quarter], ags.at[k], agr.at[slot, quarter], c, tp
        )
        copy.start()
        sent.append(copy)

    def have(slot, *quarters):
        for quarter in quarters:
            arrived(mid.at[slot, quarter], agr.at[slot, quarter])

    load_win.wait()

    def absorb(slot, fresh=False):
        scale = gain[:, pl.ds(pl.multiple_of(slot * WIDTH, WIDTH), WIDTH)]

        @pl.loop(0, 16)
        def _(i):
            here = pl.ds(pl.multiple_of((i % 4) * 32, 32), 32)
            values = mid[slot, i // 4, here, :].astype(F32)
            square = values * values
            part = square[:, 0:128] + square[:, 128:256] + square[:, 256:384] + square[:, 384:512]
            there = pl.ds(pl.multiple_of(i * 32, 32), 32)
            ssq[there, :] = part if fresh else ssq[there, :] + part
            scaled[there, :] = (values * scale).astype(BF16)

        @pl.loop(0, 6)
        def _(i):
            cols = pl.ds(pl.multiple_of((i % 2) * 256, 256), 256)
            depth = pl.ds(pl.multiple_of(slot * WIDTH, WIDTH), WIDTH)
            product = jnp.dot(scaled[...], win[i // 2, depth, cols], preferred_element_type=F32)
            acc[i // 2, :, cols] = product if fresh else acc[i // 2, :, cols] + product

    zp, zm, zz = ztp(1, xl), ztp(3, xl), ztp(2, xl)
    xp, xm, xz = ztp(1, 1 - xl), ztp(3, 1 - xl), ztp(2, 1 - xl)
    for quarter in range(4):
        send(t, quarter, xn)
        send(t, quarter, zp)
        send(t, quarter, zm)
    absorb(t, fresh=True)
    weight_step(1, 2)
    have(xn, 0, 1)
    for quarter in range(2):
        send(xn, quarter, zp)
        send(xn, quarter, zm)
    have(zm, 0, 1, 2, 3)
    send(zm, 0, zp)
    send(zm, 2, zp)
    send(zm, 2, xn)
    send(zm, 3, xn)
    have(zp, 0, 1, 2, 3)
    send(zp, 1, zm)
    send(zp, 3, zm)
    send(zp, 2, xn)
    send(zp, 3, xn)
    absorb(zm)
    weight_step(1, 3)
    absorb(zp)
    have(xm, 0, 1)
    send(xm, 0, zp)
    have(xp, 0, 1)
    send(xp, 1, zm)
    have(zz, 0, 1, 2, 3)
    send(zz, 2, xn)
    send(zz, 3, xn)
    have(xn, 2, 3)
    absorb(xn)
    absorb(zz)
    have(xm, 2, 3)
    absorb(xm)
    have(xp, 2, 3)
    absorb(xp)
    have(xz, 0, 1, 2, 3)
    absorb(xz)

    weight_last(1)

    def finish(i):
        here = pl.ds(i * 16 if isinstance(i, int) else pl.multiple_of(i * 16, 16), 16)
        meansq = jnp.sum(ssq[here, :], axis=1, keepdims=True) * (1.0 / 4096.0)
        factor = lax.rsqrt(meansq + 1e-6)
        values = [(acc[p, here, :] * factor).astype(BF16) for p in range(3)]
        for p in range(3):
            acc[p, here, :] = values[p].astype(F32)
        return values

    tails = finish(31)
    for p in range(3):
        ltail_s[p] = tails[p]
    l_copy = remote(ltail_s, ltail, hs.at[2], hr.at[2], (c + 1) % 16, t)
    l_copy.start()

    @pl.loop(0, 31)
    def _(i):
        finish(i)

    def longer(j, now, before, before2):
        mixed = [tap(sw2, 0, p) * now[p] + tap(sw2, 1, p) * before[p] + tap(sw2, 2, p) * before2[p] for p in range(3)]
        q32[rows(j), :] = mixed[0]
        uext[rows(j), :] = mixed[1] * mixed[2]

    @pl.loop(2, STEPS)
    def _(j):
        longer(
            j,
            [acc[p, rows(j), :] for p in range(3)],
            [acc[p, rows(j - 1), :] for p in range(3)],
            [acc[p, rows(j - 2), :] for p in range(3)],
        )

    arrived(ltail, hr.at[2])
    edge1, edge2 = [], []
    for p in range(3):
        got = ltail[p].astype(F32) * live
        edge2.append(jnp.where(first, pltpu.roll(got[:SEGS], 5, 0), pltpu.roll(acc[p, rows(62), :], 1, 0)))
        edge1.append(jnp.where(first, pltpu.roll(got[SEGS:], 5, 0), pltpu.roll(acc[p, rows(63), :], 1, 0)))
    y0 = [acc[p, rows(0), :] for p in range(3)]
    y1 = [acc[p, rows(1), :] for p in range(3)]
    longer(0, y0, edge1, edge2)
    longer(1, y1, y0, edge1)

    def row_of(ref, n, lane):
        return jnp.broadcast_to(ref[n : n + 1, lane], (SEGS, LANES))

    @pl.loop(0, WIDTH // LANES)
    def _(lt):
        lane = lanes(lt)
        decay = [jnp.exp(-row_of(rate, n, lane)) for n in range(POLES)]

        def step(j, states):
            u = uext[rows(j), lane]
            return tuple(decay[n] * states[n] + u for n in range(POLES))

        states = lax.fori_loop(0, STEPS, step, tuple(jnp.zeros((SEGS, LANES), F32) for _ in range(POLES)))
        for n in range(POLES):
            est[rows(n), lane] = states[n]

    place = seg1 % 4

    @pl.loop(0, WIDTH // LANES)
    def _(lt):
        lane = lanes(lt)
        for g in range(2):
            packed = []
            for h in range(2):
                total = jnp.zeros((SEGS, LANES), F32)
                for r in range(4):
                    n = g * 8 + h * 4 + r
                    span = jnp.exp(-float(STEPS) * row_of(rate, n, lane))
                    value = est[rows(n), lane]
                    value = value + span * jnp.where(place >= 1, pltpu.roll(value, 1, 0), 0.0)
                    value = value + span * span * jnp.where(place >= 2, pltpu.roll(value, 2, 0), 0.0)
                    est[rows(n), lane] = jnp.where(place >= 1, pltpu.roll(value, 1, 0), 0.0)
                    end = value if r == 3 else pltpu.roll(value, (r - 3) % 8, 0)
                    total = jnp.where(place == r, end, total)
                packed.append(total)
            st_s[pl.ds(g * 16, 16), lane] = jnp.concatenate(packed, axis=0).astype(BF16)

    def state_copy(d):
        return remote(st_s, st_r.at[d - 1], sts.at[d - 1], strv.at[d - 1], c + d, t)

    for d in range(15, 0, -1):

        @pl.when(c + d < 16)
        def _(d=d):
            state_copy(d).start()

    packs = []
    for g in range(4):
        total = jnp.zeros((SEGS, WIDTH), F32)
        for r in range(4):
            n = g * 4 + r
            total = jnp.where(seg % 4 == r, jnp.broadcast_to(rate[n : n + 1, :], (SEGS, WIDTH)), total)
        packs.append(total)
    pack = jnp.concatenate(packs, axis=0)
    hin[...] = jnp.zeros((4 * SEGS, WIDTH), F32)
    for d in range(1, 16):

        @pl.when(c - d >= 0)
        def _(d=d):
            arrived(st_r.at[d - 1], strv.at[d - 1])
            hin[...] += jnp.exp(pack * (-256.0 * (d - 1))) * st_r[d - 1].astype(F32)

    for kh in range(2):

        @pl.loop(0, 2)
        def _(half, kh=kh):
            lane = lanes(kh * 2 + half)
            decay, weight, states = [], [], []
            for n in range(POLES):
                r = row_of(rate, n, lane)
                decay.append(jnp.exp(-r))
                weight.append(row_of(resid, n, lane) * jnp.sqrt(1.0 - jnp.exp(-2.0 * r)))
                k = (n // 4) * SEGS + n % 4
                enter = jnp.where(
                    seg1 < 4,
                    jnp.broadcast_to(hin[k : k + 1, lane], (SEGS, LANES)),
                    jnp.broadcast_to(hin[k + 4 : k + 5, lane], (SEGS, LANES)),
                )
                states.append(est[rows(n), lane] + jnp.exp(r * (place.astype(F32) * (-float(STEPS)))) * enter)
            skip = jnp.broadcast_to(skip2[:, lane], (SEGS, LANES))
            out_lane = lanes(half)

            def step(i, states):
                pair = []
                for k in range(2):
                    u = uext[rows(2 * i + k), lane]
                    states = [decay[n] * states[n] + u for n in range(POLES)]
                    terms = [weight[n] * states[n] for n in range(POLES)]
                    while len(terms) > 1:
                        terms = [terms[a] + terms[a + 1] for a in range(0, len(terms), 2)]
                    pair.append(q32[rows(2 * i + k), lane] * (terms[0] + skip * u))
                zo[1, kh, pl.ds(pl.multiple_of(i * 16, 16), 16), out_lane] = jnp.concatenate(pair, axis=0).astype(BF16)
                return tuple(states)

            lax.fori_loop(0, STEPS // 2, step, tuple(states))

        z_copy(1, kh).start()

    project(1)
    project_wait(1)

    @pl.loop(0, 32)
    def _(i):
        base = mid[t, i // 8, pl.ds(pl.multiple_of((i % 8) * 16, 16), 16), :].astype(F32)
        value = base + arrivals(1, i)
        for k in range(WIDTH // LANES):
            part = value[:, LANES * k : LANES * (k + 1)]
            x32[1, k, pl.ds(2 * i, SEGS, stride=STEPS), :] = part[:SEGS]
            x32[1, k, pl.ds(2 * i + 1, SEGS, stride=STEPS), :] = part[SEGS:]

    @pl.loop(0, 32)
    def _(i):
        s = i // 16
        r = (i % 16) * 16
        here = pl.ds(pl.multiple_of(i * 16, 16), 16)
        value = jnp.concatenate([x32[1, k, here, :] for k in range(WIDTH // LANES)], axis=1)
        obf[s, pl.ds(pl.multiple_of(r, 16), 16), :] = value.astype(BF16)

    store = pltpu.make_async_copy(obf, out_h, loc.at[3])
    store.start()

    tail_copy.wait_send()
    u_copy.wait_send()
    l_copy.wait_send()
    weight_drain(0, wo1_h)
    weight_drain(1, wo2_h)
    project_drain(0)
    project_drain(1)
    for copy in sent:
        copy.wait_send()
    for d in range(1, 16):

        @pl.when(c + d < 16)
        def _(d=d):
            state_copy(d).wait_send()

    store.wait()


def local(
    residual_in, mr_qkv, mr_short_w, mr_filter, mr_skip, mr_out_w, lr_gain,
    lr_in_w, lr_short_w, lr_rate, lr_res, lr_skip, lr_out_w,
):
    vmem = pl.BlockSpec(memory_space=pltpu.VMEM)
    hbm = pl.BlockSpec(memory_space=pl.ANY)
    dma = pltpu.SemaphoreType.DMA
    scratch = [
        pltpu.VMEM((2, 3, 256, WIDTH), BF16),
        pltpu.VMEM((2, 3, 8, WIDTH), BF16),
        pltpu.VMEM((3, WIDTH // LANES, ROWS, LANES), F32),
        pltpu.VMEM((ROWS, WIDTH), F32),
        pltpu.VMEM((192 * SEGS, WIDTH), F32),
        pltpu.VMEM((TAPS * SEGS, WIDTH), F32),
        pltpu.VMEM((256, WIDTH), BF16),
        pltpu.VMEM((256, WIDTH), BF16),
        pltpu.VMEM((2, 2, ROWS, 256), BF16),
        pltpu.VMEM((2, 2, ROWS, 256), BF16),
        pltpu.VMEM((2, 8, 2, WIDTH, 256), BF16),
        pltpu.VMEM((3, 4096, WIDTH), BF16),
        pltpu.VMEM((2, 6, ROWS, 256), BF16),
        pltpu.VMEM((2, 6, ROWS, 256), BF16),
        pltpu.VMEM((ROWS, WIDTH), F32),
        pltpu.VMEM((8, 4, 128, WIDTH), BF16),
        pltpu.VMEM((ROWS, WIDTH), BF16),
        pltpu.VMEM((3, ROWS, WIDTH), F32),
        pltpu.VMEM((ROWS, LANES), F32),
        pltpu.VMEM((3, 16, WIDTH), BF16),
        pltpu.VMEM((3, 16, WIDTH), BF16),
        pltpu.VMEM((POLES * SEGS, WIDTH), F32),
        pltpu.VMEM((4 * SEGS, WIDTH), BF16),
        pltpu.VMEM((15, 4 * SEGS, WIDTH), BF16),
        pltpu.VMEM((4 * SEGS, WIDTH), F32),
        pltpu.VMEM((2, 256, WIDTH), BF16),
        pltpu.VMEM((2, 256, WIDTH), BF16),
        dma((4,)),
        dma((3,)),
        dma((3,)),
        dma((2, 3)),
        dma((2, 2, 4)),
        dma((2, 8)),
        dma((2, 8, 2)),
        dma((2, 2)),
        dma((2, 2)),
        dma((2, 6)),
        dma((2, 6)),
        dma((32,)),
        dma((8, 4)),
        dma((15,)),
        dma((15,)),
    ]
    return pl.pallas_call(
        kernel,
        out_shape=jax.ShapeDtypeStruct((2, 256, WIDTH), BF16),
        in_specs=[hbm, hbm, vmem, vmem, vmem, hbm, vmem, hbm, vmem, vmem, vmem, vmem, hbm],
        out_specs=hbm,
        scratch_shapes=scratch,
        compiler_params=pltpu.CompilerParams(
            collective_id=0, has_side_effects=True, vmem_limit_bytes=62 * 1024 * 1024
        ),
    )(
        residual_in,
        jnp.transpose(mr_qkv, (0, 2, 1, 3)),
        mr_short_w,
        mr_filter,
        mr_skip.reshape(1, WIDTH),
        mr_out_w,
        lr_gain.reshape(1, 8 * WIDTH),
        jnp.transpose(lr_in_w, (1, 0, 2)),
        lr_short_w,
        lr_rate,
        lr_res,
        lr_skip.reshape(1, WIDTH),
        lr_out_w,
    )


def solution(mesh):
    in_specs = (
        P(None, "ctx", "tp"),
        P(None, "ctx", None, "tp"),
        P(None, None, "tp"),
        P(None, "tp"),
        P("tp"),
        P("tp", "ctx"),
        P(),
        P(None, None, "tp"),
        P(None, None, "tp"),
        P(None, "tp"),
        P(None, "tp"),
        P("tp"),
        P("tp", "ctx"),
    )
    return jax.shard_map(local, mesh=mesh, in_specs=in_specs, out_specs=P(None, "ctx", "tp"), check_vma=False)
```

```python
import jax
import jax.numpy as jnp
from jax import lax
from jax.experimental import pallas as pl
from jax.experimental.pallas import tpu as pltpu
from jax.sharding import PartitionSpec as P

MESH = pl.DeviceIdType.MESH
F32 = jnp.float32
BF16 = jnp.bfloat16

SEGS = 8
STEPS = 64
ROWS = SEGS * STEPS
WIDTH = 512
TAPS = 128
POLES = 16
LANES = 128


def kernel(
    res_h, qkv_h, sw1, filt, skip1, wo1_h, gain, win_h, sw2, rate, resid, skip2, wo2_h,
    out_h,
    qkv_v, xtail, x32, q32, uext, fb, pk_s, pk_r, zo, zn, w, win, ps, pr, pacc, mid, scaled, acc, ssq,
    ltail_s, ltail, est, st_s, st_r, hin, obf, resv,
    loc, hs, hr, wsnd, fsnd, bsnd, wrecv, zs, zr, pss, prs, ags, agr, sts, strv,
):
    c = lax.axis_index("ctx")
    t = lax.axis_index("tp")
    core = c % 2
    m = c // 2
    y = m % 4
    xh = m // 4
    z = t // 2
    xl = t % 2
    sib = c + 1 - 2 * core
    xn = t + 1 - 2 * xl

    def ztp(dz, x):
        return ((z + dz) % 4) * 2 + x

    def remote(src, dst, ssem, rsem, ctx, tp):
        return pltpu.make_async_remote_copy(
            src_ref=src,
            dst_ref=dst,
            send_sem=ssem,
            recv_sem=rsem,
            device_id={"ctx": ctx, "tp": tp},
            device_id_type=MESH,
        )

    def arrived(ref, sem):
        pltpu.make_async_copy(ref, ref, sem).wait()

    load_qkv = pltpu.make_async_copy(qkv_h, qkv_v, loc.at[0])
    load_qkv.start()
    load_res = pltpu.make_async_copy(res_h, resv, loc.at[1])
    load_res.start()

    barrier = pltpu.get_barrier_semaphore()

    def greet(ctx, tp):
        pl.semaphore_signal(barrier, inc=1, device_id={"ctx": ctx, "tp": tp}, device_id_type=MESH)

    for d in range(1, 16):
        greet((c + d) % 16, t)
    greet(c, xn)
    greet((c + 8) % 16, xn)
    greet(c, ztp(1, xl))
    greet(c, ztp(3, xl))
    pl.semaphore_wait(barrier, 19)

    tail_copy = remote(qkv_h.at[:, :, 248:256, :], xtail, hs.at[0], hr.at[0], (c + 1) % 16, t)
    tail_copy.start()

    holder = (y + xl) % 2 == 0
    relay = (y + xl) % 2 == 1
    ups = ((y + 1) % 4, (y + 3) % 4)

    def place_of(k, row):
        xs = (xl, 1 - xl, 1 - xl, xl)[k]
        xhs = (xh, xh, 1 - xh, 1 - xh)[k]
        return xs * 4 + xhs * 2 + row // 2

    def ctx_of(h, row):
        return (h * 4 + row) * 2 + core

    def weight_first(stage, source):
        mine = place_of(0, y)
        target = w.at[stage, mine, core]
        arrival = wrecv.at[stage, mine, core]
        home = pltpu.make_async_copy(source, target, arrival)
        along = [
            remote(source, target, wsnd.at[stage, 0], arrival, ctx_of(xh, ups[0]), t),
            remote(source, target, wsnd.at[stage, 1], arrival, ctx_of(xh, ups[1]), t),
            remote(source, target, wsnd.at[stage, 2], arrival, ctx_of(1 - xh, y), t),
        ]
        across = [
            remote(source, target, wsnd.at[stage, 0], arrival, c, xn),
            remote(source, target, wsnd.at[stage, 1], arrival, ctx_of(1 - xh, y), xn),
        ]
        return home, along, across

    def weight_start(stage, source):
        home, along, across = weight_first(stage, source)

        @pl.when(holder)
        def _():
            home.start()
            for copy in along:
                copy.start()

        @pl.when(relay)
        def _():
            for copy in across:
                copy.start()

    def weight_pass(stage, index, sem, ctx):
        block = w.at[stage, index, core]
        return remote(block, block, sem, wrecv.at[stage, index, core], ctx, t)

    def weight_got(stage, index):
        arrived(w.at[stage, index, core], wrecv.at[stage, index, core])

    def weight_moves(stage, k):
        here, up, down, far = place_of(k, y), place_of(k, ups[0]), place_of(k, ups[1]), place_of(k, (y + 2) % 4)

        def sibling(index, n):
            return weight_pass(stage, index, bsnd.at[stage, n], sib)

        held = [sibling(here, k)]
        if k:
            held += [weight_pass(stage, here, fsnd.at[stage, n, k], ctx_of(xh, ups[n])) for n in range(2)]
        late = [sibling(far, 4 + k)]
        below = [sibling(down, k)]
        above = [sibling(up, 4 + k)]
        if k % 2 == 0:
            below.append(weight_pass(stage, down, fsnd.at[stage, 0, k], ctx_of(xh, ups[0])))
        else:
            above.append(weight_pass(stage, up, fsnd.at[stage, 0, k], ctx_of(xh, ups[1])))
        return (here, held), (far, late), (down, below), (up, above)

    def weight_hold(stage, *ks):
        @pl.when(holder)
        def _():
            for k in ks:
                first_ = weight_moves(stage, k)[0]
                weight_got(stage, first_[0])
                for copy in reversed(first_[1]):
                    copy.start()

    def weight_relay(stage, k):
        _, _, below, above = weight_moves(stage, k)

        @pl.when(relay)
        def _():
            for index, copies in (below, above):
                weight_got(stage, index)
                for copy in reversed(copies):
                    copy.start()

    def weight_last(stage):
        @pl.when(holder)
        def _():
            for k in range(4):
                _, (index, copies), _, _ = weight_moves(stage, k)
                weight_got(stage, index)
                copies[0].start()

    def weight_sibling(stage, index):
        arrived(w.at[stage, index, 1 - core], wrecv.at[stage, index, 1 - core])

    def weight_drain(stage, source):
        _, along, across = weight_first(stage, source)

        @pl.when(holder)
        def _():
            for copy in along:
                copy.wait_send()
            for k in range(4):
                first_, late, _, _ = weight_moves(stage, k)
                for copy in first_[1] + late[1]:
                    copy.wait_send()

        @pl.when(relay)
        def _():
            for copy in across:
                copy.wait_send()
            for k in range(4):
                _, _, below, above = weight_moves(stage, k)
                for copy in below[1] + above[1]:
                    copy.wait_send()

    weight_start(0, wo1_h)
    load_win = pltpu.make_async_copy(win_h, win, loc.at[2])

    seg = lax.broadcasted_iota(jnp.int32, (SEGS, WIDTH), 0)
    seg1 = lax.broadcasted_iota(jnp.int32, (SEGS, LANES), 0)
    first = seg % 4 == 0
    live = jnp.where(c > 0, 1.0, 0.0).astype(F32)

    def rows(j, count=1):
        start = j * SEGS
        return pl.ds(start if isinstance(start, int) else pl.multiple_of(start, SEGS), count * SEGS)

    def lanes(lt):
        return pl.ds(pl.multiple_of(lt * LANES, LANES), LANES)

    @pl.loop(0, TAPS // 8)
    def _(i):
        taps = filt[pl.ds(pl.multiple_of(i * 8, 8), 8), :].astype(F32)
        for k in range(8):
            fb[rows(i * 8 + k), :] = jnp.broadcast_to(taps[k : k + 1, :], (SEGS, WIDTH))

    load_qkv.wait()
    for s in range(2):
        for p in range(3):

            @pl.loop(0, 16)
            def _(i, s=s, p=p):
                here = pl.ds(pl.multiple_of(i * 16, 16), 16)
                there = pl.ds(pl.multiple_of(s * 256 + i * 16, 16), 16)
                values = qkv_v[s, p, here, :].astype(F32)
                for k in range(WIDTH // LANES):
                    x32[p, k, there, :] = values[:, LANES * k : LANES * (k + 1)]

    def tap(ref, lag, p):
        return jnp.broadcast_to(ref[lag, p : p + 1, :], (SEGS, WIDTH))

    def strided3(p, j):
        return jnp.concatenate(
            [x32[p, k, pl.ds(j, SEGS, stride=STEPS), :] for k in range(WIDTH // LANES)], axis=1
        )

    def medium(j, now, before, before2):
        mixed = [tap(sw1, 0, p) * now[p] + tap(sw1, 1, p) * before[p] + tap(sw1, 2, p) * before2[p] for p in range(3)]
        q32[rows(j), :] = mixed[0]
        uext[rows(j + 128), :] = (mixed[1] * mixed[2]).astype(BF16).astype(F32)

    last = [strided3(p, 63) for p in range(3)]
    last2 = [strided3(p, 62) for p in range(3)]
    x0 = [strided3(p, 0) for p in range(3)]
    x1 = [strided3(p, 1) for p in range(3)]
    own1 = [jnp.where(first, 0.0, pltpu.roll(v, 1, 0)) for v in last]
    own2 = [jnp.where(first, 0.0, pltpu.roll(v, 1, 0)) for v in last2]
    medium(0, x0, own1, own2)
    medium(1, x1, x0, own1)

    def medium_step(j, carried):
        now = [strided3(p, j) for p in range(3)]
        before, before2 = carried
        medium(j, now, before, before2)
        return now, before

    lax.fori_loop(2, STEPS, medium_step, (x1, x0))

    @pl.loop(0, STEPS // 4)
    def _(i):
        packed = []
        for k in range(2):
            even = uext[rows(128 + 4 * i + 2 * k), :]
            odd = uext[rows(129 + 4 * i + 2 * k), :]
            packed.append(jnp.where(seg % 4 >= 2, even, pltpu.roll(odd, 6, 0)))
        pk_s[pl.ds(pl.multiple_of(i * 16, 16), 16), :] = jnp.concatenate(packed, axis=0).astype(BF16)

    u_copy = remote(pk_s, pk_r, hs.at[1], hr.at[1], (c + 1) % 16, t)
    u_copy.start()
    weight_hold(0, 0)
    weight_relay(0, 0)

    arrived(xtail, hr.at[0])

    def halo(p, row):
        top = xtail[0, p].astype(F32)[row : row + 1, :] * live
        bottom = xtail[1, p].astype(F32)[row : row + 1, :] * live
        return jnp.where(seg < 4, jnp.broadcast_to(top, (SEGS, WIDTH)), jnp.broadcast_to(bottom, (SEGS, WIDTH)))

    full1 = [jnp.where(first, halo(p, 7), own1[p]) for p in range(3)]
    full2 = [jnp.where(first, halo(p, 6), own2[p]) for p in range(3)]
    medium(0, x0, full1, full2)
    medium(1, x1, x0, full1)

    load_win.start()
    arrived(pk_r, hr.at[1])

    @pl.loop(0, STEPS // 2)
    def _(i):
        both = pk_r[pl.ds(pl.multiple_of((i // 2) * 16, 16), 16), :].astype(F32) * live
        got = jnp.where(i % 2 == 0, both[:SEGS], both[SEGS:])
        even = uext[rows(128 + 2 * i), :]
        odd = uext[rows(129 + 2 * i), :]
        uext[rows(64 + 2 * i), :] = jnp.where(first, pltpu.roll(got, 5, 0), pltpu.roll(even, 1, 0))
        uext[rows(65 + 2 * i), :] = jnp.where(first, pltpu.roll(got, 7, 0), pltpu.roll(odd, 1, 0))
        uext[rows(2 * i), :] = jnp.where(seg % 4 < 2, pltpu.roll(got, 6, 0), pltpu.roll(even, 2, 0))
        uext[rows(1 + 2 * i), :] = jnp.where(seg % 4 < 2, got, pltpu.roll(odd, 2, 0))

    weight_hold(0, 1, 2)

    HALF = ROWS // 2

    def z_copy(stage, part):
        return remote(zo.at[stage, part], zn.at[stage, part], zs.at[stage, part], zr.at[stage, part], c, xn)

    def p_copy(stage, part, i):
        return remote(
            ps.at[stage, part, i],
            pr.at[stage, part, i],
            pss.at[stage, part, i],
            prs.at[stage, part, i],
            c,
            ztp(1 if i % 2 == 0 else 3, xl),
        )

    def term(stage, part, d, half):
        dest = (z + d) % 4
        both = jnp.concatenate([zo[stage, part], zn[stage, part]], axis=1)
        weights = jnp.concatenate([w[stage, xl * 4 + dest, half], w[stage, (1 - xl) * 4 + dest, half]], axis=0)
        return jnp.dot(both, weights, preferred_element_type=F32)

    def project_first(stage, part):
        arrived(zn.at[stage, part], zr.at[stage, part])
        for i, d, half in ((0, 2, 0), (1, 2, 1), (2, 1, 1), (3, 3, 0)):
            if part == 0 and i in (0, 2, 3):
                for source in range(2):
                    weight_sibling(stage, source * 4 + (z + d) % 4)
            ps[stage, part, i] = term(stage, part, d, half).astype(BF16)
            p_copy(stage, part, i).start()

    def project_own(stage, part):
        if part == 0:
            for source in range(2):
                weight_sibling(stage, source * 4 + z)
        for own in range(2):
            pacc[HALF * part : HALF * (part + 1), 256 * own : 256 * (own + 1)] = term(stage, part, 0, own)

    def project_relay(stage, part):
        for i, d, half in ((4, 1, 0), (5, 3, 1)):
            mine = term(stage, part, d, half)
            arrived(pr.at[stage, part, i - 4], prs.at[stage, part, i - 4])
            ps[stage, part, i] = (mine + pr[stage, part, i - 4].astype(F32)).astype(BF16)
            p_copy(stage, part, i).start()

    def project(stage):
        project_first(stage, 0)
        project_first(stage, 1)
        project_relay(stage, 0)
        project_own(stage, 0)
        project_relay(stage, 1)
        project_own(stage, 1)

    def project_wait(stage, part):
        for i in (2, 3, 4, 5):
            arrived(pr.at[stage, part, i], prs.at[stage, part, i])

    def project_drain(stage):
        for part in range(2):
            z_copy(stage, part).wait_send()
            for i in range(6):
                p_copy(stage, part, i).wait_send()

    def arrivals(stage, part, i):
        here = pl.ds(pl.multiple_of(i * 16, 16), 16)
        left = pr[stage, part, 3, here, :].astype(F32) + pr[stage, part, 4, here, :].astype(F32)
        right = pr[stage, part, 2, here, :].astype(F32) + pr[stage, part, 5, here, :].astype(F32)
        own = pacc[pl.ds(pl.multiple_of(part * HALF + i * 16, 16), 16), :]
        return own + jnp.concatenate([left, right], axis=1)

    def filter_blocks(first_block):
        @pl.loop(first_block, first_block + 4)
        def _(block):
            lane = lanes((block % 8) // 2)
            part = block // 8
            r0 = (block % 2) * 16
            j0 = part * 32 + r0

            def taps8(ib, totals):
                base = 128 + j0 - 8 * ib - 7
                window = uext[pl.ds(pl.multiple_of(base * SEGS, SEGS), 23 * SEGS), lane]
                weights = fb[pl.ds(pl.multiple_of(ib * 64, 64), 64), lane]
                totals = list(totals)
                for b in range(8):
                    f = weights[b * SEGS : (b + 1) * SEGS]
                    for a in range(16):
                        k = a + 7 - b
                        totals[a] = totals[a] + f * window[k * SEGS : (k + 1) * SEGS]
                return tuple(totals)

            totals = lax.fori_loop(0, 16, taps8, tuple(jnp.zeros((SEGS, LANES), F32) for _ in range(16)))
            skip = jnp.broadcast_to(skip1[:, lane], (SEGS, LANES))
            for a in range(0, 16, 2):
                pair = []
                for k in (a, a + 1):
                    u = uext[rows(128 + j0 + k), lane]
                    pair.append(q32[rows(j0 + k), lane] * (totals[k] + skip * u))
                zo[0, part, pl.ds(pl.multiple_of((r0 + a) * SEGS, 16), 16), lane] = jnp.concatenate(
                    pair, axis=0
                ).astype(BF16)

    filter_blocks(0)
    weight_hold(0, 3)
    weight_relay(0, 1)
    filter_blocks(4)
    z_copy(0, 0).start()
    weight_relay(0, 2)
    filter_blocks(8)
    filter_blocks(12)
    z_copy(0, 1).start()
    weight_relay(0, 3)
    weight_last(0)
    weight_start(1, wo2_h)

    load_res.wait()

    @pl.loop(0, 32)
    def _(i):
        s = i // 16
        r = (i % 16) * 16
        values = resv[s, pl.ds(pl.multiple_of(r, 16), 16), :].astype(F32)
        for k in range(WIDTH // LANES):
            x32[0, k, pl.ds(pl.multiple_of(i * 16, 16), 16), :] = values[:, LANES * k : LANES * (k + 1)]

    @pl.loop(0, STEPS)
    def _(j):
        for k in range(WIDTH // LANES):
            x32[1, k, rows(j), :] = x32[0, k, pl.ds(j, SEGS, stride=STEPS), :]

    project(0)
    weight_hold(1, 0, 1, 2)
    weight_relay(1, 0)

    sent = []

    def send(slot, quarter, tp):
        k = len(sent)
        copy = remote(
            mid.at[slot, quarter], mid.at[slot, quarter], ags.at[k], agr.at[slot, quarter], c, tp
        )
        copy.start()
        sent.append(copy)

    zp, zm, zz = ztp(1, xl), ztp(3, xl), ztp(2, xl)
    xp, xm, xz = ztp(1, 1 - xl), ztp(3, 1 - xl), ztp(2, 1 - xl)
    for part in range(2):
        project_wait(0, part)

        @pl.loop(0, 16)
        def _(i, part=part):
            here = pl.ds(pl.multiple_of(part * HALF + i * 16, 16), 16)
            before = jnp.concatenate([x32[1, k, here, :] for k in range(WIDTH // LANES)], axis=1)
            value = (before + arrivals(0, part, i)).astype(BF16)
            mid[t, part * 2 + i // 8, pl.ds(pl.multiple_of((i % 8) * 16, 16), 16), :] = value

        for quarter in (2 * part, 2 * part + 1):
            send(t, quarter, xn)
            send(t, quarter, zp)
            send(t, quarter, zm)

    def have(slot, *quarters):
        for quarter in quarters:
            arrived(mid.at[slot, quarter], agr.at[slot, quarter])

    load_win.wait()

    def absorb(*slots, fresh=False):
        count = len(slots)
        scales = [gain[:, pl.ds(pl.multiple_of(slot * WIDTH, WIDTH), WIDTH)] for slot in slots]

        @pl.loop(0, 16)
        def _(i):
            here = pl.ds(pl.multiple_of((i % 4) * 32, 32), 32)
            there = pl.ds(pl.multiple_of(i * 32, 32), 32)
            total = 0.0 if fresh else ssq[there, :]
            for k, slot in enumerate(slots):
                values = mid[slot, i // 4, here, :].astype(F32)
                square = values * values
                total += square[:, 0:128] + square[:, 128:256] + square[:, 256:384] + square[:, 384:512]
                scaled[there, WIDTH * k : WIDTH * (k + 1)] = (values * scales[k]).astype(BF16)
            ssq[there, :] = total

        @pl.loop(0, 6)
        def _(i):
            cols = pl.ds(pl.multiple_of((i % 2) * 256, 256), 256)
            weights = [win[i // 2, pl.ds(pl.multiple_of(slot * WIDTH, WIDTH), WIDTH), cols] for slot in slots]
            product = jnp.dot(
                scaled[:, 0 : WIDTH * count], jnp.concatenate(weights, axis=0), preferred_element_type=F32
            )
            acc[i // 2, :, cols] = product if fresh else acc[i // 2, :, cols] + product

    absorb(t, fresh=True)
    weight_hold(1, 3)
    weight_relay(1, 1)
    have(xn, 0, 1)
    for quarter in range(2):
        send(xn, quarter, zp)
        send(xn, quarter, zm)
    have(zm, 0, 1, 2, 3)
    send(zm, 0, zp)
    send(zm, 2, zp)
    send(zm, 2, xn)
    send(zm, 3, xn)
    have(zp, 0, 1, 2, 3)
    send(zp, 1, zm)
    send(zp, 3, zm)
    send(zp, 2, xn)
    send(zp, 3, xn)
    absorb(zm, zp)
    weight_relay(1, 2)
    have(xm, 0, 1)
    send(xm, 0, zp)
    have(xp, 0, 1)
    send(xp, 1, zm)
    have(zz, 0, 1, 2, 3)
    send(zz, 2, xn)
    send(zz, 3, xn)
    have(xn, 2, 3)
    absorb(xn, zz)
    weight_relay(1, 3)
    have(xm, 2, 3)
    have(xp, 2, 3)
    absorb(xm, xp)
    have(xz, 0, 1, 2, 3)
    absorb(xz)
    weight_last(1)

    def finish(i):
        here = pl.ds(i * 16 if isinstance(i, int) else pl.multiple_of(i * 16, 16), 16)
        meansq = jnp.sum(ssq[here, :], axis=1, keepdims=True) * (1.0 / 4096.0)
        factor = lax.rsqrt(meansq + 1e-6)
        values = [(acc[p, here, :] * factor).astype(BF16) for p in range(3)]
        for p in range(3):
            acc[p, here, :] = values[p].astype(F32)
        return values

    tails = finish(31)
    for p in range(3):
        ltail_s[p] = tails[p]
    l_copy = remote(ltail_s, ltail, hs.at[2], hr.at[2], (c + 1) % 16, t)
    l_copy.start()

    @pl.loop(0, 31)
    def _(i):
        finish(i)

    def longer(j, now, before, before2):
        mixed = [tap(sw2, 0, p) * now[p] + tap(sw2, 1, p) * before[p] + tap(sw2, 2, p) * before2[p] for p in range(3)]
        q32[rows(j), :] = mixed[0]
        uext[rows(j), :] = mixed[1] * mixed[2]

    @pl.loop(2, STEPS)
    def _(j):
        longer(
            j,
            [acc[p, rows(j), :] for p in range(3)],
            [acc[p, rows(j - 1), :] for p in range(3)],
            [acc[p, rows(j - 2), :] for p in range(3)],
        )

    arrived(ltail, hr.at[2])
    edge1, edge2 = [], []
    for p in range(3):
        got = ltail[p].astype(F32) * live
        edge2.append(jnp.where(first, pltpu.roll(got[:SEGS], 5, 0), pltpu.roll(acc[p, rows(62), :], 1, 0)))
        edge1.append(jnp.where(first, pltpu.roll(got[SEGS:], 5, 0), pltpu.roll(acc[p, rows(63), :], 1, 0)))
    y0 = [acc[p, rows(0), :] for p in range(3)]
    y1 = [acc[p, rows(1), :] for p in range(3)]
    longer(0, y0, edge1, edge2)
    longer(1, y1, y0, edge1)

    def row_of(ref, n, lane):
        return jnp.broadcast_to(ref[n : n + 1, lane], (SEGS, LANES))

    @pl.loop(0, WIDTH // LANES)
    def _(lt):
        lane = lanes(lt)
        decay = [jnp.exp(-row_of(rate, n, lane)) for n in range(POLES)]

        def step(j, states):
            u = uext[rows(j), lane]
            return tuple(decay[n] * states[n] + u for n in range(POLES))

        states = lax.fori_loop(0, STEPS, step, tuple(jnp.zeros((SEGS, LANES), F32) for _ in range(POLES)))
        for n in range(POLES):
            est[rows(n), lane] = states[n]

    place = seg1 % 4

    @pl.loop(0, WIDTH // LANES)
    def _(lt):
        lane = lanes(lt)
        for g in range(2):
            packed = []
            for h in range(2):
                total = jnp.zeros((SEGS, LANES), F32)
                for r in range(4):
                    n = g * 8 + h * 4 + r
                    span = jnp.exp(-float(STEPS) * row_of(rate, n, lane))
                    value = est[rows(n), lane]
                    value = value + span * jnp.where(place >= 1, pltpu.roll(value, 1, 0), 0.0)
                    value = value + span * span * jnp.where(place >= 2, pltpu.roll(value, 2, 0), 0.0)
                    est[rows(n), lane] = jnp.where(place >= 1, pltpu.roll(value, 1, 0), 0.0)
                    end = value if r == 3 else pltpu.roll(value, (r - 3) % 8, 0)
                    total = jnp.where(place == r, end, total)
                packed.append(total)
            st_s[pl.ds(g * 16, 16), lane] = jnp.concatenate(packed, axis=0).astype(BF16)

    def state_copy(d):
        return remote(st_s, st_r.at[d - 1], sts.at[d - 1], strv.at[d - 1], c + d, t)

    for d in range(15, 0, -1):

        @pl.when(c + d < 16)
        def _(d=d):
            state_copy(d).start()

    packs = []
    for g in range(4):
        total = jnp.zeros((SEGS, WIDTH), F32)
        for r in range(4):
            n = g * 4 + r
            total = jnp.where(seg % 4 == r, jnp.broadcast_to(rate[n : n + 1, :], (SEGS, WIDTH)), total)
        packs.append(total)
    pack = jnp.concatenate(packs, axis=0)
    hin[...] = jnp.zeros((4 * SEGS, WIDTH), F32)
    for d in range(1, 16):

        @pl.when(c - d >= 0)
        def _(d=d):
            arrived(st_r.at[d - 1], strv.at[d - 1])
            hin[...] += jnp.exp(pack * (-256.0 * (d - 1))) * st_r[d - 1].astype(F32)

    for part in range(2):

        @pl.loop(0, WIDTH // LANES)
        def _(lt, part=part):
            lane = lanes(lt)
            decay, weight, states = [], [], []
            for n in range(POLES):
                r = row_of(rate, n, lane)
                decay.append(jnp.exp(-r))
                weight.append(row_of(resid, n, lane) * jnp.sqrt(1.0 - jnp.exp(-2.0 * r)))
                state = est[rows(n), lane]
                if part == 0:
                    k = (n // 4) * SEGS + n % 4
                    enter = jnp.where(
                        seg1 < 4,
                        jnp.broadcast_to(hin[k : k + 1, lane], (SEGS, LANES)),
                        jnp.broadcast_to(hin[k + 4 : k + 5, lane], (SEGS, LANES)),
                    )
                    state = state + jnp.exp(r * (place.astype(F32) * (-float(STEPS)))) * enter
                states.append(state)
            skip = jnp.broadcast_to(skip2[:, lane], (SEGS, LANES))

            def step(i, states):
                pair = []
                for k in range(2):
                    j = part * (STEPS // 2) + 2 * i + k
                    u = uext[rows(j), lane]
                    states = [decay[n] * states[n] + u for n in range(POLES)]
                    terms = [weight[n] * states[n] for n in range(POLES)]
                    while len(terms) > 1:
                        terms = [terms[a] + terms[a + 1] for a in range(0, len(terms), 2)]
                    pair.append(q32[rows(j), lane] * (terms[0] + skip * u))
                zo[1, part, pl.ds(pl.multiple_of(i * 16, 16), 16), lane] = jnp.concatenate(pair, axis=0).astype(BF16)
                return tuple(states)

            states = lax.fori_loop(0, STEPS // 4, step, tuple(states))
            if part == 0:
                for n in range(POLES):
                    est[rows(n), lane] = states[n]

        z_copy(1, part).start()

    project(1)
    for part in range(2):
        project_wait(1, part)

        @pl.loop(0, 16)
        def _(i, part=part):
            base = mid[t, part * 2 + i // 8, pl.ds(pl.multiple_of((i % 8) * 16, 16), 16), :].astype(F32)
            value = base + arrivals(1, part, i)
            j = part * (STEPS // 2) + 2 * i
            for k in range(WIDTH // LANES):
                piece = value[:, LANES * k : LANES * (k + 1)]
                x32[2, k, pl.ds(j, SEGS, stride=STEPS), :] = piece[:SEGS]
                x32[2, k, pl.ds(j + 1, SEGS, stride=STEPS), :] = piece[SEGS:]

    @pl.loop(0, 32)
    def _(i):
        s = i // 16
        r = (i % 16) * 16
        here = pl.ds(pl.multiple_of(i * 16, 16), 16)
        value = jnp.concatenate([x32[2, k, here, :] for k in range(WIDTH // LANES)], axis=1)
        obf[s, pl.ds(pl.multiple_of(r, 16), 16), :] = value.astype(BF16)

    store = pltpu.make_async_copy(obf, out_h, loc.at[3])
    store.start()

    tail_copy.wait_send()
    u_copy.wait_send()
    l_copy.wait_send()
    weight_drain(0, wo1_h)
    weight_drain(1, wo2_h)
    project_drain(0)
    project_drain(1)
    for copy in sent:
        copy.wait_send()
    for d in range(1, 16):

        @pl.when(c + d < 16)
        def _(d=d):
            state_copy(d).wait_send()

    store.wait()


def local(
    residual_in, mr_qkv, mr_short_w, mr_filter, mr_skip, mr_out_w, lr_gain,
    lr_in_w, lr_short_w, lr_rate, lr_res, lr_skip, lr_out_w,
):
    vmem = pl.BlockSpec(memory_space=pltpu.VMEM)
    hbm = pl.BlockSpec(memory_space=pl.ANY)
    dma = pltpu.SemaphoreType.DMA
    scratch = [
        pltpu.VMEM((2, 3, 256, WIDTH), BF16),
        pltpu.VMEM((2, 3, 8, WIDTH), BF16),
        pltpu.VMEM((3, WIDTH // LANES, ROWS, LANES), F32),
        pltpu.VMEM((ROWS, WIDTH), F32),
        pltpu.VMEM((192 * SEGS, WIDTH), F32),
        pltpu.VMEM((TAPS * SEGS, WIDTH), F32),
        pltpu.VMEM((256, WIDTH), BF16),
        pltpu.VMEM((256, WIDTH), BF16),
        pltpu.VMEM((2, 2, ROWS // 2, WIDTH), BF16),
        pltpu.VMEM((2, 2, ROWS // 2, WIDTH), BF16),
        pltpu.VMEM((2, 8, 2, WIDTH, 256), BF16),
        pltpu.VMEM((3, 4096, WIDTH), BF16),
        pltpu.VMEM((2, 2, 6, ROWS // 2, 256), BF16),
        pltpu.VMEM((2, 2, 6, ROWS // 2, 256), BF16),
        pltpu.VMEM((ROWS, WIDTH), F32),
        pltpu.VMEM((8, 4, 128, WIDTH), BF16),
        pltpu.VMEM((ROWS, 2 * WIDTH), BF16),
        pltpu.VMEM((3, ROWS, WIDTH), F32),
        pltpu.VMEM((ROWS, LANES), F32),
        pltpu.VMEM((3, 16, WIDTH), BF16),
        pltpu.VMEM((3, 16, WIDTH), BF16),
        pltpu.VMEM((POLES * SEGS, WIDTH), F32),
        pltpu.VMEM((4 * SEGS, WIDTH), BF16),
        pltpu.VMEM((15, 4 * SEGS, WIDTH), BF16),
        pltpu.VMEM((4 * SEGS, WIDTH), F32),
        pltpu.VMEM((2, 256, WIDTH), BF16),
        pltpu.VMEM((2, 256, WIDTH), BF16),
        dma((4,)),
        dma((3,)),
        dma((3,)),
        dma((2, 3)),
        dma((2, 2, 4)),
        dma((2, 8)),
        dma((2, 8, 2)),
        dma((2, 2)),
        dma((2, 2)),
        dma((2, 2, 6)),
        dma((2, 2, 6)),
        dma((32,)),
        dma((8, 4)),
        dma((15,)),
        dma((15,)),
    ]
    return pl.pallas_call(
        kernel,
        out_shape=jax.ShapeDtypeStruct((2, 256, WIDTH), BF16),
        in_specs=[hbm, hbm, vmem, vmem, vmem, hbm, vmem, hbm, vmem, vmem, vmem, vmem, hbm],
        out_specs=hbm,
        scratch_shapes=scratch,
        compiler_params=pltpu.CompilerParams(
            collective_id=0, has_side_effects=True, vmem_limit_bytes=62 * 1024 * 1024
        ),
    )(
        residual_in,
        jnp.transpose(mr_qkv, (0, 2, 1, 3)),
        mr_short_w,
        mr_filter,
        mr_skip.reshape(1, WIDTH),
        mr_out_w,
        lr_gain.reshape(1, 8 * WIDTH),
        jnp.transpose(lr_in_w, (1, 0, 2)),
        lr_short_w,
        lr_rate,
        lr_res,
        lr_skip.reshape(1, WIDTH),
        lr_out_w,
    )


def solution(mesh):
    in_specs = (
        P(None, "ctx", "tp"),
        P(None, "ctx", None, "tp"),
        P(None, None, "tp"),
        P(None, "tp"),
        P("tp"),
        P("tp", "ctx"),
        P(),
        P(None, None, "tp"),
        P(None, None, "tp"),
        P(None, "tp"),
        P(None, "tp"),
        P("tp"),
        P("tp", "ctx"),
    )
    return jax.shard_map(local, mesh=mesh, in_specs=in_specs, out_specs=P(None, "ctx", "tp"), check_vma=False)
```

```python
import jax
import jax.numpy as jnp
from jax import lax
from jax.experimental import pallas as pl
from jax.experimental.pallas import tpu as pltpu
from jax.sharding import PartitionSpec as P

MESH = pl.DeviceIdType.MESH
F32 = jnp.float32
BF16 = jnp.bfloat16

SEGS = 8
STEPS = 64
ROWS = SEGS * STEPS
WIDTH = 512
TAPS = 128
POLES = 16
LANES = 128


def kernel(
    res_h, qkv_h, sw1, filt, skip1, wo1_h, gain, win_h, sw2, rate, resid, skip2, wo2_h,
    out_h,
    qkv_v, xtail, x32, q32, uext, fb, pk_s, pk_r, zo, zn, w, win, ps, pr, pacc, mid, scaled, acc, ssq,
    ltail_s, ltail, est, st_s, st_r, hin, obf, resv,
    loc, hs, hr, wsnd, fsnd, bsnd, wrecv, zs, zr, pss, prs, ags, agr, sts, strv,
):
    c = lax.axis_index("ctx")
    t = lax.axis_index("tp")
    core = c % 2
    m = c // 2
    y = m % 4
    xh = m // 4
    z = t // 2
    xl = t % 2
    sib = c + 1 - 2 * core
    xn = t + 1 - 2 * xl

    def ztp(dz, x):
        return ((z + dz) % 4) * 2 + x

    def remote(src, dst, ssem, rsem, ctx, tp):
        return pltpu.make_async_remote_copy(
            src_ref=src,
            dst_ref=dst,
            send_sem=ssem,
            recv_sem=rsem,
            device_id={"ctx": ctx, "tp": tp},
            device_id_type=MESH,
        )

    def arrived(ref, sem):
        pltpu.make_async_copy(ref, ref, sem).wait()

    load_qkv = pltpu.make_async_copy(qkv_h, qkv_v, loc.at[0])
    load_qkv.start()
    load_res = pltpu.make_async_copy(res_h, resv, loc.at[1])
    load_res.start()

    barrier = pltpu.get_barrier_semaphore()

    def greet(ctx, tp):
        pl.semaphore_signal(barrier, inc=1, device_id={"ctx": ctx, "tp": tp}, device_id_type=MESH)

    for d in range(1, 16):
        greet((c + d) % 16, t)
    greet(c, xn)
    greet((c + 8) % 16, xn)
    greet(c, ztp(1, xl))
    greet(c, ztp(3, xl))
    pl.semaphore_wait(barrier, 19)

    tail_copy = remote(qkv_h.at[:, :, 248:256, :], xtail, hs.at[0], hr.at[0], (c + 1) % 16, t)
    tail_copy.start()

    holder = (y + xl) % 2 == 0
    relay = (y + xl) % 2 == 1
    ups = ((y + 1) % 4, (y + 3) % 4)
    late_h = ((z + 2) % 4 // 2 + xh) % 2
    odd = z % 2

    def place_of(k, row):
        turn_h = (0, late_h, 1, 1 - late_h)[k]
        turn_l = (0, 1, 1 - late_h, late_h)[k]
        return (xl + turn_l) % 2 * 4 + (xh + turn_h) % 2 * 2 + row // 2

    def ctx_of(h, row):
        return (h * 4 + row) * 2 + core

    def weight_first(stage, source):
        mine = place_of(0, y)
        target = w.at[stage, mine, core]
        arrival = wrecv.at[stage, mine, core]
        home = pltpu.make_async_copy(source, target, arrival)
        along = [
            remote(source, target, wsnd.at[stage, 0], arrival, ctx_of(xh, ups[0]), t),
            remote(source, target, wsnd.at[stage, 1], arrival, ctx_of(xh, ups[1]), t),
            remote(source, target, wsnd.at[stage, 2], arrival, ctx_of(1 - xh, y), t),
        ]
        across = [
            remote(source, target, wsnd.at[stage, 0], arrival, c, xn),
            remote(source, target, wsnd.at[stage, 1], arrival, ctx_of(1 - xh, y), xn),
        ]
        return home, along, across

    def weight_start(stage, source):
        home, along, across = weight_first(stage, source)

        @pl.when(holder)
        def _():
            home.start()
            for copy in along:
                copy.start()

        @pl.when(relay)
        def _():
            for copy in across:
                copy.start()

    def weight_pass(stage, index, sem, ctx):
        block = w.at[stage, index, core]
        return remote(block, block, sem, wrecv.at[stage, index, core], ctx, t)

    def weight_got(stage, index):
        arrived(w.at[stage, index, core], wrecv.at[stage, index, core])

    def weight_moves(stage, k):
        here, up, down, far = place_of(k, y), place_of(k, ups[0]), place_of(k, ups[1]), place_of(k, (y + 2) % 4)

        def sibling(index, n):
            return weight_pass(stage, index, bsnd.at[stage, n], sib)

        held = [sibling(here, k)]
        if k:
            held += [weight_pass(stage, here, fsnd.at[stage, n, k], ctx_of(xh, ups[n])) for n in range(2)]
        late = [sibling(far, 4 + k)]
        below = [sibling(down, k)]
        above = [sibling(up, 4 + k)]
        if k % 2 == 0:
            below.append(weight_pass(stage, down, fsnd.at[stage, 0, k], ctx_of(xh, ups[0])))
        else:
            above.append(weight_pass(stage, up, fsnd.at[stage, 0, k], ctx_of(xh, ups[1])))
        return (here, held), (far, late), (down, below), (up, above)

    def weight_hold(stage, *ks):
        @pl.when(holder)
        def _():
            for k in ks:
                first_ = weight_moves(stage, k)[0]
                weight_got(stage, first_[0])
                for copy in reversed(first_[1]):
                    copy.start()

    def weight_relay(stage, k):
        _, _, below, above = weight_moves(stage, k)

        @pl.when(relay)
        def _():
            for index, copies in (below, above):
                weight_got(stage, index)
                for copy in reversed(copies):
                    copy.start()

    def weight_late(stage, *ks):
        @pl.when(holder)
        def _():
            for k in ks:
                _, (index, copies), _, _ = weight_moves(stage, k)
                weight_got(stage, index)
                copies[0].start()

    def weight_sibling(stage, index):
        arrived(w.at[stage, index, 1 - core], wrecv.at[stage, index, 1 - core])

    def weight_drain(stage, source):
        _, along, across = weight_first(stage, source)

        @pl.when(holder)
        def _():
            for copy in along:
                copy.wait_send()
            for k in range(4):
                first_, late, _, _ = weight_moves(stage, k)
                for copy in first_[1] + late[1]:
                    copy.wait_send()

        @pl.when(relay)
        def _():
            for copy in across:
                copy.wait_send()
            for k in range(4):
                _, _, below, above = weight_moves(stage, k)
                for copy in below[1] + above[1]:
                    copy.wait_send()

    weight_start(0, wo1_h)
    load_win = pltpu.make_async_copy(win_h, win, loc.at[2])

    seg = lax.broadcasted_iota(jnp.int32, (SEGS, WIDTH), 0)
    seg1 = lax.broadcasted_iota(jnp.int32, (SEGS, LANES), 0)
    first = seg % 4 == 0
    live = jnp.where(c > 0, 1.0, 0.0).astype(F32)

    def rows(j, count=1):
        start = j * SEGS
        return pl.ds(start if isinstance(start, int) else pl.multiple_of(start, SEGS), count * SEGS)

    def lanes(lt):
        return pl.ds(pl.multiple_of(lt * LANES, LANES), LANES)

    @pl.loop(0, TAPS // 8)
    def _(i):
        taps = filt[pl.ds(pl.multiple_of(i * 8, 8), 8), :].astype(F32)
        for k in range(8):
            fb[rows(i * 8 + k), :] = jnp.broadcast_to(taps[k : k + 1, :], (SEGS, WIDTH))

    load_qkv.wait()
    for s in range(2):
        for p in range(3):

            @pl.loop(0, 16)
            def _(i, s=s, p=p):
                here = pl.ds(pl.multiple_of(i * 16, 16), 16)
                there = pl.ds(pl.multiple_of(s * 256 + i * 16, 16), 16)
                values = qkv_v[s, p, here, :].astype(F32)
                for k in range(WIDTH // LANES):
                    x32[p, k, there, :] = values[:, LANES * k : LANES * (k + 1)]

    def tap(ref, lag, p):
        return jnp.broadcast_to(ref[lag, p : p + 1, :], (SEGS, WIDTH))

    def strided3(p, j):
        return jnp.concatenate(
            [x32[p, k, pl.ds(j, SEGS, stride=STEPS), :] for k in range(WIDTH // LANES)], axis=1
        )

    def medium(j, now, before, before2):
        mixed = [tap(sw1, 0, p) * now[p] + tap(sw1, 1, p) * before[p] + tap(sw1, 2, p) * before2[p] for p in range(3)]
        q32[rows(j), :] = mixed[0]
        uext[rows(j + 128), :] = (mixed[1] * mixed[2]).astype(BF16).astype(F32)

    last = [strided3(p, 63) for p in range(3)]
    last2 = [strided3(p, 62) for p in range(3)]
    x0 = [strided3(p, 0) for p in range(3)]
    x1 = [strided3(p, 1) for p in range(3)]
    own1 = [jnp.where(first, 0.0, pltpu.roll(v, 1, 0)) for v in last]
    own2 = [jnp.where(first, 0.0, pltpu.roll(v, 1, 0)) for v in last2]
    medium(0, x0, own1, own2)
    medium(1, x1, x0, own1)

    def medium_step(j, carried):
        now = [strided3(p, j) for p in range(3)]
        before, before2 = carried
        medium(j, now, before, before2)
        return now, before

    lax.fori_loop(2, STEPS, medium_step, (x1, x0))

    @pl.loop(0, STEPS // 4)
    def _(i):
        packed = []
        for k in range(2):
            even = uext[rows(128 + 4 * i + 2 * k), :]
            odd = uext[rows(129 + 4 * i + 2 * k), :]
            packed.append(jnp.where(seg % 4 >= 2, even, pltpu.roll(odd, 6, 0)))
        pk_s[pl.ds(pl.multiple_of(i * 16, 16), 16), :] = jnp.concatenate(packed, axis=0).astype(BF16)

    u_copy = remote(pk_s, pk_r, hs.at[1], hr.at[1], (c + 1) % 16, t)
    u_copy.start()
    weight_hold(0, 0)
    weight_relay(0, 0)

    arrived(xtail, hr.at[0])

    def halo(p, row):
        top = xtail[0, p].astype(F32)[row : row + 1, :] * live
        bottom = xtail[1, p].astype(F32)[row : row + 1, :] * live
        return jnp.where(seg < 4, jnp.broadcast_to(top, (SEGS, WIDTH)), jnp.broadcast_to(bottom, (SEGS, WIDTH)))

    full1 = [jnp.where(first, halo(p, 7), own1[p]) for p in range(3)]
    full2 = [jnp.where(first, halo(p, 6), own2[p]) for p in range(3)]
    medium(0, x0, full1, full2)
    medium(1, x1, x0, full1)

    load_win.start()
    arrived(pk_r, hr.at[1])

    @pl.loop(0, STEPS // 2)
    def _(i):
        both = pk_r[pl.ds(pl.multiple_of((i // 2) * 16, 16), 16), :].astype(F32) * live
        got = jnp.where(i % 2 == 0, both[:SEGS], both[SEGS:])
        even = uext[rows(128 + 2 * i), :]
        odd = uext[rows(129 + 2 * i), :]
        uext[rows(64 + 2 * i), :] = jnp.where(first, pltpu.roll(got, 5, 0), pltpu.roll(even, 1, 0))
        uext[rows(65 + 2 * i), :] = jnp.where(first, pltpu.roll(got, 7, 0), pltpu.roll(odd, 1, 0))
        uext[rows(2 * i), :] = jnp.where(seg % 4 < 2, pltpu.roll(got, 6, 0), pltpu.roll(even, 2, 0))
        uext[rows(1 + 2 * i), :] = jnp.where(seg % 4 < 2, got, pltpu.roll(odd, 2, 0))

    weight_hold(0, 1, 2)

    HALF = ROWS // 2

    def z_copy(stage, part):
        return remote(zo.at[stage, part], zn.at[stage, part], zs.at[stage, part], zr.at[stage, part], c, xn)

    def p_copy(stage, part, i):
        return remote(
            ps.at[stage, part, i],
            pr.at[stage, part, i],
            pss.at[stage, part, i],
            prs.at[stage, part, i],
            c,
            ztp(1 + 2 * (i % 2), xl),
        )

    def term(stage, part, d, half):
        dest = (z + d) % 4
        both = jnp.concatenate([zo[stage, part], zn[stage, part]], axis=1)
        weights = jnp.concatenate([w[stage, xl * 4 + dest, half], w[stage, (1 - xl) * 4 + dest, half]], axis=0)
        return jnp.dot(both, weights, preferred_element_type=F32)

    early = ((0, 2, 0), (1, 2, 1), (3 - odd, 3 - 2 * odd, odd))
    later = ((2 + odd, 1 + 2 * odd, 1 - odd),)
    passed = ((5 - odd, 3 - 2 * odd, 1 - odd), (4 + odd, 1 + 2 * odd, odd))

    def project_direct(stage, part, pieces):
        for i, d, half in pieces:
            ps[stage, part, i] = term(stage, part, d, half).astype(BF16)
            p_copy(stage, part, i).start()

    def project_relay(stage, part, pieces):
        for i, d, half in pieces:
            mine = term(stage, part, d, half)
            arrived(pr.at[stage, part, i - 4], prs.at[stage, part, i - 4])
            ps[stage, part, i] = (mine + pr[stage, part, i - 4].astype(F32)).astype(BF16)
            p_copy(stage, part, i).start()

    def project_own(stage, part):
        for own in range(2):
            pacc[HALF * part : HALF * (part + 1), 256 * own : 256 * (own + 1)] = term(stage, part, 0, own)

    def project_early(stage):
        for d in (2, 3 - 2 * odd):
            for source in range(2):
                weight_sibling(stage, source * 4 + (z + d) % 4)
        for part in range(2):
            arrived(zn.at[stage, part], zr.at[stage, part])
            project_direct(stage, part, early)

    def project_rest(stage):
        for d in (1 + 2 * odd, 0):
            for source in range(2):
                weight_sibling(stage, source * 4 + (z + d) % 4)
        project_direct(stage, 0, later)
        project_direct(stage, 1, later)
        project_relay(stage, 0, passed)
        project_own(stage, 0)
        project_relay(stage, 1, passed)
        project_own(stage, 1)

    def project_wait(stage, part):
        for i in (2, 3, 4, 5):
            arrived(pr.at[stage, part, i], prs.at[stage, part, i])

    def project_drain(stage):
        for part in range(2):
            z_copy(stage, part).wait_send()
            for i in range(6):
                p_copy(stage, part, i).wait_send()

    def arrivals(stage, part, i):
        here = pl.ds(pl.multiple_of(i * 16, 16), 16)
        left = pr[stage, part, 3, here, :].astype(F32) + pr[stage, part, 4, here, :].astype(F32)
        right = pr[stage, part, 2, here, :].astype(F32) + pr[stage, part, 5, here, :].astype(F32)
        own = pacc[pl.ds(pl.multiple_of(part * HALF + i * 16, 16), 16), :]
        return own + jnp.concatenate([left, right], axis=1)

    def filter_blocks(first_block):
        @pl.loop(first_block, first_block + 4)
        def _(block):
            lane = lanes((block % 8) // 2)
            part = block // 8
            r0 = (block % 2) * 16
            j0 = part * 32 + r0

            def taps8(ib, totals):
                base = 128 + j0 - 8 * ib - 7
                window = uext[pl.ds(pl.multiple_of(base * SEGS, SEGS), 23 * SEGS), lane]
                weights = fb[pl.ds(pl.multiple_of(ib * 64, 64), 64), lane]
                totals = list(totals)
                for b in range(8):
                    f = weights[b * SEGS : (b + 1) * SEGS]
                    for a in range(16):
                        k = a + 7 - b
                        totals[a] = totals[a] + f * window[k * SEGS : (k + 1) * SEGS]
                return tuple(totals)

            totals = lax.fori_loop(0, 16, taps8, tuple(jnp.zeros((SEGS, LANES), F32) for _ in range(16)))
            skip = jnp.broadcast_to(skip1[:, lane], (SEGS, LANES))
            for a in range(0, 16, 2):
                pair = []
                for k in (a, a + 1):
                    u = uext[rows(128 + j0 + k), lane]
                    pair.append(q32[rows(j0 + k), lane] * (totals[k] + skip * u))
                zo[0, part, pl.ds(pl.multiple_of((r0 + a) * SEGS, 16), 16), lane] = jnp.concatenate(
                    pair, axis=0
                ).astype(BF16)

    filter_blocks(0)
    weight_hold(0, 3)
    weight_relay(0, 1)
    filter_blocks(4)
    z_copy(0, 0).start()
    weight_late(0, 0)
    filter_blocks(8)
    weight_relay(0, 2)
    weight_late(0, 1)
    filter_blocks(12)
    z_copy(0, 1).start()

    load_res.wait()

    @pl.loop(0, 32)
    def _(i):
        s = i // 16
        r = (i % 16) * 16
        values = resv[s, pl.ds(pl.multiple_of(r, 16), 16), :].astype(F32)
        for k in range(WIDTH // LANES):
            x32[0, k, pl.ds(pl.multiple_of(i * 16, 16), 16), :] = values[:, LANES * k : LANES * (k + 1)]

    @pl.loop(0, STEPS)
    def _(j):
        for k in range(WIDTH // LANES):
            x32[1, k, rows(j), :] = x32[0, k, pl.ds(j, SEGS, stride=STEPS), :]

    weight_late(0, 2)
    project_early(0)
    weight_relay(0, 3)
    weight_late(0, 3)
    weight_start(1, wo2_h)
    project_rest(0)
    weight_hold(1, 0, 1, 2)
    weight_relay(1, 0)

    sent = []

    def send(slot, quarter, tp):
        k = len(sent)
        copy = remote(
            mid.at[slot, quarter], mid.at[slot, quarter], ags.at[k], agr.at[slot, quarter], c, tp
        )
        copy.start()
        sent.append(copy)

    zp, zm, zz = ztp(1, xl), ztp(3, xl), ztp(2, xl)
    xp, xm, xz = ztp(1, 1 - xl), ztp(3, 1 - xl), ztp(2, 1 - xl)
    for part in range(2):
        project_wait(0, part)

        @pl.loop(0, 16)
        def _(i, part=part):
            here = pl.ds(pl.multiple_of(part * HALF + i * 16, 16), 16)
            before = jnp.concatenate([x32[1, k, here, :] for k in range(WIDTH // LANES)], axis=1)
            value = (before + arrivals(0, part, i)).astype(BF16)
            mid[t, part * 2 + i // 8, pl.ds(pl.multiple_of((i % 8) * 16, 16), 16), :] = value

        for quarter in (2 * part, 2 * part + 1):
            send(t, quarter, xn)
            send(t, quarter, zp)
            send(t, quarter, zm)

    def have(slot, *quarters):
        for quarter in quarters:
            arrived(mid.at[slot, quarter], agr.at[slot, quarter])

    load_win.wait()

    def absorb(*slots, fresh=False):
        count = len(slots)
        scales = [gain[:, pl.ds(pl.multiple_of(slot * WIDTH, WIDTH), WIDTH)] for slot in slots]

        @pl.loop(0, 16)
        def _(i):
            here = pl.ds(pl.multiple_of((i % 4) * 32, 32), 32)
            there = pl.ds(pl.multiple_of(i * 32, 32), 32)
            total = 0.0 if fresh else ssq[there, :]
            for k, slot in enumerate(slots):
                values = mid[slot, i // 4, here, :].astype(F32)
                square = values * values
                total += square[:, 0:128] + square[:, 128:256] + square[:, 256:384] + square[:, 384:512]
                scaled[there, WIDTH * k : WIDTH * (k + 1)] = (values * scales[k]).astype(BF16)
            ssq[there, :] = total

        @pl.loop(0, 6)
        def _(i):
            cols = pl.ds(pl.multiple_of((i % 2) * 256, 256), 256)
            weights = [win[i // 2, pl.ds(pl.multiple_of(slot * WIDTH, WIDTH), WIDTH), cols] for slot in slots]
            product = jnp.dot(
                scaled[:, 0 : WIDTH * count], jnp.concatenate(weights, axis=0), preferred_element_type=F32
            )
            acc[i // 2, :, cols] = product if fresh else acc[i // 2, :, cols] + product

    absorb(t, fresh=True)
    weight_hold(1, 3)
    weight_relay(1, 1)
    have(xn, 0, 1)
    for quarter in range(2):
        send(xn, quarter, zp)
        send(xn, quarter, zm)
    have(zm, 0, 1, 2, 3)
    send(zm, 0, zp)
    send(zm, 2, zp)
    send(zm, 2, xn)
    send(zm, 3, xn)
    have(zp, 0, 1, 2, 3)
    send(zp, 1, zm)
    send(zp, 3, zm)
    send(zp, 2, xn)
    send(zp, 3, xn)
    absorb(zm, zp)
    weight_relay(1, 2)
    have(xm, 0, 1)
    send(xm, 0, zp)
    have(xp, 0, 1)
    send(xp, 1, zm)
    have(zz, 0, 1, 2, 3)
    send(zz, 2, xn)
    send(zz, 3, xn)
    have(xn, 2, 3)
    absorb(xn, zz)
    weight_relay(1, 3)
    have(xm, 2, 3)
    have(xp, 2, 3)
    absorb(xm, xp)
    have(xz, 0, 1, 2, 3)
    absorb(xz)
    weight_late(1, 0, 1, 2, 3)

    def finish(i):
        here = pl.ds(i * 16 if isinstance(i, int) else pl.multiple_of(i * 16, 16), 16)
        meansq = jnp.sum(ssq[here, :], axis=1, keepdims=True) * (1.0 / 4096.0)
        factor = lax.rsqrt(meansq + 1e-6)
        values = [(acc[p, here, :] * factor).astype(BF16) for p in range(3)]
        for p in range(3):
            acc[p, here, :] = values[p].astype(F32)
        return values

    tails = finish(31)
    for p in range(3):
        ltail_s[p] = tails[p]
    l_copy = remote(ltail_s, ltail, hs.at[2], hr.at[2], (c + 1) % 16, t)
    l_copy.start()

    @pl.loop(0, 31)
    def _(i):
        finish(i)

    def longer(j, now, before, before2):
        mixed = [tap(sw2, 0, p) * now[p] + tap(sw2, 1, p) * before[p] + tap(sw2, 2, p) * before2[p] for p in range(3)]
        q32[rows(j), :] = mixed[0]
        uext[rows(j), :] = mixed[1] * mixed[2]

    @pl.loop(2, STEPS)
    def _(j):
        longer(
            j,
            [acc[p, rows(j), :] for p in range(3)],
            [acc[p, rows(j - 1), :] for p in range(3)],
            [acc[p, rows(j - 2), :] for p in range(3)],
        )

    arrived(ltail, hr.at[2])
    edge1, edge2 = [], []
    for p in range(3):
        got = ltail[p].astype(F32) * live
        edge2.append(jnp.where(first, pltpu.roll(got[:SEGS], 5, 0), pltpu.roll(acc[p, rows(62), :], 1, 0)))
        edge1.append(jnp.where(first, pltpu.roll(got[SEGS:], 5, 0), pltpu.roll(acc[p, rows(63), :], 1, 0)))
    y0 = [acc[p, rows(0), :] for p in range(3)]
    y1 = [acc[p, rows(1), :] for p in range(3)]
    longer(0, y0, edge1, edge2)
    longer(1, y1, y0, edge1)

    def row_of(ref, n, lane):
        return jnp.broadcast_to(ref[n : n + 1, lane], (SEGS, LANES))

    @pl.loop(0, WIDTH // LANES)
    def _(lt):
        lane = lanes(lt)
        decay = [jnp.exp(-row_of(rate, n, lane)) for n in range(POLES)]

        def step(j, states):
            u = uext[rows(j), lane]
            return tuple(decay[n] * states[n] + u for n in range(POLES))

        states = lax.fori_loop(0, STEPS, step, tuple(jnp.zeros((SEGS, LANES), F32) for _ in range(POLES)))
        for n in range(POLES):
            est[rows(n), lane] = states[n]

    place = seg1 % 4

    @pl.loop(0, WIDTH // LANES)
    def _(lt):
        lane = lanes(lt)
        for g in range(2):
            packed = []
            for h in range(2):
                total = jnp.zeros((SEGS, LANES), F32)
                for r in range(4):
                    n = g * 8 + h * 4 + r
                    span = jnp.exp(-float(STEPS) * row_of(rate, n, lane))
                    value = est[rows(n), lane]
                    value = value + span * jnp.where(place >= 1, pltpu.roll(value, 1, 0), 0.0)
                    value = value + span * span * jnp.where(place >= 2, pltpu.roll(value, 2, 0), 0.0)
                    est[rows(n), lane] = jnp.where(place >= 1, pltpu.roll(value, 1, 0), 0.0)
                    end = value if r == 3 else pltpu.roll(value, (r - 3) % 8, 0)
                    total = jnp.where(place == r, end, total)
                packed.append(total)
            st_s[pl.ds(g * 16, 16), lane] = jnp.concatenate(packed, axis=0).astype(BF16)

    def state_copy(d):
        return remote(st_s, st_r.at[d - 1], sts.at[d - 1], strv.at[d - 1], c + d, t)

    for d in range(15, 0, -1):

        @pl.when(c + d < 16)
        def _(d=d):
            state_copy(d).start()

    packs = []
    for g in range(4):
        total = jnp.zeros((SEGS, WIDTH), F32)
        for r in range(4):
            n = g * 4 + r
            total = jnp.where(seg % 4 == r, jnp.broadcast_to(rate[n : n + 1, :], (SEGS, WIDTH)), total)
        packs.append(total)
    pack = jnp.concatenate(packs, axis=0)
    hin[...] = jnp.zeros((4 * SEGS, WIDTH), F32)
    for d in range(1, 16):

        @pl.when(c - d >= 0)
        def _(d=d):
            arrived(st_r.at[d - 1], strv.at[d - 1])
            hin[...] += jnp.exp(pack * (-256.0 * (d - 1))) * st_r[d - 1].astype(F32)

    for part in range(2):

        @pl.loop(0, WIDTH // LANES)
        def _(lt, part=part):
            lane = lanes(lt)
            decay, weight, states = [], [], []
            for n in range(POLES):
                r = row_of(rate, n, lane)
                decay.append(jnp.exp(-r))
                weight.append(row_of(resid, n, lane) * jnp.sqrt(1.0 - jnp.exp(-2.0 * r)))
                state = est[rows(n), lane]
                if part == 0:
                    k = (n // 4) * SEGS + n % 4
                    enter = jnp.where(
                        seg1 < 4,
                        jnp.broadcast_to(hin[k : k + 1, lane], (SEGS, LANES)),
                        jnp.broadcast_to(hin[k + 4 : k + 5, lane], (SEGS, LANES)),
                    )
                    state = state + jnp.exp(r * (place.astype(F32) * (-float(STEPS)))) * enter
                states.append(state)
            skip = jnp.broadcast_to(skip2[:, lane], (SEGS, LANES))

            def step(i, states):
                pair = []
                for k in range(2):
                    j = part * (STEPS // 2) + 2 * i + k
                    u = uext[rows(j), lane]
                    states = [decay[n] * states[n] + u for n in range(POLES)]
                    terms = [weight[n] * states[n] for n in range(POLES)]
                    while len(terms) > 1:
                        terms = [terms[a] + terms[a + 1] for a in range(0, len(terms), 2)]
                    pair.append(q32[rows(j), lane] * (terms[0] + skip * u))
                zo[1, part, pl.ds(pl.multiple_of(i * 16, 16), 16), lane] = jnp.concatenate(pair, axis=0).astype(BF16)
                return tuple(states)

            states = lax.fori_loop(0, STEPS // 4, step, tuple(states))
            if part == 0:
                for n in range(POLES):
                    est[rows(n), lane] = states[n]

        z_copy(1, part).start()

    project_early(1)
    project_rest(1)
    for part in range(2):
        project_wait(1, part)

        @pl.loop(0, 16)
        def _(i, part=part):
            base = mid[t, part * 2 + i // 8, pl.ds(pl.multiple_of((i % 8) * 16, 16), 16), :].astype(F32)
            value = base + arrivals(1, part, i)
            j = part * (STEPS // 2) + 2 * i
            for k in range(WIDTH // LANES):
                piece = value[:, LANES * k : LANES * (k + 1)]
                x32[2, k, pl.ds(j, SEGS, stride=STEPS), :] = piece[:SEGS]
                x32[2, k, pl.ds(j + 1, SEGS, stride=STEPS), :] = piece[SEGS:]

    @pl.loop(0, 32)
    def _(i):
        s = i // 16
        r = (i % 16) * 16
        here = pl.ds(pl.multiple_of(i * 16, 16), 16)
        value = jnp.concatenate([x32[2, k, here, :] for k in range(WIDTH // LANES)], axis=1)
        obf[s, pl.ds(pl.multiple_of(r, 16), 16), :] = value.astype(BF16)

    store = pltpu.make_async_copy(obf, out_h, loc.at[3])
    store.start()

    tail_copy.wait_send()
    u_copy.wait_send()
    l_copy.wait_send()
    weight_drain(0, wo1_h)
    weight_drain(1, wo2_h)
    project_drain(0)
    project_drain(1)
    for copy in sent:
        copy.wait_send()
    for d in range(1, 16):

        @pl.when(c + d < 16)
        def _(d=d):
            state_copy(d).wait_send()

    store.wait()


def local(
    residual_in, mr_qkv, mr_short_w, mr_filter, mr_skip, mr_out_w, lr_gain,
    lr_in_w, lr_short_w, lr_rate, lr_res, lr_skip, lr_out_w,
):
    vmem = pl.BlockSpec(memory_space=pltpu.VMEM)
    hbm = pl.BlockSpec(memory_space=pl.ANY)
    dma = pltpu.SemaphoreType.DMA
    scratch = [
        pltpu.VMEM((2, 3, 256, WIDTH), BF16),
        pltpu.VMEM((2, 3, 8, WIDTH), BF16),
        pltpu.VMEM((3, WIDTH // LANES, ROWS, LANES), F32),
        pltpu.VMEM((ROWS, WIDTH), F32),
        pltpu.VMEM((192 * SEGS, WIDTH), F32),
        pltpu.VMEM((TAPS * SEGS, WIDTH), F32),
        pltpu.VMEM((256, WIDTH), BF16),
        pltpu.VMEM((256, WIDTH), BF16),
        pltpu.VMEM((2, 2, ROWS // 2, WIDTH), BF16),
        pltpu.VMEM((2, 2, ROWS // 2, WIDTH), BF16),
        pltpu.VMEM((2, 8, 2, WIDTH, 256), BF16),
        pltpu.VMEM((3, 4096, WIDTH), BF16),
        pltpu.VMEM((2, 2, 6, ROWS // 2, 256), BF16),
        pltpu.VMEM((2, 2, 6, ROWS // 2, 256), BF16),
        pltpu.VMEM((ROWS, WIDTH), F32),
        pltpu.VMEM((8, 4, 128, WIDTH), BF16),
        pltpu.VMEM((ROWS, 2 * WIDTH), BF16),
        pltpu.VMEM((3, ROWS, WIDTH), F32),
        pltpu.VMEM((ROWS, LANES), F32),
        pltpu.VMEM((3, 16, WIDTH), BF16),
        pltpu.VMEM((3, 16, WIDTH), BF16),
        pltpu.VMEM((POLES * SEGS, WIDTH), F32),
        pltpu.VMEM((4 * SEGS, WIDTH), BF16),
        pltpu.VMEM((15, 4 * SEGS, WIDTH), BF16),
        pltpu.VMEM((4 * SEGS, WIDTH), F32),
        pltpu.VMEM((2, 256, WIDTH), BF16),
        pltpu.VMEM((2, 256, WIDTH), BF16),
        dma((4,)),
        dma((3,)),
        dma((3,)),
        dma((2, 3)),
        dma((2, 2, 4)),
        dma((2, 8)),
        dma((2, 8, 2)),
        dma((2, 2)),
        dma((2, 2)),
        dma((2, 2, 6)),
        dma((2, 2, 6)),
        dma((32,)),
        dma((8, 4)),
        dma((15,)),
        dma((15,)),
    ]
    return pl.pallas_call(
        kernel,
        out_shape=jax.ShapeDtypeStruct((2, 256, WIDTH), BF16),
        in_specs=[hbm, hbm, vmem, vmem, vmem, hbm, vmem, hbm, vmem, vmem, vmem, vmem, hbm],
        out_specs=hbm,
        scratch_shapes=scratch,
        compiler_params=pltpu.CompilerParams(
            collective_id=0, has_side_effects=True, vmem_limit_bytes=62 * 1024 * 1024
        ),
    )(
        residual_in,
        jnp.transpose(mr_qkv, (0, 2, 1, 3)),
        mr_short_w,
        mr_filter,
        mr_skip.reshape(1, WIDTH),
        mr_out_w,
        lr_gain.reshape(1, 8 * WIDTH),
        jnp.transpose(lr_in_w, (1, 0, 2)),
        lr_short_w,
        lr_rate,
        lr_res,
        lr_skip.reshape(1, WIDTH),
        lr_out_w,
    )


def solution(mesh):
    in_specs = (
        P(None, "ctx", "tp"),
        P(None, "ctx", None, "tp"),
        P(None, None, "tp"),
        P(None, "tp"),
        P("tp"),
        P("tp", "ctx"),
        P(),
        P(None, None, "tp"),
        P(None, None, "tp"),
        P(None, "tp"),
        P(None, "tp"),
        P("tp"),
        P("tp", "ctx"),
    )
    return jax.shard_map(local, mesh=mesh, in_specs=in_specs, out_specs=P(None, "ctx", "tp"), check_vma=False)
```

```python
import jax
import jax.numpy as jnp
from jax import lax
from jax.experimental import pallas as pl
from jax.experimental.pallas import tpu as pltpu
from jax.sharding import PartitionSpec as P

MESH = pl.DeviceIdType.MESH
F32 = jnp.float32
BF16 = jnp.bfloat16

SEGS = 8
STEPS = 64
ROWS = SEGS * STEPS
WIDTH = 512
TAPS = 128
POLES = 16
LANES = 128


def kernel(
    res_h, qkv_h, sw1, filt, skip1, wo1_h, gain, win_h, sw2, rate, resid, skip2, wo2_h,
    out_h,
    qkv_v, xtail, x32, q32, uext, fb, pk_s, pk_r, zo, zn, w, win, ps, pr, pacc, mid, scaled, acc, ssq,
    ltail_s, ltail, est, decays, weights, st_s, st_r, hin, obf, resv,
    loc, hs, hr, wsnd, fsnd, bsnd, wrecv, zs, zr, pss, prs, ags, agr, sts, strv,
):
    c = lax.axis_index("ctx")
    t = lax.axis_index("tp")
    core = c % 2
    m = c // 2
    y = m % 4
    xh = m // 4
    z = t // 2
    xl = t % 2
    sib = c + 1 - 2 * core
    xn = t + 1 - 2 * xl

    def ztp(dz, x):
        return ((z + dz) % 4) * 2 + x

    def remote(src, dst, ssem, rsem, ctx, tp):
        return pltpu.make_async_remote_copy(
            src_ref=src,
            dst_ref=dst,
            send_sem=ssem,
            recv_sem=rsem,
            device_id={"ctx": ctx, "tp": tp},
            device_id_type=MESH,
        )

    def arrived(ref, sem):
        pltpu.make_async_copy(ref, ref, sem).wait()

    load_qkv = pltpu.make_async_copy(qkv_h, qkv_v, loc.at[0])
    load_qkv.start()
    load_res = pltpu.make_async_copy(res_h, resv, loc.at[1])
    load_res.start()

    barrier = pltpu.get_barrier_semaphore()

    def greet(ctx, tp):
        pl.semaphore_signal(barrier, inc=1, device_id={"ctx": ctx, "tp": tp}, device_id_type=MESH)

    for d in range(1, 16):
        greet((c + d) % 16, t)
    greet(c, xn)
    greet((c + 8) % 16, xn)
    greet(c, ztp(1, xl))
    greet(c, ztp(3, xl))
    pl.semaphore_wait(barrier, 19)

    tail_copy = remote(qkv_h.at[:, :, 248:256, :], xtail, hs.at[0], hr.at[0], (c + 1) % 16, t)
    tail_copy.start()

    holder = (y + xl) % 2 == 0
    relay = (y + xl) % 2 == 1
    ups = ((y + 1) % 4, (y + 3) % 4)

    def place_of(k, row):
        xs = (xl, 1 - xl, 1 - xl, xl)[k]
        xhs = (xh, xh, 1 - xh, 1 - xh)[k]
        return xs * 4 + xhs * 2 + row // 2

    def ctx_of(h, row):
        return (h * 4 + row) * 2 + core

    def weight_first(stage, source):
        mine = place_of(0, y)
        target = w.at[stage, mine, core]
        arrival = wrecv.at[stage, mine, core]
        home = pltpu.make_async_copy(source, target, arrival)
        along = [
            remote(source, target, wsnd.at[stage, 0], arrival, ctx_of(xh, ups[0]), t),
            remote(source, target, wsnd.at[stage, 1], arrival, ctx_of(xh, ups[1]), t),
            remote(source, target, wsnd.at[stage, 2], arrival, ctx_of(1 - xh, y), t),
        ]
        across = [
            remote(source, target, wsnd.at[stage, 0], arrival, c, xn),
            remote(source, target, wsnd.at[stage, 1], arrival, ctx_of(1 - xh, y), xn),
        ]
        return home, along, across

    def weight_start(stage, source):
        home, along, across = weight_first(stage, source)

        @pl.when(holder)
        def _():
            home.start()
            for copy in along:
                copy.start()

        @pl.when(relay)
        def _():
            for copy in across:
                copy.start()

    def weight_pass(stage, index, sem, ctx):
        block = w.at[stage, index, core]
        return remote(block, block, sem, wrecv.at[stage, index, core], ctx, t)

    def weight_pass_half(stage, index, half, sem, ctx):
        block = w.at[stage, index, core, 256 * half : 256 * (half + 1), :]
        return remote(block, block, sem, wrecv.at[stage, index, core], ctx, t)

    def weight_got(stage, index):
        arrived(w.at[stage, index, core], wrecv.at[stage, index, core])

    def weight_moves(stage, k):
        here, up, down, far = place_of(k, y), place_of(k, ups[0]), place_of(k, ups[1]), place_of(k, (y + 2) % 4)

        def sibling(index, n):
            return weight_pass(stage, index, bsnd.at[stage, n], sib)

        held = [sibling(here, k)]
        if k:
            held += [weight_pass(stage, here, fsnd.at[stage, n, k], ctx_of(xh, ups[n])) for n in range(2)]
        late = [sibling(far, 4 + k)]
        below = [sibling(down, k), weight_pass_half(stage, down, 0, fsnd.at[stage, 0, k], ctx_of(xh, ups[0]))]
        above = [sibling(up, 4 + k), weight_pass_half(stage, up, 1, fsnd.at[stage, 1, k], ctx_of(xh, ups[1]))]
        return (here, held), (far, late), (down, below), (up, above)

    def weight_hold(stage, *ks):
        @pl.when(holder)
        def _():
            for k in ks:
                first_ = weight_moves(stage, k)[0]
                weight_got(stage, first_[0])
                for copy in reversed(first_[1]):
                    copy.start()

    def weight_relay(stage, k):
        _, _, below, above = weight_moves(stage, k)

        @pl.when(relay)
        def _():
            for index, copies in (below, above):
                weight_got(stage, index)
                for copy in reversed(copies):
                    copy.start()

    def weight_late(stage, *ks):
        @pl.when(holder)
        def _():
            for k in ks:
                _, (index, copies), _, _ = weight_moves(stage, k)
                weight_got(stage, index)
                copies[0].start()

    def weight_sibling(stage, index):
        arrived(w.at[stage, index, 1 - core], wrecv.at[stage, index, 1 - core])

    def weight_drain(stage, source):
        _, along, across = weight_first(stage, source)

        @pl.when(holder)
        def _():
            for copy in along:
                copy.wait_send()
            for k in range(4):
                first_, late, _, _ = weight_moves(stage, k)
                for copy in first_[1] + late[1]:
                    copy.wait_send()

        @pl.when(relay)
        def _():
            for copy in across:
                copy.wait_send()
            for k in range(4):
                _, _, below, above = weight_moves(stage, k)
                for copy in below[1] + above[1]:
                    copy.wait_send()

    weight_start(0, wo1_h)
    load_win = pltpu.make_async_copy(win_h, win, loc.at[2])

    seg = lax.broadcasted_iota(jnp.int32, (SEGS, WIDTH), 0)
    seg1 = lax.broadcasted_iota(jnp.int32, (SEGS, LANES), 0)
    first = seg % 4 == 0
    live = jnp.where(c > 0, 1.0, 0.0).astype(F32)

    def rows(j, count=1):
        start = j * SEGS
        return pl.ds(start if isinstance(start, int) else pl.multiple_of(start, SEGS), count * SEGS)

    def lanes(lt):
        return pl.ds(pl.multiple_of(lt * LANES, LANES), LANES)

    @pl.loop(0, TAPS // 8)
    def _(i):
        taps = filt[pl.ds(pl.multiple_of(i * 8, 8), 8), :].astype(F32)
        for k in range(8):
            fb[rows(i * 8 + k), :] = jnp.broadcast_to(taps[k : k + 1, :], (SEGS, WIDTH))

    load_qkv.wait()
    for s in range(2):
        for p in range(3):

            @pl.loop(0, 16)
            def _(i, s=s, p=p):
                here = pl.ds(pl.multiple_of(i * 16, 16), 16)
                there = pl.ds(pl.multiple_of(s * 256 + i * 16, 16), 16)
                values = qkv_v[s, p, here, :].astype(F32)
                for k in range(WIDTH // LANES):
                    x32[p, k, there, :] = values[:, LANES * k : LANES * (k + 1)]

    def tap(ref, lag, p):
        return jnp.broadcast_to(ref[lag, p : p + 1, :], (SEGS, WIDTH))

    def strided3(p, j):
        return jnp.concatenate(
            [x32[p, k, pl.ds(j, SEGS, stride=STEPS), :] for k in range(WIDTH // LANES)], axis=1
        )

    def medium(j, now, before, before2):
        mixed = [tap(sw1, 0, p) * now[p] + tap(sw1, 1, p) * before[p] + tap(sw1, 2, p) * before2[p] for p in range(3)]
        q32[rows(j), :] = mixed[0]
        uext[rows(j + 128), :] = (mixed[1] * mixed[2]).astype(BF16).astype(F32)

    last = [strided3(p, 63) for p in range(3)]
    last2 = [strided3(p, 62) for p in range(3)]
    x0 = [strided3(p, 0) for p in range(3)]
    x1 = [strided3(p, 1) for p in range(3)]
    own1 = [jnp.where(first, 0.0, pltpu.roll(v, 1, 0)) for v in last]
    own2 = [jnp.where(first, 0.0, pltpu.roll(v, 1, 0)) for v in last2]
    medium(0, x0, own1, own2)
    medium(1, x1, x0, own1)

    def medium_step(j, carried):
        now = [strided3(p, j) for p in range(3)]
        before, before2 = carried
        medium(j, now, before, before2)
        return now, before

    lax.fori_loop(2, STEPS, medium_step, (x1, x0))

    @pl.loop(0, STEPS // 4)
    def _(i):
        packed = []
        for k in range(2):
            even = uext[rows(128 + 4 * i + 2 * k), :]
            odd = uext[rows(129 + 4 * i + 2 * k), :]
            packed.append(jnp.where(seg % 4 >= 2, even, pltpu.roll(odd, 6, 0)))
        pk_s[pl.ds(pl.multiple_of(i * 16, 16), 16), :] = jnp.concatenate(packed, axis=0).astype(BF16)

    u_copy = remote(pk_s, pk_r, hs.at[1], hr.at[1], (c + 1) % 16, t)
    u_copy.start()
    weight_hold(0, 0, 1, 2)
    weight_relay(0, 0)

    arrived(xtail, hr.at[0])

    def halo(p, row):
        top = xtail[0, p].astype(F32)[row : row + 1, :] * live
        bottom = xtail[1, p].astype(F32)[row : row + 1, :] * live
        return jnp.where(seg < 4, jnp.broadcast_to(top, (SEGS, WIDTH)), jnp.broadcast_to(bottom, (SEGS, WIDTH)))

    full1 = [jnp.where(first, halo(p, 7), own1[p]) for p in range(3)]
    full2 = [jnp.where(first, halo(p, 6), own2[p]) for p in range(3)]
    medium(0, x0, full1, full2)
    medium(1, x1, x0, full1)

    load_win.start()
    arrived(pk_r, hr.at[1])

    @pl.loop(0, STEPS // 2)
    def _(i):
        both = pk_r[pl.ds(pl.multiple_of((i // 2) * 16, 16), 16), :].astype(F32) * live
        got = jnp.where(i % 2 == 0, both[:SEGS], both[SEGS:])
        even = uext[rows(128 + 2 * i), :]
        odd = uext[rows(129 + 2 * i), :]
        uext[rows(64 + 2 * i), :] = jnp.where(first, pltpu.roll(got, 5, 0), pltpu.roll(even, 1, 0))
        uext[rows(65 + 2 * i), :] = jnp.where(first, pltpu.roll(got, 7, 0), pltpu.roll(odd, 1, 0))
        uext[rows(2 * i), :] = jnp.where(seg % 4 < 2, pltpu.roll(got, 6, 0), pltpu.roll(even, 2, 0))
        uext[rows(1 + 2 * i), :] = jnp.where(seg % 4 < 2, got, pltpu.roll(odd, 2, 0))


    HALF = ROWS // 2

    def z_copy(stage, part):
        return remote(zo.at[stage, part], zn.at[stage, part], zs.at[stage, part], zr.at[stage, part], c, xn)

    def p_copy(stage, part, i):
        return remote(
            ps.at[stage, part, i],
            pr.at[stage, part, i],
            pss.at[stage, part, i],
            prs.at[stage, part, i],
            c,
            ztp(1 if i % 2 == 0 else 3, xl),
        )

    def term(stage, part, d, half):
        dest = (z + d) % 4
        both = jnp.concatenate([zo[stage, part], zn[stage, part]], axis=1)
        weights = jnp.concatenate([w[stage, xl * 4 + dest, half], w[stage, (1 - xl) * 4 + dest, half]], axis=0)
        return jnp.dot(both, weights, preferred_element_type=F32)

    def project_first(stage, part):
        arrived(zn.at[stage, part], zr.at[stage, part])
        for i, d, half in ((0, 2, 0), (1, 2, 1), (2, 1, 1), (3, 3, 0)):
            if part == 0 and i in (0, 2, 3):
                for source in range(2):
                    weight_sibling(stage, source * 4 + (z + d) % 4)
            ps[stage, part, i] = term(stage, part, d, half).astype(BF16)
            p_copy(stage, part, i).start()

    def project_own(stage, part):
        if part == 0:
            for source in range(2):
                weight_sibling(stage, source * 4 + z)
        for own in range(2):
            pacc[HALF * part : HALF * (part + 1), 256 * own : 256 * (own + 1)] = term(stage, part, 0, own)

    def project_relay(stage, part):
        for i, d, half in ((4, 1, 0), (5, 3, 1)):
            mine = term(stage, part, d, half)
            arrived(pr.at[stage, part, i - 4], prs.at[stage, part, i - 4])
            ps[stage, part, i] = (mine + pr[stage, part, i - 4].astype(F32)).astype(BF16)
            p_copy(stage, part, i).start()

    def project(stage):
        project_first(stage, 0)
        project_first(stage, 1)
        project_relay(stage, 0)
        project_own(stage, 0)
        project_relay(stage, 1)
        project_own(stage, 1)

    def project_wait(stage, part):
        for i in (2, 3, 4, 5):
            arrived(pr.at[stage, part, i], prs.at[stage, part, i])

    def project_drain(stage):
        for part in range(2):
            z_copy(stage, part).wait_send()
            for i in range(6):
                p_copy(stage, part, i).wait_send()

    def arrivals(stage, part, i):
        here = pl.ds(pl.multiple_of(i * 16, 16), 16)
        left = pr[stage, part, 3, here, :].astype(F32) + pr[stage, part, 4, here, :].astype(F32)
        right = pr[stage, part, 2, here, :].astype(F32) + pr[stage, part, 5, here, :].astype(F32)
        own = pacc[pl.ds(pl.multiple_of(part * HALF + i * 16, 16), 16), :]
        return own + jnp.concatenate([left, right], axis=1)

    def filter_blocks(first_block):
        @pl.loop(first_block, first_block + 2)
        def _(block):
            lane = lanes((block % 8) // 2)
            part = block // 8
            r0 = (block % 2) * 16
            j0 = part * 32 + r0

            def taps8(ib, totals):
                base = 128 + j0 - 8 * ib - 7
                window = uext[pl.ds(pl.multiple_of(base * SEGS, SEGS), 23 * SEGS), lane]
                weights = fb[pl.ds(pl.multiple_of(ib * 64, 64), 64), lane]
                totals = list(totals)
                for b in range(8):
                    f = weights[b * SEGS : (b + 1) * SEGS]
                    for a in range(16):
                        k = a + 7 - b
                        totals[a] = totals[a] + f * window[k * SEGS : (k + 1) * SEGS]
                return tuple(totals)

            totals = lax.fori_loop(0, 16, taps8, tuple(jnp.zeros((SEGS, LANES), F32) for _ in range(16)))
            skip = jnp.broadcast_to(skip1[:, lane], (SEGS, LANES))
            for a in range(0, 16, 2):
                pair = []
                for k in (a, a + 1):
                    u = uext[rows(128 + j0 + k), lane]
                    pair.append(q32[rows(j0 + k), lane] * (totals[k] + skip * u))
                zo[0, part, pl.ds(pl.multiple_of((r0 + a) * SEGS, 16), 16), lane] = jnp.concatenate(
                    pair, axis=0
                ).astype(BF16)

    filter_blocks(0)
    filter_blocks(2)
    weight_hold(0, 3)
    weight_relay(0, 1)
    filter_blocks(4)
    filter_blocks(6)
    z_copy(0, 0).start()
    weight_late(0, 0)
    filter_blocks(8)
    weight_relay(0, 2)
    weight_late(0, 1)
    filter_blocks(10)
    filter_blocks(12)
    weight_relay(0, 3)
    weight_late(0, 2)
    filter_blocks(14)
    z_copy(0, 1).start()
    weight_late(0, 3)
    weight_start(1, wo2_h)

    load_res.wait()

    @pl.loop(0, 32)
    def _(i):
        s = i // 16
        r = (i % 16) * 16
        values = resv[s, pl.ds(pl.multiple_of(r, 16), 16), :].astype(F32)
        for k in range(WIDTH // LANES):
            x32[0, k, pl.ds(pl.multiple_of(i * 16, 16), 16), :] = values[:, LANES * k : LANES * (k + 1)]

    @pl.loop(0, STEPS)
    def _(j):
        for k in range(WIDTH // LANES):
            x32[1, k, rows(j), :] = x32[0, k, pl.ds(j, SEGS, stride=STEPS), :]

    project(0)
    weight_hold(1, 0, 1, 2)
    weight_relay(1, 0)

    sent = []

    def send(slot, quarter, tp):
        k = len(sent)
        copy = remote(
            mid.at[slot, quarter], mid.at[slot, quarter], ags.at[k], agr.at[slot, quarter], c, tp
        )
        copy.start()
        sent.append(copy)

    zp, zm, zz = ztp(1, xl), ztp(3, xl), ztp(2, xl)
    xp, xm, xz = ztp(1, 1 - xl), ztp(3, 1 - xl), ztp(2, 1 - xl)
    for part in range(2):
        project_wait(0, part)

        @pl.loop(0, 16)
        def _(i, part=part):
            here = pl.ds(pl.multiple_of(part * HALF + i * 16, 16), 16)
            before = jnp.concatenate([x32[1, k, here, :] for k in range(WIDTH // LANES)], axis=1)
            value = (before + arrivals(0, part, i)).astype(BF16)
            mid[t, part * 2 + i // 8, pl.ds(pl.multiple_of((i % 8) * 16, 16), 16), :] = value

        for quarter in (2 * part, 2 * part + 1):
            send(t, quarter, xn)
            send(t, quarter, zp)
            send(t, quarter, zm)

    def have(slot, *quarters):
        for quarter in quarters:
            arrived(mid.at[slot, quarter], agr.at[slot, quarter])

    load_win.wait()

    def absorb(*slots, fresh=False):
        count = len(slots)
        scales = [gain[:, pl.ds(pl.multiple_of(slot * WIDTH, WIDTH), WIDTH)] for slot in slots]

        @pl.loop(0, 16)
        def _(i):
            here = pl.ds(pl.multiple_of((i % 4) * 32, 32), 32)
            there = pl.ds(pl.multiple_of(i * 32, 32), 32)
            total = 0.0 if fresh else ssq[there, :]
            for k, slot in enumerate(slots):
                values = mid[slot, i // 4, here, :].astype(F32)
                square = values * values
                total += square[:, 0:128] + square[:, 128:256] + square[:, 256:384] + square[:, 384:512]
                scaled[there, WIDTH * k : WIDTH * (k + 1)] = (values * scales[k]).astype(BF16)
            ssq[there, :] = total

        @pl.loop(0, 6)
        def _(i):
            cols = pl.ds(pl.multiple_of((i % 2) * 256, 256), 256)
            weights = [win[i // 2, pl.ds(pl.multiple_of(slot * WIDTH, WIDTH), WIDTH), cols] for slot in slots]
            product = jnp.dot(
                scaled[:, 0 : WIDTH * count], jnp.concatenate(weights, axis=0), preferred_element_type=F32
            )
            acc[i // 2, :, cols] = product if fresh else acc[i // 2, :, cols] + product

    absorb(t, fresh=True)
    weight_hold(1, 3)
    weight_relay(1, 1)
    have(xn, 0, 1)
    for quarter in range(2):
        send(xn, quarter, zp)
        send(xn, quarter, zm)
    have(zm, 0, 1, 2, 3)
    send(zm, 0, zp)
    send(zm, 2, zp)
    send(zm, 2, xn)
    send(zm, 3, xn)
    have(zp, 0, 1, 2, 3)
    send(zp, 1, zm)
    send(zp, 3, zm)
    send(zp, 2, xn)
    send(zp, 3, xn)
    absorb(zm, zp)
    weight_relay(1, 2)
    have(xm, 0, 1)
    send(xm, 0, zp)
    have(xp, 0, 1)
    send(xp, 1, zm)
    have(zz, 0, 1, 2, 3)
    send(zz, 2, xn)
    send(zz, 3, xn)
    have(xn, 2, 3)
    absorb(xn, zz)
    weight_relay(1, 3)
    have(xm, 2, 3)
    have(xp, 2, 3)
    absorb(xm, xp)
    have(xz, 0, 1, 2, 3)
    absorb(xz)
    weight_late(1, 0, 1, 2, 3)

    def finish(i):
        here = pl.ds(i * 16 if isinstance(i, int) else pl.multiple_of(i * 16, 16), 16)
        meansq = jnp.sum(ssq[here, :], axis=1, keepdims=True) * (1.0 / 4096.0)
        factor = lax.rsqrt(meansq + 1e-6)
        values = [(acc[p, here, :] * factor).astype(BF16) for p in range(3)]
        for p in range(3):
            acc[p, here, :] = values[p].astype(F32)
        return values

    tails = finish(31)
    for p in range(3):
        ltail_s[p] = tails[p]
    l_copy = remote(ltail_s, ltail, hs.at[2], hr.at[2], (c + 1) % 16, t)
    l_copy.start()

    @pl.loop(0, 31)
    def _(i):
        finish(i)

    def longer(j, now, before, before2):
        mixed = [tap(sw2, 0, p) * now[p] + tap(sw2, 1, p) * before[p] + tap(sw2, 2, p) * before2[p] for p in range(3)]
        q32[rows(j), :] = mixed[0]
        uext[rows(j), :] = mixed[1] * mixed[2]

    @pl.loop(2, STEPS)
    def _(j):
        longer(
            j,
            [acc[p, rows(j), :] for p in range(3)],
            [acc[p, rows(j - 1), :] for p in range(3)],
            [acc[p, rows(j - 2), :] for p in range(3)],
        )

    arrived(ltail, hr.at[2])
    edge1, edge2 = [], []
    for p in range(3):
        got = ltail[p].astype(F32) * live
        edge2.append(jnp.where(first, pltpu.roll(got[:SEGS], 5, 0), pltpu.roll(acc[p, rows(62), :], 1, 0)))
        edge1.append(jnp.where(first, pltpu.roll(got[SEGS:], 5, 0), pltpu.roll(acc[p, rows(63), :], 1, 0)))
    y0 = [acc[p, rows(0), :] for p in range(3)]
    y1 = [acc[p, rows(1), :] for p in range(3)]
    longer(0, y0, edge1, edge2)
    longer(1, y1, y0, edge1)

    def row_of(ref, n, lane):
        return jnp.broadcast_to(ref[n : n + 1, lane], (SEGS, LANES))

    @pl.loop(0, WIDTH // LANES)
    def _(lt):
        lane = lanes(lt)
        decay = [jnp.exp(-row_of(rate, n, lane)) for n in range(POLES)]

        def step(i, states):
            for k in range(4):
                u = uext[rows(4 * i + k), lane]
                states = [decay[n] * states[n] + u for n in range(POLES)]
            return tuple(states)

        states = lax.fori_loop(0, STEPS // 4, step, tuple(jnp.zeros((SEGS, LANES), F32) for _ in range(POLES)))
        for n in range(POLES):
            est[rows(n), lane] = states[n]
            decays[rows(n), lane] = decay[n]

    place = seg1 % 4

    @pl.loop(0, WIDTH // LANES)
    def _(lt):
        lane = lanes(lt)
        for g in range(2):
            packed = []
            for h in range(2):
                total = jnp.zeros((SEGS, LANES), F32)
                for r in range(4):
                    n = g * 8 + h * 4 + r
                    span = jnp.exp(-float(STEPS) * row_of(rate, n, lane))
                    value = est[rows(n), lane]
                    value = value + span * jnp.where(place >= 1, pltpu.roll(value, 1, 0), 0.0)
                    value = value + span * span * jnp.where(place >= 2, pltpu.roll(value, 2, 0), 0.0)
                    est[rows(n), lane] = jnp.where(place >= 1, pltpu.roll(value, 1, 0), 0.0)
                    end = value if r == 3 else pltpu.roll(value, (r - 3) % 8, 0)
                    total = jnp.where(place == r, end, total)
                packed.append(total)
            st_s[pl.ds(g * 16, 16), lane] = jnp.concatenate(packed, axis=0).astype(BF16)

    def state_copy(d):
        return remote(st_s, st_r.at[d - 1], sts.at[d - 1], strv.at[d - 1], c + d, t)

    for d in range(15, 0, -1):

        @pl.when(c + d < 16)
        def _(d=d):
            state_copy(d).start()

    @pl.loop(0, WIDTH // LANES)
    def _(lt):
        lane = lanes(lt)
        for n in range(POLES):
            weights[rows(n), lane] = row_of(resid, n, lane) * jnp.sqrt(1.0 - jnp.exp(-2.0 * row_of(rate, n, lane)))

    packs = []
    for g in range(4):
        total = jnp.zeros((SEGS, WIDTH), F32)
        for r in range(4):
            n = g * 4 + r
            total = jnp.where(seg % 4 == r, jnp.broadcast_to(rate[n : n + 1, :], (SEGS, WIDTH)), total)
        packs.append(total)
    pack = jnp.concatenate(packs, axis=0)
    hin[...] = jnp.zeros((4 * SEGS, WIDTH), F32)
    for d in range(1, 16):

        @pl.when(c - d >= 0)
        def _(d=d):
            arrived(st_r.at[d - 1], strv.at[d - 1])
            hin[...] += jnp.exp(pack * (-256.0 * (d - 1))) * st_r[d - 1].astype(F32)

    for part in range(2):

        @pl.loop(0, WIDTH // LANES)
        def _(lt, part=part):
            lane = lanes(lt)
            decay, weight, states = [], [], []
            for n in range(POLES):
                decay.append(decays[rows(n), lane])
                weight.append(weights[rows(n), lane])
                state = est[rows(n), lane]
                if part == 0:
                    r = row_of(rate, n, lane)
                    k = (n // 4) * SEGS + n % 4
                    enter = jnp.where(
                        seg1 < 4,
                        jnp.broadcast_to(hin[k : k + 1, lane], (SEGS, LANES)),
                        jnp.broadcast_to(hin[k + 4 : k + 5, lane], (SEGS, LANES)),
                    )
                    state = state + jnp.exp(r * (place.astype(F32) * (-float(STEPS)))) * enter
                states.append(state)
            skip = jnp.broadcast_to(skip2[:, lane], (SEGS, LANES))

            def step(i, states):
                pair = []
                for k in range(2):
                    j = part * (STEPS // 2) + 2 * i + k
                    u = uext[rows(j), lane]
                    states = [decay[n] * states[n] + u for n in range(POLES)]
                    terms = [weight[n] * states[n] for n in range(POLES)]
                    while len(terms) > 1:
                        terms = [terms[a] + terms[a + 1] for a in range(0, len(terms), 2)]
                    pair.append(q32[rows(j), lane] * (terms[0] + skip * u))
                zo[1, part, pl.ds(pl.multiple_of(i * 16, 16), 16), lane] = jnp.concatenate(pair, axis=0).astype(BF16)
                return tuple(states)

            states = lax.fori_loop(0, STEPS // 4, step, tuple(states))
            if part == 0:
                for n in range(POLES):
                    est[rows(n), lane] = states[n]

        z_copy(1, part).start()

    project(1)
    for part in range(2):
        project_wait(1, part)

        @pl.loop(0, 16)
        def _(i, part=part):
            base = mid[t, part * 2 + i // 8, pl.ds(pl.multiple_of((i % 8) * 16, 16), 16), :].astype(F32)
            value = base + arrivals(1, part, i)
            j = part * (STEPS // 2) + 2 * i
            for k in range(WIDTH // LANES):
                piece = value[:, LANES * k : LANES * (k + 1)]
                x32[2, k, pl.ds(j, SEGS, stride=STEPS), :] = piece[:SEGS]
                x32[2, k, pl.ds(j + 1, SEGS, stride=STEPS), :] = piece[SEGS:]

    @pl.loop(0, 32)
    def _(i):
        s = i // 16
        r = (i % 16) * 16
        here = pl.ds(pl.multiple_of(i * 16, 16), 16)
        value = jnp.concatenate([x32[2, k, here, :] for k in range(WIDTH // LANES)], axis=1)
        obf[s, pl.ds(pl.multiple_of(r, 16), 16), :] = value.astype(BF16)

    store = pltpu.make_async_copy(obf, out_h, loc.at[3])
    store.start()

    tail_copy.wait_send()
    u_copy.wait_send()
    l_copy.wait_send()
    weight_drain(0, wo1_h)
    weight_drain(1, wo2_h)
    project_drain(0)
    project_drain(1)
    for copy in sent:
        copy.wait_send()
    for d in range(1, 16):

        @pl.when(c + d < 16)
        def _(d=d):
            state_copy(d).wait_send()

    store.wait()


def local(
    residual_in, mr_qkv, mr_short_w, mr_filter, mr_skip, mr_out_w, lr_gain,
    lr_in_w, lr_short_w, lr_rate, lr_res, lr_skip, lr_out_w,
):
    vmem = pl.BlockSpec(memory_space=pltpu.VMEM)
    hbm = pl.BlockSpec(memory_space=pl.ANY)
    dma = pltpu.SemaphoreType.DMA
    scratch = [
        pltpu.VMEM((2, 3, 256, WIDTH), BF16),
        pltpu.VMEM((2, 3, 8, WIDTH), BF16),
        pltpu.VMEM((3, WIDTH // LANES, ROWS, LANES), F32),
        pltpu.VMEM((ROWS, WIDTH), F32),
        pltpu.VMEM((192 * SEGS, WIDTH), F32),
        pltpu.VMEM((TAPS * SEGS, WIDTH), F32),
        pltpu.VMEM((256, WIDTH), BF16),
        pltpu.VMEM((256, WIDTH), BF16),
        pltpu.VMEM((2, 2, ROWS // 2, WIDTH), BF16),
        pltpu.VMEM((2, 2, ROWS // 2, WIDTH), BF16),
        pltpu.VMEM((2, 8, 2, WIDTH, 256), BF16),
        pltpu.VMEM((3, 4096, WIDTH), BF16),
        pltpu.VMEM((2, 2, 6, ROWS // 2, 256), BF16),
        pltpu.VMEM((2, 2, 6, ROWS // 2, 256), BF16),
        pltpu.VMEM((ROWS, WIDTH), F32),
        pltpu.VMEM((8, 4, 128, WIDTH), BF16),
        pltpu.VMEM((ROWS, 2 * WIDTH), BF16),
        pltpu.VMEM((3, ROWS, WIDTH), F32),
        pltpu.VMEM((ROWS, LANES), F32),
        pltpu.VMEM((3, 16, WIDTH), BF16),
        pltpu.VMEM((3, 16, WIDTH), BF16),
        pltpu.VMEM((POLES * SEGS, WIDTH), F32),
        pltpu.VMEM((POLES * SEGS, WIDTH), F32),
        pltpu.VMEM((POLES * SEGS, WIDTH), F32),
        pltpu.VMEM((4 * SEGS, WIDTH), BF16),
        pltpu.VMEM((15, 4 * SEGS, WIDTH), BF16),
        pltpu.VMEM((4 * SEGS, WIDTH), F32),
        pltpu.VMEM((2, 256, WIDTH), BF16),
        pltpu.VMEM((2, 256, WIDTH), BF16),
        dma((4,)),
        dma((3,)),
        dma((3,)),
        dma((2, 3)),
        dma((2, 2, 4)),
        dma((2, 8)),
        dma((2, 8, 2)),
        dma((2, 2)),
        dma((2, 2)),
        dma((2, 2, 6)),
        dma((2, 2, 6)),
        dma((32,)),
        dma((8, 4)),
        dma((15,)),
        dma((15,)),
    ]
    return pl.pallas_call(
        kernel,
        out_shape=jax.ShapeDtypeStruct((2, 256, WIDTH), BF16),
        in_specs=[hbm, hbm, vmem, vmem, vmem, hbm, vmem, hbm, vmem, vmem, vmem, vmem, hbm],
        out_specs=hbm,
        scratch_shapes=scratch,
        compiler_params=pltpu.CompilerParams(
            collective_id=0, has_side_effects=True, vmem_limit_bytes=62 * 1024 * 1024
        ),
    )(
        residual_in,
        jnp.transpose(mr_qkv, (0, 2, 1, 3)),
        mr_short_w,
        mr_filter,
        mr_skip.reshape(1, WIDTH),
        mr_out_w,
        lr_gain.reshape(1, 8 * WIDTH),
        jnp.transpose(lr_in_w, (1, 0, 2)),
        lr_short_w,
        lr_rate,
        lr_res,
        lr_skip.reshape(1, WIDTH),
        lr_out_w,
    )


def solution(mesh):
    in_specs = (
        P(None, "ctx", "tp"),
        P(None, "ctx", None, "tp"),
        P(None, None, "tp"),
        P(None, "tp"),
        P("tp"),
        P("tp", "ctx"),
        P(),
        P(None, None, "tp"),
        P(None, None, "tp"),
        P(None, "tp"),
        P(None, "tp"),
        P("tp"),
        P("tp", "ctx"),
    )
    return jax.shard_map(local, mesh=mesh, in_specs=in_specs, out_specs=P(None, "ctx", "tp"), check_vma=False)
```

```python
import jax
import jax.numpy as jnp
from jax import lax
from jax.experimental import pallas as pl
from jax.experimental.pallas import tpu as pltpu
from jax.sharding import PartitionSpec as P

MESH = pl.DeviceIdType.MESH
F32 = jnp.float32
BF16 = jnp.bfloat16

SEGS = 8
STEPS = 64
ROWS = SEGS * STEPS
WIDTH = 512
TAPS = 128
POLES = 16
LANES = 128


def kernel(
    res_h, qkv_h, sw1, filt, skip1, wo1_h, gain, win_h, sw2, rate, resid, skip2, wo2_h,
    out_h,
    qkv_v, xtail, x32, q32, uext, fb, pk_s, pk_r, zo, zn, w, win, ps, pr, pacc, mid, scaled, acc, ssq,
    ltail_s, ltail, est, decays, weights, st_s, st_r, hin, obf, resv,
    loc, hs, hr, wsnd, fsnd, bsnd, wrecv, zs, zr, pss, prs, ags, agr, sts, strv,
):
    c = lax.axis_index("ctx")
    t = lax.axis_index("tp")
    core = c % 2
    m = c // 2
    y = m % 4
    xh = m // 4
    z = t // 2
    xl = t % 2
    sib = c + 1 - 2 * core
    xn = t + 1 - 2 * xl

    def ztp(dz, x):
        return ((z + dz) % 4) * 2 + x

    def remote(src, dst, ssem, rsem, ctx, tp):
        return pltpu.make_async_remote_copy(
            src_ref=src,
            dst_ref=dst,
            send_sem=ssem,
            recv_sem=rsem,
            device_id={"ctx": ctx, "tp": tp},
            device_id_type=MESH,
        )

    def arrived(ref, sem):
        pltpu.make_async_copy(ref, ref, sem).wait()

    load_qkv = pltpu.make_async_copy(qkv_h, qkv_v, loc.at[0])
    load_qkv.start()
    load_res = pltpu.make_async_copy(res_h, resv, loc.at[1])
    load_res.start()

    barrier = pltpu.get_barrier_semaphore()

    def greet(ctx, tp):
        pl.semaphore_signal(barrier, inc=1, device_id={"ctx": ctx, "tp": tp}, device_id_type=MESH)

    for d in range(1, 16):
        greet((c + d) % 16, t)
    greet(c, xn)
    greet((c + 8) % 16, xn)
    greet(c, ztp(1, xl))
    greet(c, ztp(3, xl))
    pl.semaphore_wait(barrier, 19)

    tail_copy = remote(qkv_h.at[:, :, 248:256, :], xtail, hs.at[0], hr.at[0], (c + 1) % 16, t)
    tail_copy.start()

    holder = (y + xl) % 2 == 0
    relay = (y + xl) % 2 == 1
    ups = ((y + 1) % 4, (y + 3) % 4)

    def place_of(k, row):
        xs = (xl, 1 - xl, 1 - xl, xl)[k]
        xhs = (xh, xh, 1 - xh, 1 - xh)[k]
        return xs * 4 + xhs * 2 + row // 2

    def ctx_of(h, row):
        return (h * 4 + row) * 2 + core

    def weight_first(stage, source):
        mine = place_of(0, y)
        target = w.at[stage, mine, core]
        arrival = wrecv.at[stage, mine, core]
        home = pltpu.make_async_copy(source, target, arrival)
        along = [
            remote(source, target, wsnd.at[stage, 0], arrival, ctx_of(xh, ups[0]), t),
            remote(source, target, wsnd.at[stage, 1], arrival, ctx_of(xh, ups[1]), t),
            remote(source, target, wsnd.at[stage, 2], arrival, ctx_of(1 - xh, y), t),
        ]
        across = [
            remote(source, target, wsnd.at[stage, 0], arrival, c, xn),
            remote(source, target, wsnd.at[stage, 1], arrival, ctx_of(1 - xh, y), xn),
        ]
        return home, along, across

    def weight_start(stage, source):
        home, along, across = weight_first(stage, source)

        @pl.when(holder)
        def _():
            home.start()
            for copy in along:
                copy.start()

        @pl.when(relay)
        def _():
            for copy in across:
                copy.start()

    def weight_pass(stage, index, sem, ctx):
        block = w.at[stage, index, core]
        return remote(block, block, sem, wrecv.at[stage, index, core], ctx, t)

    def weight_pass_half(stage, index, half, sem, ctx):
        block = w.at[stage, index, core, 256 * half : 256 * (half + 1), :]
        return remote(block, block, sem, wrecv.at[stage, index, core], ctx, t)

    def weight_got(stage, index):
        arrived(w.at[stage, index, core], wrecv.at[stage, index, core])

    def weight_moves(stage, k):
        here, up, down, far = place_of(k, y), place_of(k, ups[0]), place_of(k, ups[1]), place_of(k, (y + 2) % 4)

        def sibling(index, n):
            return weight_pass(stage, index, bsnd.at[stage, n], sib)

        held = [sibling(here, k)]
        if k:
            held += [weight_pass(stage, here, fsnd.at[stage, n, k], ctx_of(xh, ups[n])) for n in range(2)]
        late = [sibling(far, 4 + k)]
        below = [sibling(down, k), weight_pass_half(stage, down, 0, fsnd.at[stage, 0, k], ctx_of(xh, ups[0]))]
        above = [sibling(up, 4 + k), weight_pass_half(stage, up, 1, fsnd.at[stage, 1, k], ctx_of(xh, ups[1]))]
        return (here, held), (far, late), (down, below), (up, above)

    def weight_hold(stage, *ks):
        @pl.when(holder)
        def _():
            for k in ks:
                first_ = weight_moves(stage, k)[0]
                weight_got(stage, first_[0])
                for copy in reversed(first_[1]):
                    copy.start()

    def weight_relay(stage, k):
        _, _, below, above = weight_moves(stage, k)

        @pl.when(relay)
        def _():
            for index, copies in (below, above):
                weight_got(stage, index)
                for copy in reversed(copies):
                    copy.start()

    def weight_late(stage, *ks):
        @pl.when(holder)
        def _():
            for k in ks:
                _, (index, copies), _, _ = weight_moves(stage, k)
                weight_got(stage, index)
                copies[0].start()

    def weight_sibling(stage, index):
        arrived(w.at[stage, index, 1 - core], wrecv.at[stage, index, 1 - core])

    def weight_drain(stage, source):
        _, along, across = weight_first(stage, source)

        @pl.when(holder)
        def _():
            for copy in along:
                copy.wait_send()
            for k in range(4):
                first_, late, _, _ = weight_moves(stage, k)
                for copy in first_[1] + late[1]:
                    copy.wait_send()

        @pl.when(relay)
        def _():
            for copy in across:
                copy.wait_send()
            for k in range(4):
                _, _, below, above = weight_moves(stage, k)
                for copy in below[1] + above[1]:
                    copy.wait_send()

    weight_start(0, wo1_h)
    load_win = pltpu.make_async_copy(win_h, win, loc.at[2])

    seg = lax.broadcasted_iota(jnp.int32, (SEGS, WIDTH), 0)
    seg1 = lax.broadcasted_iota(jnp.int32, (SEGS, LANES), 0)
    first = seg % 4 == 0
    live = jnp.where(c > 0, 1.0, 0.0).astype(F32)

    def rows(j, count=1):
        start = j * SEGS
        return pl.ds(start if isinstance(start, int) else pl.multiple_of(start, SEGS), count * SEGS)

    def lanes(lt):
        return pl.ds(pl.multiple_of(lt * LANES, LANES), LANES)

    @pl.loop(0, TAPS // 8)
    def _(i):
        taps = filt[pl.ds(pl.multiple_of(i * 8, 8), 8), :].astype(F32)
        for k in range(8):
            fb[rows(i * 8 + k), :] = jnp.broadcast_to(taps[k : k + 1, :], (SEGS, WIDTH))

    load_qkv.wait()
    for s in range(2):
        for p in range(3):

            @pl.loop(0, 16)
            def _(i, s=s, p=p):
                here = pl.ds(pl.multiple_of(i * 16, 16), 16)
                there = pl.ds(pl.multiple_of(s * 256 + i * 16, 16), 16)
                values = qkv_v[s, p, here, :].astype(F32)
                for k in range(WIDTH // LANES):
                    x32[p, k, there, :] = values[:, LANES * k : LANES * (k + 1)]

    def tap(ref, lag, p):
        return jnp.broadcast_to(ref[lag, p : p + 1, :], (SEGS, WIDTH))

    def strided3(p, j):
        return jnp.concatenate(
            [x32[p, k, pl.ds(j, SEGS, stride=STEPS), :] for k in range(WIDTH // LANES)], axis=1
        )

    def medium(j, now, before, before2):
        mixed = [tap(sw1, 0, p) * now[p] + tap(sw1, 1, p) * before[p] + tap(sw1, 2, p) * before2[p] for p in range(3)]
        q32[rows(j), :] = mixed[0]
        uext[rows(j + 128), :] = (mixed[1] * mixed[2]).astype(BF16).astype(F32)

    last = [strided3(p, 63) for p in range(3)]
    last2 = [strided3(p, 62) for p in range(3)]
    x0 = [strided3(p, 0) for p in range(3)]
    x1 = [strided3(p, 1) for p in range(3)]
    own1 = [jnp.where(first, 0.0, pltpu.roll(v, 1, 0)) for v in last]
    own2 = [jnp.where(first, 0.0, pltpu.roll(v, 1, 0)) for v in last2]
    medium(0, x0, own1, own2)
    medium(1, x1, x0, own1)

    def medium_step(j, carried):
        now = [strided3(p, j) for p in range(3)]
        before, before2 = carried
        medium(j, now, before, before2)
        return now, before

    lax.fori_loop(2, STEPS, medium_step, (x1, x0))

    @pl.loop(0, STEPS // 4)
    def _(i):
        packed = []
        for k in range(2):
            even = uext[rows(128 + 4 * i + 2 * k), :]
            odd = uext[rows(129 + 4 * i + 2 * k), :]
            packed.append(jnp.where(seg % 4 >= 2, even, pltpu.roll(odd, 6, 0)))
        pk_s[pl.ds(pl.multiple_of(i * 16, 16), 16), :] = jnp.concatenate(packed, axis=0).astype(BF16)

    u_copy = remote(pk_s, pk_r, hs.at[1], hr.at[1], (c + 1) % 16, t)
    u_copy.start()
    weight_hold(0, 0, 1, 2)
    weight_relay(0, 0)

    arrived(xtail, hr.at[0])

    def halo(p, row):
        top = xtail[0, p].astype(F32)[row : row + 1, :] * live
        bottom = xtail[1, p].astype(F32)[row : row + 1, :] * live
        return jnp.where(seg < 4, jnp.broadcast_to(top, (SEGS, WIDTH)), jnp.broadcast_to(bottom, (SEGS, WIDTH)))

    full1 = [jnp.where(first, halo(p, 7), own1[p]) for p in range(3)]
    full2 = [jnp.where(first, halo(p, 6), own2[p]) for p in range(3)]
    medium(0, x0, full1, full2)
    medium(1, x1, x0, full1)

    load_win.start()
    arrived(pk_r, hr.at[1])

    @pl.loop(0, STEPS // 2)
    def _(i):
        both = pk_r[pl.ds(pl.multiple_of((i // 2) * 16, 16), 16), :].astype(F32) * live
        got = jnp.where(i % 2 == 0, both[:SEGS], both[SEGS:])
        even = uext[rows(128 + 2 * i), :]
        odd = uext[rows(129 + 2 * i), :]
        uext[rows(64 + 2 * i), :] = jnp.where(first, pltpu.roll(got, 5, 0), pltpu.roll(even, 1, 0))
        uext[rows(65 + 2 * i), :] = jnp.where(first, pltpu.roll(got, 7, 0), pltpu.roll(odd, 1, 0))
        uext[rows(2 * i), :] = jnp.where(seg % 4 < 2, pltpu.roll(got, 6, 0), pltpu.roll(even, 2, 0))
        uext[rows(1 + 2 * i), :] = jnp.where(seg % 4 < 2, got, pltpu.roll(odd, 2, 0))


    HALF = ROWS // 2

    def z_copy(stage, part):
        return remote(zo.at[stage, part], zn.at[stage, part], zs.at[stage, part], zr.at[stage, part], c, xn)

    def p_copy(stage, part, i):
        return remote(
            ps.at[stage, part, i],
            pr.at[stage, part, i],
            pss.at[stage, part, i],
            prs.at[stage, part, i],
            c,
            ztp(1 if i % 2 == 0 else 3, xl),
        )

    def term(stage, part, d, half):
        dest = (z + d) % 4
        both = jnp.concatenate([zo[stage, part], zn[stage, part]], axis=1)
        weights = jnp.concatenate([w[stage, xl * 4 + dest, half], w[stage, (1 - xl) * 4 + dest, half]], axis=0)
        return jnp.dot(both, weights, preferred_element_type=F32)

    def project_first(stage, part):
        arrived(zn.at[stage, part], zr.at[stage, part])
        for i, d, half in ((0, 2, 0), (1, 2, 1), (2, 1, 1), (3, 3, 0)):
            if part == 0 and i in (0, 2, 3):
                for source in range(2):
                    weight_sibling(stage, source * 4 + (z + d) % 4)
            ps[stage, part, i] = term(stage, part, d, half).astype(BF16)
            p_copy(stage, part, i).start()

    def project_own(stage, part):
        if part == 0:
            for source in range(2):
                weight_sibling(stage, source * 4 + z)
        for own in range(2):
            pacc[HALF * part : HALF * (part + 1), 256 * own : 256 * (own + 1)] = term(stage, part, 0, own)

    def project_relay(stage, part):
        for i, d, half in ((4, 1, 0), (5, 3, 1)):
            mine = term(stage, part, d, half)
            arrived(pr.at[stage, part, i - 4], prs.at[stage, part, i - 4])
            ps[stage, part, i] = (mine + pr[stage, part, i - 4].astype(F32)).astype(BF16)
            p_copy(stage, part, i).start()

    def project(stage, take, between):
        project_first(stage, 0)
        project_own(stage, 0)
        project_relay(stage, 0)
        project_first(stage, 1)
        project_own(stage, 1)
        take(0)
        project_relay(stage, 1)
        between()
        take(1)

    def project_wait(stage, part):
        for i in (2, 3, 4, 5):
            arrived(pr.at[stage, part, i], prs.at[stage, part, i])

    def project_drain(stage):
        for part in range(2):
            z_copy(stage, part).wait_send()
            for i in range(6):
                p_copy(stage, part, i).wait_send()

    def arrivals(stage, part, i):
        here = pl.ds(pl.multiple_of(i * 16, 16), 16)
        left = pr[stage, part, 3, here, :].astype(F32) + pr[stage, part, 4, here, :].astype(F32)
        right = pr[stage, part, 2, here, :].astype(F32) + pr[stage, part, 5, here, :].astype(F32)
        own = pacc[pl.ds(pl.multiple_of(part * HALF + i * 16, 16), 16), :]
        return own + jnp.concatenate([left, right], axis=1)

    def filter_blocks(first_block):
        @pl.loop(first_block, first_block + 2)
        def _(block):
            lane = lanes((block % 8) // 2)
            part = block // 8
            r0 = (block % 2) * 16
            j0 = part * 32 + r0

            def taps8(ib, totals):
                base = 128 + j0 - 8 * ib - 7
                window = uext[pl.ds(pl.multiple_of(base * SEGS, SEGS), 23 * SEGS), lane]
                weights = fb[pl.ds(pl.multiple_of(ib * 64, 64), 64), lane]
                totals = list(totals)
                for b in range(8):
                    f = weights[b * SEGS : (b + 1) * SEGS]
                    for a in range(16):
                        k = a + 7 - b
                        totals[a] = totals[a] + f * window[k * SEGS : (k + 1) * SEGS]
                return tuple(totals)

            totals = lax.fori_loop(0, 16, taps8, tuple(jnp.zeros((SEGS, LANES), F32) for _ in range(16)))
            skip = jnp.broadcast_to(skip1[:, lane], (SEGS, LANES))
            for a in range(0, 16, 2):
                pair = []
                for k in (a, a + 1):
                    u = uext[rows(128 + j0 + k), lane]
                    pair.append(q32[rows(j0 + k), lane] * (totals[k] + skip * u))
                zo[0, part, pl.ds(pl.multiple_of((r0 + a) * SEGS, 16), 16), lane] = jnp.concatenate(
                    pair, axis=0
                ).astype(BF16)

    filter_blocks(0)
    filter_blocks(2)
    weight_hold(0, 3)
    weight_relay(0, 1)
    filter_blocks(4)
    filter_blocks(6)
    z_copy(0, 0).start()
    weight_late(0, 0)
    filter_blocks(8)
    weight_relay(0, 2)
    weight_late(0, 1)
    filter_blocks(10)
    filter_blocks(12)
    weight_relay(0, 3)
    weight_late(0, 2)
    filter_blocks(14)
    z_copy(0, 1).start()
    weight_late(0, 3)
    weight_start(1, wo2_h)

    load_res.wait()

    @pl.loop(0, 32)
    def _(i):
        s = i // 16
        r = (i % 16) * 16
        values = resv[s, pl.ds(pl.multiple_of(r, 16), 16), :].astype(F32)
        for k in range(WIDTH // LANES):
            x32[0, k, pl.ds(pl.multiple_of(i * 16, 16), 16), :] = values[:, LANES * k : LANES * (k + 1)]

    @pl.loop(0, STEPS)
    def _(j):
        for k in range(WIDTH // LANES):
            x32[1, k, rows(j), :] = x32[0, k, pl.ds(j, SEGS, stride=STEPS), :]

    sent = []

    def send(slot, quarter, tp):
        k = len(sent)
        copy = remote(
            mid.at[slot, quarter], mid.at[slot, quarter], ags.at[k], agr.at[slot, quarter], c, tp
        )
        copy.start()
        sent.append(copy)

    zp, zm, zz = ztp(1, xl), ztp(3, xl), ztp(2, xl)
    xp, xm, xz = ztp(1, 1 - xl), ztp(3, 1 - xl), ztp(2, 1 - xl)
    def take_middle(part):
        project_wait(0, part)

        @pl.loop(0, 16)
        def _(i):
            here = pl.ds(pl.multiple_of(part * HALF + i * 16, 16), 16)
            before = jnp.concatenate([x32[1, k, here, :] for k in range(WIDTH // LANES)], axis=1)
            value = (before + arrivals(0, part, i)).astype(BF16)
            mid[t, part * 2 + i // 8, pl.ds(pl.multiple_of((i % 8) * 16, 16), 16), :] = value

        for quarter in (2 * part, 2 * part + 1):
            send(t, quarter, xn)
            send(t, quarter, zp)
            send(t, quarter, zm)

    def next_weights():
        weight_hold(1, 0, 1, 2)
        weight_relay(1, 0)

    project(0, take_middle, next_weights)

    def have(slot, *quarters):
        for quarter in quarters:
            arrived(mid.at[slot, quarter], agr.at[slot, quarter])

    load_win.wait()

    def absorb(*slots, fresh=False):
        count = len(slots)
        scales = [gain[:, pl.ds(pl.multiple_of(slot * WIDTH, WIDTH), WIDTH)] for slot in slots]

        @pl.loop(0, 16)
        def _(i):
            here = pl.ds(pl.multiple_of((i % 4) * 32, 32), 32)
            there = pl.ds(pl.multiple_of(i * 32, 32), 32)
            total = 0.0 if fresh else ssq[there, :]
            for k, slot in enumerate(slots):
                values = mid[slot, i // 4, here, :].astype(F32)
                square = values * values
                total += square[:, 0:128] + square[:, 128:256] + square[:, 256:384] + square[:, 384:512]
                scaled[there, WIDTH * k : WIDTH * (k + 1)] = (values * scales[k]).astype(BF16)
            ssq[there, :] = total

        @pl.loop(0, 6)
        def _(i):
            cols = pl.ds(pl.multiple_of((i % 2) * 256, 256), 256)
            weights = [win[i // 2, pl.ds(pl.multiple_of(slot * WIDTH, WIDTH), WIDTH), cols] for slot in slots]
            product = jnp.dot(
                scaled[:, 0 : WIDTH * count], jnp.concatenate(weights, axis=0), preferred_element_type=F32
            )
            acc[i // 2, :, cols] = product if fresh else acc[i // 2, :, cols] + product

    absorb(t, fresh=True)
    weight_hold(1, 3)
    weight_relay(1, 1)
    have(xn, 0, 1)
    for quarter in range(2):
        send(xn, quarter, zp)
        send(xn, quarter, zm)
    have(zm, 0, 1, 2, 3)
    send(zm, 0, zp)
    send(zm, 2, zp)
    send(zm, 2, xn)
    send(zm, 3, xn)
    have(zp, 0, 1, 2, 3)
    send(zp, 1, zm)
    send(zp, 3, zm)
    send(zp, 2, xn)
    send(zp, 3, xn)
    absorb(zm, zp)
    weight_relay(1, 2)
    have(xm, 0, 1)
    send(xm, 0, zp)
    have(xp, 0, 1)
    send(xp, 1, zm)
    have(zz, 0, 1, 2, 3)
    send(zz, 2, xn)
    send(zz, 3, xn)
    have(xn, 2, 3)
    absorb(xn, zz)
    weight_relay(1, 3)
    have(xm, 2, 3)
    have(xp, 2, 3)
    absorb(xm, xp)
    have(xz, 0, 1, 2, 3)
    absorb(xz)
    weight_late(1, 0, 1, 2, 3)

    def factors(start, count):
        here = pl.ds(start if isinstance(start, int) else pl.multiple_of(start, count), count)
        meansq = jnp.sum(ssq[here, :], axis=1, keepdims=True) * (1.0 / 4096.0)
        ssq[here, :] = jnp.broadcast_to(lax.rsqrt(meansq + 1e-6), (count, LANES))

    def rounded(p, here):
        factor = jnp.concatenate([ssq[here, :]] * (WIDTH // LANES), axis=1)
        return (acc[p, here, :] * factor).astype(BF16)

    def normal(j):
        return [rounded(p, rows(j)).astype(F32) for p in range(3)]

    factors(ROWS - 16, 16)
    for p in range(3):
        ltail_s[p] = rounded(p, pl.ds(ROWS - 16, 16))
    l_copy = remote(ltail_s, ltail, hs.at[2], hr.at[2], (c + 1) % 16, t)
    l_copy.start()

    @pl.loop(0, 7)
    def _(i):
        factors(i * 64, 64)

    factors(448, 32)
    factors(480, 16)

    def longer(j, now, before, before2):
        mixed = [tap(sw2, 0, p) * now[p] + tap(sw2, 1, p) * before[p] + tap(sw2, 2, p) * before2[p] for p in range(3)]
        q32[rows(j), :] = mixed[0]
        uext[rows(j), :] = mixed[1] * mixed[2]

    y0, y1 = normal(0), normal(1)

    def longer_step(j, carried):
        now = normal(j)
        before, before2 = carried
        longer(j, now, before, before2)
        return now, before

    y63, y62 = lax.fori_loop(2, STEPS, longer_step, (y1, y0))

    arrived(ltail, hr.at[2])
    edge1, edge2 = [], []
    for p in range(3):
        got = ltail[p].astype(F32) * live
        edge2.append(jnp.where(first, pltpu.roll(got[:SEGS], 5, 0), pltpu.roll(y62[p], 1, 0)))
        edge1.append(jnp.where(first, pltpu.roll(got[SEGS:], 5, 0), pltpu.roll(y63[p], 1, 0)))
    longer(0, y0, edge1, edge2)
    longer(1, y1, y0, edge1)

    def row_of(ref, n, lane):
        return jnp.broadcast_to(ref[n : n + 1, lane], (SEGS, LANES))

    @pl.loop(0, WIDTH // LANES)
    def _(lt):
        lane = lanes(lt)
        decay = [jnp.exp(-row_of(rate, n, lane)) for n in range(POLES)]

        def step(i, states):
            for k in range(4):
                u = uext[rows(4 * i + k), lane]
                states = [decay[n] * states[n] + u for n in range(POLES)]
            return tuple(states)

        states = lax.fori_loop(0, STEPS // 4, step, tuple(jnp.zeros((SEGS, LANES), F32) for _ in range(POLES)))
        for n in range(POLES):
            est[rows(n), lane] = states[n]
            decays[rows(n), lane] = decay[n]

    place = seg1 % 4

    @pl.loop(0, WIDTH // LANES)
    def _(lt):
        lane = lanes(lt)
        for g in range(2):
            packed = []
            for h in range(2):
                total = jnp.zeros((SEGS, LANES), F32)
                for r in range(4):
                    n = g * 8 + h * 4 + r
                    span = jnp.exp(-float(STEPS) * row_of(rate, n, lane))
                    value = est[rows(n), lane]
                    value = value + span * jnp.where(place >= 1, pltpu.roll(value, 1, 0), 0.0)
                    value = value + span * span * jnp.where(place >= 2, pltpu.roll(value, 2, 0), 0.0)
                    est[rows(n), lane] = jnp.where(place >= 1, pltpu.roll(value, 1, 0), 0.0)
                    end = value if r == 3 else pltpu.roll(value, (r - 3) % 8, 0)
                    total = jnp.where(place == r, end, total)
                packed.append(total)
            st_s[pl.ds(g * 16, 16), lane] = jnp.concatenate(packed, axis=0).astype(BF16)

    def state_copy(d):
        return remote(st_s, st_r.at[d - 1], sts.at[d - 1], strv.at[d - 1], c + d, t)

    for d in range(15, 0, -1):

        @pl.when(c + d < 16)
        def _(d=d):
            state_copy(d).start()

    @pl.loop(0, WIDTH // LANES)
    def _(lt):
        lane = lanes(lt)
        for n in range(POLES):
            weights[rows(n), lane] = row_of(resid, n, lane) * jnp.sqrt(1.0 - jnp.exp(-2.0 * row_of(rate, n, lane)))

    packs = []
    for g in range(4):
        total = jnp.zeros((SEGS, WIDTH), F32)
        for r in range(4):
            n = g * 4 + r
            total = jnp.where(seg % 4 == r, jnp.broadcast_to(rate[n : n + 1, :], (SEGS, WIDTH)), total)
        packs.append(total)
    pack = jnp.concatenate(packs, axis=0)
    hin[...] = jnp.zeros((4 * SEGS, WIDTH), F32)
    for d in range(1, 16):

        @pl.when(c - d >= 0)
        def _(d=d):
            arrived(st_r.at[d - 1], strv.at[d - 1])
            hin[...] += jnp.exp(pack * (-256.0 * (d - 1))) * st_r[d - 1].astype(F32)

    for part in range(2):

        @pl.loop(0, WIDTH // LANES)
        def _(lt, part=part):
            lane = lanes(lt)
            decay, weight, states = [], [], []
            for n in range(POLES):
                decay.append(decays[rows(n), lane])
                weight.append(weights[rows(n), lane])
                state = est[rows(n), lane]
                if part == 0:
                    r = row_of(rate, n, lane)
                    k = (n // 4) * SEGS + n % 4
                    enter = jnp.where(
                        seg1 < 4,
                        jnp.broadcast_to(hin[k : k + 1, lane], (SEGS, LANES)),
                        jnp.broadcast_to(hin[k + 4 : k + 5, lane], (SEGS, LANES)),
                    )
                    state = state + jnp.exp(r * (place.astype(F32) * (-float(STEPS)))) * enter
                states.append(state)
            skip = jnp.broadcast_to(skip2[:, lane], (SEGS, LANES))

            def step(i, states):
                pair = []
                for k in range(2):
                    j = part * (STEPS // 2) + 2 * i + k
                    u = uext[rows(j), lane]
                    states = [decay[n] * states[n] + u for n in range(POLES)]
                    terms = [weight[n] * states[n] for n in range(POLES)]
                    while len(terms) > 1:
                        terms = [terms[a] + terms[a + 1] for a in range(0, len(terms), 2)]
                    pair.append(q32[rows(j), lane] * (terms[0] + skip * u))
                zo[1, part, pl.ds(pl.multiple_of(i * 16, 16), 16), lane] = jnp.concatenate(pair, axis=0).astype(BF16)
                return tuple(states)

            states = lax.fori_loop(0, STEPS // 4, step, tuple(states))
            if part == 0:
                for n in range(POLES):
                    est[rows(n), lane] = states[n]

        z_copy(1, part).start()

    def take_last(part):
        project_wait(1, part)

        @pl.loop(0, 16)
        def _(i):
            base = mid[t, part * 2 + i // 8, pl.ds(pl.multiple_of((i % 8) * 16, 16), 16), :].astype(F32)
            value = base + arrivals(1, part, i)
            j = part * (STEPS // 2) + 2 * i
            for k in range(WIDTH // LANES):
                piece = value[:, LANES * k : LANES * (k + 1)]
                x32[2, k, pl.ds(j, SEGS, stride=STEPS), :] = piece[:SEGS]
                x32[2, k, pl.ds(j + 1, SEGS, stride=STEPS), :] = piece[SEGS:]

        @pl.loop(0, 8)
        def _(i):
            here = pl.ds(pl.multiple_of(i * STEPS + part * 32, 32), 32)
            there = pl.ds(pl.multiple_of(i % 4 * STEPS + part * 32, 32), 32)
            value = jnp.concatenate([x32[2, k, here, :] for k in range(WIDTH // LANES)], axis=1)
            obf[i // 4, there, :] = value.astype(BF16)

    project(1, take_last, lambda: None)

    store = pltpu.make_async_copy(obf, out_h, loc.at[3])
    store.start()

    tail_copy.wait_send()
    u_copy.wait_send()
    l_copy.wait_send()
    weight_drain(0, wo1_h)
    weight_drain(1, wo2_h)
    project_drain(0)
    project_drain(1)
    for copy in sent:
        copy.wait_send()
    for d in range(1, 16):

        @pl.when(c + d < 16)
        def _(d=d):
            state_copy(d).wait_send()

    store.wait()


def local(
    residual_in, mr_qkv, mr_short_w, mr_filter, mr_skip, mr_out_w, lr_gain,
    lr_in_w, lr_short_w, lr_rate, lr_res, lr_skip, lr_out_w,
):
    vmem = pl.BlockSpec(memory_space=pltpu.VMEM)
    hbm = pl.BlockSpec(memory_space=pl.ANY)
    dma = pltpu.SemaphoreType.DMA
    scratch = [
        pltpu.VMEM((2, 3, 256, WIDTH), BF16),
        pltpu.VMEM((2, 3, 8, WIDTH), BF16),
        pltpu.VMEM((3, WIDTH // LANES, ROWS, LANES), F32),
        pltpu.VMEM((ROWS, WIDTH), F32),
        pltpu.VMEM((192 * SEGS, WIDTH), F32),
        pltpu.VMEM((TAPS * SEGS, WIDTH), F32),
        pltpu.VMEM((256, WIDTH), BF16),
        pltpu.VMEM((256, WIDTH), BF16),
        pltpu.VMEM((2, 2, ROWS // 2, WIDTH), BF16),
        pltpu.VMEM((2, 2, ROWS // 2, WIDTH), BF16),
        pltpu.VMEM((2, 8, 2, WIDTH, 256), BF16),
        pltpu.VMEM((3, 4096, WIDTH), BF16),
        pltpu.VMEM((2, 2, 6, ROWS // 2, 256), BF16),
        pltpu.VMEM((2, 2, 6, ROWS // 2, 256), BF16),
        pltpu.VMEM((ROWS, WIDTH), F32),
        pltpu.VMEM((8, 4, 128, WIDTH), BF16),
        pltpu.VMEM((ROWS, 2 * WIDTH), BF16),
        pltpu.VMEM((3, ROWS, WIDTH), F32),
        pltpu.VMEM((ROWS, LANES), F32),
        pltpu.VMEM((3, 16, WIDTH), BF16),
        pltpu.VMEM((3, 16, WIDTH), BF16),
        pltpu.VMEM((POLES * SEGS, WIDTH), F32),
        pltpu.VMEM((POLES * SEGS, WIDTH), F32),
        pltpu.VMEM((POLES * SEGS, WIDTH), F32),
        pltpu.VMEM((4 * SEGS, WIDTH), BF16),
        pltpu.VMEM((15, 4 * SEGS, WIDTH), BF16),
        pltpu.VMEM((4 * SEGS, WIDTH), F32),
        pltpu.VMEM((2, 256, WIDTH), BF16),
        pltpu.VMEM((2, 256, WIDTH), BF16),
        dma((4,)),
        dma((3,)),
        dma((3,)),
        dma((2, 3)),
        dma((2, 2, 4)),
        dma((2, 8)),
        dma((2, 8, 2)),
        dma((2, 2)),
        dma((2, 2)),
        dma((2, 2, 6)),
        dma((2, 2, 6)),
        dma((32,)),
        dma((8, 4)),
        dma((15,)),
        dma((15,)),
    ]
    return pl.pallas_call(
        kernel,
        out_shape=jax.ShapeDtypeStruct((2, 256, WIDTH), BF16),
        in_specs=[hbm, hbm, vmem, vmem, vmem, hbm, vmem, hbm, vmem, vmem, vmem, vmem, hbm],
        out_specs=hbm,
        scratch_shapes=scratch,
        compiler_params=pltpu.CompilerParams(
            collective_id=0, has_side_effects=True, vmem_limit_bytes=62 * 1024 * 1024
        ),
    )(
        residual_in,
        jnp.transpose(mr_qkv, (0, 2, 1, 3)),
        mr_short_w,
        mr_filter,
        mr_skip.reshape(1, WIDTH),
        mr_out_w,
        lr_gain.reshape(1, 8 * WIDTH),
        jnp.transpose(lr_in_w, (1, 0, 2)),
        lr_short_w,
        lr_rate,
        lr_res,
        lr_skip.reshape(1, WIDTH),
        lr_out_w,
    )


def solution(mesh):
    in_specs = (
        P(None, "ctx", "tp"),
        P(None, "ctx", None, "tp"),
        P(None, None, "tp"),
        P(None, "tp"),
        P("tp"),
        P("tp", "ctx"),
        P(),
        P(None, None, "tp"),
        P(None, None, "tp"),
        P(None, "tp"),
        P(None, "tp"),
        P("tp"),
        P("tp", "ctx"),
    )
    return jax.shard_map(local, mesh=mesh, in_specs=in_specs, out_specs=P(None, "ctx", "tp"), check_vma=False)
```

```python
import jax
import jax.numpy as jnp
from jax import lax
from jax.experimental import pallas as pl
from jax.experimental.pallas import tpu as pltpu
from jax.sharding import PartitionSpec as P

MESH = pl.DeviceIdType.MESH
F32 = jnp.float32
BF16 = jnp.bfloat16

SEGS = 8
STEPS = 64
ROWS = SEGS * STEPS
WIDTH = 512
TAPS = 128
POLES = 16
LANES = 128


def kernel(
    res_h, qkv_h, sw1, filt, skip1, wo1_h, gain, win_h, sw2, rate, resid, skip2, wo2_h,
    out_h,
    qkv_v, xtail, x32, q32, uext, ueven, uodd, fb, pk_s, pk_r, zo, zn, w, win, ps, pr, pacc, mid, scaled, acc, ssq,
    ltail_s, ltail, est, decays, weights, st_s, st_r, hin, obf, resv,
    loc, hs, hr, wsnd, fsnd, bsnd, wrecv, zs, zr, pss, prs, ags, agr, sts, strv,
):
    c = lax.axis_index("ctx")
    t = lax.axis_index("tp")
    core = c % 2
    m = c // 2
    y = m % 4
    xh = m // 4
    z = t // 2
    xl = t % 2
    sib = c + 1 - 2 * core
    xn = t + 1 - 2 * xl

    def ztp(dz, x):
        return ((z + dz) % 4) * 2 + x

    def remote(src, dst, ssem, rsem, ctx, tp):
        return pltpu.make_async_remote_copy(
            src_ref=src,
            dst_ref=dst,
            send_sem=ssem,
            recv_sem=rsem,
            device_id={"ctx": ctx, "tp": tp},
            device_id_type=MESH,
        )

    def arrived(ref, sem):
        pltpu.make_async_copy(ref, ref, sem).wait()

    load_qkv = pltpu.make_async_copy(qkv_h, qkv_v, loc.at[0])
    load_qkv.start()
    load_res = pltpu.make_async_copy(res_h, resv, loc.at[1])
    load_res.start()

    barrier = pltpu.get_barrier_semaphore()

    def greet(ctx, tp):
        pl.semaphore_signal(barrier, inc=1, device_id={"ctx": ctx, "tp": tp}, device_id_type=MESH)

    for d in range(1, 16):
        greet((c + d) % 16, t)
    greet(c, xn)
    greet((c + 8) % 16, xn)
    greet(c, ztp(1, xl))
    greet(c, ztp(3, xl))
    pl.semaphore_wait(barrier, 19)

    tail_copy = remote(qkv_h.at[:, :, 248:256, :], xtail, hs.at[0], hr.at[0], (c + 1) % 16, t)
    tail_copy.start()

    holder = (y + xl) % 2 == 0
    relay = (y + xl) % 2 == 1
    ups = ((y + 1) % 4, (y + 3) % 4)

    def place_of(k, row):
        xs = (xl, 1 - xl, 1 - xl, xl)[k]
        xhs = (xh, xh, 1 - xh, 1 - xh)[k]
        return xs * 4 + xhs * 2 + row // 2

    def ctx_of(h, row):
        return (h * 4 + row) * 2 + core

    def weight_first(stage, source):
        mine = place_of(0, y)
        target = w.at[stage, mine, core]
        arrival = wrecv.at[stage, mine, core]
        home = pltpu.make_async_copy(source, target, arrival)
        along = [
            remote(source, target, wsnd.at[stage, 0], arrival, ctx_of(xh, ups[0]), t),
            remote(source, target, wsnd.at[stage, 1], arrival, ctx_of(xh, ups[1]), t),
            remote(source, target, wsnd.at[stage, 2], arrival, ctx_of(1 - xh, y), t),
        ]
        across = [
            remote(source, target, wsnd.at[stage, 0], arrival, c, xn),
            remote(source, target, wsnd.at[stage, 1], arrival, ctx_of(1 - xh, y), xn),
        ]
        return home, along, across

    def weight_start(stage, source):
        home, along, across = weight_first(stage, source)

        @pl.when(holder)
        def _():
            home.start()
            for copy in along:
                copy.start()

        @pl.when(relay)
        def _():
            for copy in across:
                copy.start()

    def weight_pass(stage, index, sem, ctx):
        block = w.at[stage, index, core]
        return remote(block, block, sem, wrecv.at[stage, index, core], ctx, t)

    def weight_pass_half(stage, index, half, sem, ctx):
        block = w.at[stage, index, core, 256 * half : 256 * (half + 1), :]
        return remote(block, block, sem, wrecv.at[stage, index, core], ctx, t)

    def weight_got(stage, index):
        arrived(w.at[stage, index, core], wrecv.at[stage, index, core])

    def weight_moves(stage, k):
        here, up, down, far = place_of(k, y), place_of(k, ups[0]), place_of(k, ups[1]), place_of(k, (y + 2) % 4)

        def sibling(index, n):
            return weight_pass(stage, index, bsnd.at[stage, n], sib)

        held = [sibling(here, k)]
        if k:
            held += [weight_pass(stage, here, fsnd.at[stage, n, k], ctx_of(xh, ups[n])) for n in range(2)]
        late = [sibling(far, 4 + k)]
        below = [sibling(down, k), weight_pass_half(stage, down, 0, fsnd.at[stage, 0, k], ctx_of(xh, ups[0]))]
        above = [sibling(up, 4 + k), weight_pass_half(stage, up, 1, fsnd.at[stage, 1, k], ctx_of(xh, ups[1]))]
        return (here, held), (far, late), (down, below), (up, above)

    def weight_hold(stage, *ks):
        @pl.when(holder)
        def _():
            for k in ks:
                first_ = weight_moves(stage, k)[0]
                weight_got(stage, first_[0])
                for copy in reversed(first_[1]):
                    copy.start()

    def weight_relay(stage, k):
        _, _, below, above = weight_moves(stage, k)

        @pl.when(relay)
        def _():
            for index, copies in (below, above):
                weight_got(stage, index)
                for copy in reversed(copies):
                    copy.start()

    def weight_late(stage, *ks):
        @pl.when(holder)
        def _():
            for k in ks:
                _, (index, copies), _, _ = weight_moves(stage, k)
                weight_got(stage, index)
                copies[0].start()

    def weight_sibling(stage, index):
        arrived(w.at[stage, index, 1 - core], wrecv.at[stage, index, 1 - core])

    def weight_drain(stage, source):
        _, along, across = weight_first(stage, source)

        @pl.when(holder)
        def _():
            for copy in along:
                copy.wait_send()
            for k in range(4):
                first_, late, _, _ = weight_moves(stage, k)
                for copy in first_[1] + late[1]:
                    copy.wait_send()

        @pl.when(relay)
        def _():
            for copy in across:
                copy.wait_send()
            for k in range(4):
                _, _, below, above = weight_moves(stage, k)
                for copy in below[1] + above[1]:
                    copy.wait_send()

    weight_start(0, wo1_h)
    load_win = pltpu.make_async_copy(win_h, win, loc.at[2])

    seg = lax.broadcasted_iota(jnp.int32, (SEGS, WIDTH), 0)
    seg1 = lax.broadcasted_iota(jnp.int32, (SEGS, LANES), 0)
    first = seg % 4 == 0
    live = jnp.where(c > 0, 1.0, 0.0).astype(F32)

    def rows(j, count=1):
        start = j * SEGS
        return pl.ds(start if isinstance(start, int) else pl.multiple_of(start, SEGS), count * SEGS)

    def lanes(lt):
        return pl.ds(pl.multiple_of(lt * LANES, LANES), LANES)

    @pl.loop(0, TAPS // 8)
    def _(i):
        taps = filt[pl.ds(pl.multiple_of(i * 8, 8), 8), :].astype(F32)
        for k in range(8):
            fb[pl.ds(pl.multiple_of((i * 8 + k) * 16, 16), 16), :] = jnp.broadcast_to(
                taps[k : k + 1, :], (16, WIDTH)
            ).astype(BF16)

    load_qkv.wait()
    for s in range(2):
        for p in range(3):

            @pl.loop(0, 16)
            def _(i, s=s, p=p):
                here = pl.ds(pl.multiple_of(i * 16, 16), 16)
                there = pl.ds(pl.multiple_of(s * 256 + i * 16, 16), 16)
                values = qkv_v[s, p, here, :].astype(F32)
                for k in range(WIDTH // LANES):
                    x32[p, k, there, :] = values[:, LANES * k : LANES * (k + 1)]

    def tap(ref, lag, p):
        return jnp.broadcast_to(ref[lag, p : p + 1, :], (SEGS, WIDTH))

    def strided3(p, j):
        return jnp.concatenate(
            [x32[p, k, pl.ds(j, SEGS, stride=STEPS), :] for k in range(WIDTH // LANES)], axis=1
        )

    def medium(j, now, before, before2):
        mixed = [tap(sw1, 0, p) * now[p] + tap(sw1, 1, p) * before[p] + tap(sw1, 2, p) * before2[p] for p in range(3)]
        q32[rows(j), :] = mixed[0]
        uext[rows(j + 128), :] = (mixed[1] * mixed[2]).astype(BF16).astype(F32)

    last = [strided3(p, 63) for p in range(3)]
    last2 = [strided3(p, 62) for p in range(3)]
    x0 = [strided3(p, 0) for p in range(3)]
    x1 = [strided3(p, 1) for p in range(3)]
    own1 = [jnp.where(first, 0.0, pltpu.roll(v, 1, 0)) for v in last]
    own2 = [jnp.where(first, 0.0, pltpu.roll(v, 1, 0)) for v in last2]
    medium(0, x0, own1, own2)
    medium(1, x1, x0, own1)

    def medium_step(j, carried):
        now = [strided3(p, j) for p in range(3)]
        before, before2 = carried
        medium(j, now, before, before2)
        return now, before

    lax.fori_loop(2, STEPS, medium_step, (x1, x0))

    @pl.loop(0, STEPS // 4)
    def _(i):
        packed = []
        for k in range(2):
            even = uext[rows(128 + 4 * i + 2 * k), :]
            odd = uext[rows(129 + 4 * i + 2 * k), :]
            packed.append(jnp.where(seg % 4 >= 2, even, pltpu.roll(odd, 6, 0)))
        pk_s[pl.ds(pl.multiple_of(i * 16, 16), 16), :] = jnp.concatenate(packed, axis=0).astype(BF16)

    u_copy = remote(pk_s, pk_r, hs.at[1], hr.at[1], (c + 1) % 16, t)
    u_copy.start()
    weight_hold(0, 0, 1, 2)
    weight_relay(0, 0)

    arrived(xtail, hr.at[0])

    def halo(p, row):
        top = xtail[0, p].astype(F32)[row : row + 1, :] * live
        bottom = xtail[1, p].astype(F32)[row : row + 1, :] * live
        return jnp.where(seg < 4, jnp.broadcast_to(top, (SEGS, WIDTH)), jnp.broadcast_to(bottom, (SEGS, WIDTH)))

    full1 = [jnp.where(first, halo(p, 7), own1[p]) for p in range(3)]
    full2 = [jnp.where(first, halo(p, 6), own2[p]) for p in range(3)]
    medium(0, x0, full1, full2)
    medium(1, x1, x0, full1)

    load_win.start()
    arrived(pk_r, hr.at[1])

    @pl.loop(0, STEPS // 2)
    def _(i):
        both = pk_r[pl.ds(pl.multiple_of((i // 2) * 16, 16), 16), :].astype(F32) * live
        got = jnp.where(i % 2 == 0, both[:SEGS], both[SEGS:])
        even = uext[rows(128 + 2 * i), :]
        odd = uext[rows(129 + 2 * i), :]
        uext[rows(64 + 2 * i), :] = jnp.where(first, pltpu.roll(got, 5, 0), pltpu.roll(even, 1, 0))
        uext[rows(65 + 2 * i), :] = jnp.where(first, pltpu.roll(got, 7, 0), pltpu.roll(odd, 1, 0))
        uext[rows(2 * i), :] = jnp.where(seg % 4 < 2, pltpu.roll(got, 6, 0), pltpu.roll(even, 2, 0))
        uext[rows(1 + 2 * i), :] = jnp.where(seg % 4 < 2, got, pltpu.roll(odd, 2, 0))


    HALF = ROWS // 2

    def z_copy(stage, part):
        return remote(zo.at[stage, part], zn.at[stage, part], zs.at[stage, part], zr.at[stage, part], c, xn)

    def p_copy(stage, part, i):
        return remote(
            ps.at[stage, part, i],
            pr.at[stage, part, i],
            pss.at[stage, part, i],
            prs.at[stage, part, i],
            c,
            ztp(1 if i % 2 == 0 else 3, xl),
        )

    def term(stage, part, d, half):
        dest = (z + d) % 4
        both = jnp.concatenate([zo[stage, part], zn[stage, part]], axis=1)
        weights = jnp.concatenate([w[stage, xl * 4 + dest, half], w[stage, (1 - xl) * 4 + dest, half]], axis=0)
        return jnp.dot(both, weights, preferred_element_type=F32)

    def project_first(stage, part):
        arrived(zn.at[stage, part], zr.at[stage, part])
        for i, d, half in ((0, 2, 0), (1, 2, 1), (2, 1, 1), (3, 3, 0)):
            if part == 0 and i in (0, 2, 3):
                for source in range(2):
                    weight_sibling(stage, source * 4 + (z + d) % 4)
            ps[stage, part, i] = term(stage, part, d, half).astype(BF16)
            p_copy(stage, part, i).start()

    def project_own(stage, part):
        if part == 0:
            for source in range(2):
                weight_sibling(stage, source * 4 + z)
        for own in range(2):
            pacc[HALF * part : HALF * (part + 1), 256 * own : 256 * (own + 1)] = term(stage, part, 0, own)

    def project_relay(stage, part):
        for i, d, half in ((4, 1, 0), (5, 3, 1)):
            mine = term(stage, part, d, half)
            arrived(pr.at[stage, part, i - 4], prs.at[stage, part, i - 4])
            ps[stage, part, i] = (mine + pr[stage, part, i - 4].astype(F32)).astype(BF16)
            p_copy(stage, part, i).start()

    def project(stage):
        project_first(stage, 0)
        project_first(stage, 1)
        project_relay(stage, 0)
        project_own(stage, 0)
        project_relay(stage, 1)
        project_own(stage, 1)

    def project_wait(stage, part):
        for i in (2, 3, 4, 5):
            arrived(pr.at[stage, part, i], prs.at[stage, part, i])

    def project_drain(stage):
        for part in range(2):
            z_copy(stage, part).wait_send()
            for i in range(6):
                p_copy(stage, part, i).wait_send()

    def arrivals(stage, part, i):
        here = pl.ds(pl.multiple_of(i * 16, 16), 16)
        left = pr[stage, part, 3, here, :].astype(F32) + pr[stage, part, 4, here, :].astype(F32)
        right = pr[stage, part, 2, here, :].astype(F32) + pr[stage, part, 5, here, :].astype(F32)
        own = pacc[pl.ds(pl.multiple_of(part * HALF + i * 16, 16), 16), :]
        return own + jnp.concatenate([left, right], axis=1)

    def filter_blocks(first_block):
        @pl.loop(first_block, first_block + 2)
        def _(block):
            lane = lanes((block % 8) // 2)
            part = block // 8
            r0 = (block % 2) * 16
            j0 = part * 32 + r0

            def taps8(ib, totals):
                base = 64 + j0 // 2 - 4 * ib - 3
                window = pl.ds(pl.multiple_of(base * 16, 16), 11 * 16)
                even, odd_ = ueven[window, lane], uodd[window, lane]
                taps = fb[pl.ds(pl.multiple_of(ib * 128, 128), 128), lane]
                totals = list(totals)
                for a in range(8):
                    terms = []
                    for b in range(8):
                        k = 3 - b // 2 + a
                        u = (odd_ if b % 2 else even)[k * 16 : (k + 1) * 16]
                        terms.append(taps[b * 16 : (b + 1) * 16] * u)
                    while len(terms) > 1:
                        terms = [terms[n] + terms[n + 1] for n in range(0, len(terms), 2)]
                    totals[a] = totals[a] + terms[0].astype(F32)
                return tuple(totals)

            totals = lax.fori_loop(0, 16, taps8, tuple(jnp.zeros((16, LANES), F32) for _ in range(8)))
            skip = jnp.broadcast_to(skip1[:, lane], (16, LANES))
            for a in range(8):
                u = uext[rows(128 + j0 + 2 * a, 2), lane]
                value = q32[rows(j0 + 2 * a, 2), lane] * (totals[a] + skip * u)
                zo[0, part, pl.ds(pl.multiple_of((r0 + 2 * a) * SEGS, 16), 16), lane] = value.astype(BF16)

    def pairs(first_pair, last_pair):
        @pl.loop(first_pair, last_pair)
        def _(i):
            here = pl.ds(pl.multiple_of(i * 16, 16), 16)
            ueven[here, :] = uext[rows(2 * i, 2), :].astype(BF16)
            uodd[here, :] = uext[rows(2 * i - 1, 2), :].astype(BF16)

    pairs(1, 96)
    filter_blocks(0)
    filter_blocks(2)
    weight_hold(0, 3)
    filter_blocks(4)
    filter_blocks(6)
    z_copy(0, 0).start()
    filter_blocks(8)
    filter_blocks(10)
    weight_relay(0, 1)
    filter_blocks(12)
    filter_blocks(14)
    z_copy(0, 1).start()
    weight_late(0, 0)
    weight_relay(0, 2)
    weight_late(0, 1)
    weight_relay(0, 3)
    weight_late(0, 2, 3)
    weight_start(1, wo2_h)

    load_res.wait()

    @pl.loop(0, 32)
    def _(i):
        s = i // 16
        r = (i % 16) * 16
        values = resv[s, pl.ds(pl.multiple_of(r, 16), 16), :].astype(F32)
        for k in range(WIDTH // LANES):
            x32[0, k, pl.ds(pl.multiple_of(i * 16, 16), 16), :] = values[:, LANES * k : LANES * (k + 1)]

    @pl.loop(0, STEPS)
    def _(j):
        for k in range(WIDTH // LANES):
            x32[1, k, rows(j), :] = x32[0, k, pl.ds(j, SEGS, stride=STEPS), :]

    project(0)
    weight_hold(1, 0, 1, 2)
    weight_relay(1, 0)

    sent = []

    def send(slot, quarter, tp):
        k = len(sent)
        copy = remote(
            mid.at[slot, quarter], mid.at[slot, quarter], ags.at[k], agr.at[slot, quarter], c, tp
        )
        copy.start()
        sent.append(copy)

    zp, zm, zz = ztp(1, xl), ztp(3, xl), ztp(2, xl)
    xp, xm, xz = ztp(1, 1 - xl), ztp(3, 1 - xl), ztp(2, 1 - xl)
    for part in range(2):
        project_wait(0, part)

        @pl.loop(0, 16)
        def _(i, part=part):
            here = pl.ds(pl.multiple_of(part * HALF + i * 16, 16), 16)
            before = jnp.concatenate([x32[1, k, here, :] for k in range(WIDTH // LANES)], axis=1)
            value = (before + arrivals(0, part, i)).astype(BF16)
            mid[t, part * 2 + i // 8, pl.ds(pl.multiple_of((i % 8) * 16, 16), 16), :] = value

        for quarter in (2 * part, 2 * part + 1):
            send(t, quarter, xn)
            send(t, quarter, zp)
            send(t, quarter, zm)

    def have(slot, *quarters):
        for quarter in quarters:
            arrived(mid.at[slot, quarter], agr.at[slot, quarter])

    load_win.wait()

    def absorb(*slots, fresh=False):
        count = len(slots)
        scales = [gain[:, pl.ds(pl.multiple_of(slot * WIDTH, WIDTH), WIDTH)] for slot in slots]

        @pl.loop(0, 16)
        def _(i):
            here = pl.ds(pl.multiple_of((i % 4) * 32, 32), 32)
            there = pl.ds(pl.multiple_of(i * 32, 32), 32)
            total = 0.0 if fresh else ssq[there, :]
            for k, slot in enumerate(slots):
                values = mid[slot, i // 4, here, :].astype(F32)
                square = values * values
                total += square[:, 0:128] + square[:, 128:256] + square[:, 256:384] + square[:, 384:512]
                scaled[there, WIDTH * k : WIDTH * (k + 1)] = (values * scales[k]).astype(BF16)
            ssq[there, :] = total

        @pl.loop(0, 6)
        def _(i):
            cols = pl.ds(pl.multiple_of((i % 2) * 256, 256), 256)
            weights = [win[i // 2, pl.ds(pl.multiple_of(slot * WIDTH, WIDTH), WIDTH), cols] for slot in slots]
            product = jnp.dot(
                scaled[:, 0 : WIDTH * count], jnp.concatenate(weights, axis=0), preferred_element_type=F32
            )
            acc[i // 2, :, cols] = product if fresh else acc[i // 2, :, cols] + product

    absorb(t, fresh=True)
    weight_hold(1, 3)
    weight_relay(1, 1)
    have(xn, 0, 1)
    for quarter in range(2):
        send(xn, quarter, zp)
        send(xn, quarter, zm)
    have(zm, 0, 1, 2, 3)
    send(zm, 0, zp)
    send(zm, 2, zp)
    send(zm, 2, xn)
    send(zm, 3, xn)
    have(zp, 0, 1, 2, 3)
    send(zp, 1, zm)
    send(zp, 3, zm)
    send(zp, 2, xn)
    send(zp, 3, xn)
    absorb(zm, zp)
    weight_relay(1, 2)
    have(xm, 0, 1)
    send(xm, 0, zp)
    have(xp, 0, 1)
    send(xp, 1, zm)
    have(zz, 0, 1, 2, 3)
    send(zz, 2, xn)
    send(zz, 3, xn)
    have(xn, 2, 3)
    absorb(xn, zz)
    weight_relay(1, 3)
    have(xm, 2, 3)
    have(xp, 2, 3)
    absorb(xm, xp)
    have(xz, 0, 1, 2, 3)
    absorb(xz)
    weight_late(1, 0, 1, 2, 3)

    def finish(i):
        here = pl.ds(i * 16 if isinstance(i, int) else pl.multiple_of(i * 16, 16), 16)
        meansq = jnp.sum(ssq[here, :], axis=1, keepdims=True) * (1.0 / 4096.0)
        factor = lax.rsqrt(meansq + 1e-6)
        values = [(acc[p, here, :] * factor).astype(BF16) for p in range(3)]
        for p in range(3):
            acc[p, here, :] = values[p].astype(F32)
        return values

    tails = finish(31)
    for p in range(3):
        ltail_s[p] = tails[p]
    l_copy = remote(ltail_s, ltail, hs.at[2], hr.at[2], (c + 1) % 16, t)
    l_copy.start()

    @pl.loop(0, 31)
    def _(i):
        finish(i)

    def longer(j, now, before, before2):
        mixed = [tap(sw2, 0, p) * now[p] + tap(sw2, 1, p) * before[p] + tap(sw2, 2, p) * before2[p] for p in range(3)]
        q32[rows(j), :] = mixed[0]
        uext[rows(j), :] = mixed[1] * mixed[2]

    @pl.loop(2, STEPS)
    def _(j):
        longer(
            j,
            [acc[p, rows(j), :] for p in range(3)],
            [acc[p, rows(j - 1), :] for p in range(3)],
            [acc[p, rows(j - 2), :] for p in range(3)],
        )

    arrived(ltail, hr.at[2])
    edge1, edge2 = [], []
    for p in range(3):
        got = ltail[p].astype(F32) * live
        edge2.append(jnp.where(first, pltpu.roll(got[:SEGS], 5, 0), pltpu.roll(acc[p, rows(62), :], 1, 0)))
        edge1.append(jnp.where(first, pltpu.roll(got[SEGS:], 5, 0), pltpu.roll(acc[p, rows(63), :], 1, 0)))
    y0 = [acc[p, rows(0), :] for p in range(3)]
    y1 = [acc[p, rows(1), :] for p in range(3)]
    longer(0, y0, edge1, edge2)
    longer(1, y1, y0, edge1)

    def row_of(ref, n, lane):
        return jnp.broadcast_to(ref[n : n + 1, lane], (SEGS, LANES))

    @pl.loop(0, WIDTH // LANES)
    def _(lt):
        lane = lanes(lt)
        decay = [jnp.exp(-row_of(rate, n, lane)) for n in range(POLES)]

        def step(i, states):
            for k in range(4):
                u = uext[rows(4 * i + k), lane]
                states = [decay[n] * states[n] + u for n in range(POLES)]
            return tuple(states)

        states = lax.fori_loop(0, STEPS // 4, step, tuple(jnp.zeros((SEGS, LANES), F32) for _ in range(POLES)))
        for n in range(POLES):
            est[rows(n), lane] = states[n]
            decays[rows(n), lane] = decay[n]

    place = seg1 % 4

    @pl.loop(0, WIDTH // LANES)
    def _(lt):
        lane = lanes(lt)
        for g in range(2):
            packed = []
            for h in range(2):
                total = jnp.zeros((SEGS, LANES), F32)
                for r in range(4):
                    n = g * 8 + h * 4 + r
                    span = jnp.exp(-float(STEPS) * row_of(rate, n, lane))
                    value = est[rows(n), lane]
                    value = value + span * jnp.where(place >= 1, pltpu.roll(value, 1, 0), 0.0)
                    value = value + span * span * jnp.where(place >= 2, pltpu.roll(value, 2, 0), 0.0)
                    est[rows(n), lane] = jnp.where(place >= 1, pltpu.roll(value, 1, 0), 0.0)
                    end = value if r == 3 else pltpu.roll(value, (r - 3) % 8, 0)
                    total = jnp.where(place == r, end, total)
                packed.append(total)
            st_s[pl.ds(g * 16, 16), lane] = jnp.concatenate(packed, axis=0).astype(BF16)

    def state_copy(d):
        return remote(st_s, st_r.at[d - 1], sts.at[d - 1], strv.at[d - 1], c + d, t)

    for d in range(15, 0, -1):

        @pl.when(c + d < 16)
        def _(d=d):
            state_copy(d).start()

    @pl.loop(0, WIDTH // LANES)
    def _(lt):
        lane = lanes(lt)
        for n in range(POLES):
            weights[rows(n), lane] = row_of(resid, n, lane) * jnp.sqrt(1.0 - jnp.exp(-2.0 * row_of(rate, n, lane)))

    packs = []
    for g in range(4):
        total = jnp.zeros((SEGS, WIDTH), F32)
        for r in range(4):
            n = g * 4 + r
            total = jnp.where(seg % 4 == r, jnp.broadcast_to(rate[n : n + 1, :], (SEGS, WIDTH)), total)
        packs.append(total)
    pack = jnp.concatenate(packs, axis=0)
    hin[...] = jnp.zeros((4 * SEGS, WIDTH), F32)
    for d in range(1, 16):

        @pl.when(c - d >= 0)
        def _(d=d):
            arrived(st_r.at[d - 1], strv.at[d - 1])
            hin[...] += jnp.exp(pack * (-256.0 * (d - 1))) * st_r[d - 1].astype(F32)

    for part in range(2):

        @pl.loop(0, WIDTH // LANES)
        def _(lt, part=part):
            lane = lanes(lt)
            decay, weight, states = [], [], []
            for n in range(POLES):
                decay.append(decays[rows(n), lane])
                weight.append(weights[rows(n), lane])
                state = est[rows(n), lane]
                if part == 0:
                    r = row_of(rate, n, lane)
                    k = (n // 4) * SEGS + n % 4
                    enter = jnp.where(
                        seg1 < 4,
                        jnp.broadcast_to(hin[k : k + 1, lane], (SEGS, LANES)),
                        jnp.broadcast_to(hin[k + 4 : k + 5, lane], (SEGS, LANES)),
                    )
                    state = state + jnp.exp(r * (place.astype(F32) * (-float(STEPS)))) * enter
                states.append(state)
            skip = jnp.broadcast_to(skip2[:, lane], (SEGS, LANES))

            def step(i, states):
                pair = []
                for k in range(2):
                    j = part * (STEPS // 2) + 2 * i + k
                    u = uext[rows(j), lane]
                    states = [decay[n] * states[n] + u for n in range(POLES)]
                    terms = [weight[n] * states[n] for n in range(POLES)]
                    while len(terms) > 1:
                        terms = [terms[a] + terms[a + 1] for a in range(0, len(terms), 2)]
                    pair.append(q32[rows(j), lane] * (terms[0] + skip * u))
                zo[1, part, pl.ds(pl.multiple_of(i * 16, 16), 16), lane] = jnp.concatenate(pair, axis=0).astype(BF16)
                return tuple(states)

            states = lax.fori_loop(0, STEPS // 4, step, tuple(states))
            if part == 0:
                for n in range(POLES):
                    est[rows(n), lane] = states[n]

        z_copy(1, part).start()

    project(1)
    for part in range(2):
        project_wait(1, part)

        @pl.loop(0, 16)
        def _(i, part=part):
            base = mid[t, part * 2 + i // 8, pl.ds(pl.multiple_of((i % 8) * 16, 16), 16), :].astype(F32)
            value = base + arrivals(1, part, i)
            j = part * (STEPS // 2) + 2 * i
            for k in range(WIDTH // LANES):
                piece = value[:, LANES * k : LANES * (k + 1)]
                x32[2, k, pl.ds(j, SEGS, stride=STEPS), :] = piece[:SEGS]
                x32[2, k, pl.ds(j + 1, SEGS, stride=STEPS), :] = piece[SEGS:]

    @pl.loop(0, 32)
    def _(i):
        s = i // 16
        r = (i % 16) * 16
        here = pl.ds(pl.multiple_of(i * 16, 16), 16)
        value = jnp.concatenate([x32[2, k, here, :] for k in range(WIDTH // LANES)], axis=1)
        obf[s, pl.ds(pl.multiple_of(r, 16), 16), :] = value.astype(BF16)

    store = pltpu.make_async_copy(obf, out_h, loc.at[3])
    store.start()

    tail_copy.wait_send()
    u_copy.wait_send()
    l_copy.wait_send()
    weight_drain(0, wo1_h)
    weight_drain(1, wo2_h)
    project_drain(0)
    project_drain(1)
    for copy in sent:
        copy.wait_send()
    for d in range(1, 16):

        @pl.when(c + d < 16)
        def _(d=d):
            state_copy(d).wait_send()

    store.wait()


def local(
    residual_in, mr_qkv, mr_short_w, mr_filter, mr_skip, mr_out_w, lr_gain,
    lr_in_w, lr_short_w, lr_rate, lr_res, lr_skip, lr_out_w,
):
    vmem = pl.BlockSpec(memory_space=pltpu.VMEM)
    hbm = pl.BlockSpec(memory_space=pl.ANY)
    dma = pltpu.SemaphoreType.DMA
    scratch = [
        pltpu.VMEM((2, 3, 256, WIDTH), BF16),
        pltpu.VMEM((2, 3, 8, WIDTH), BF16),
        pltpu.VMEM((3, WIDTH // LANES, ROWS, LANES), F32),
        pltpu.VMEM((ROWS, WIDTH), F32),
        pltpu.VMEM((192 * SEGS, WIDTH), F32),
        pltpu.VMEM((96 * 16, WIDTH), BF16),
        pltpu.VMEM((96 * 16, WIDTH), BF16),
        pltpu.VMEM((TAPS * 16, WIDTH), BF16),
        pltpu.VMEM((256, WIDTH), BF16),
        pltpu.VMEM((256, WIDTH), BF16),
        pltpu.VMEM((2, 2, ROWS // 2, WIDTH), BF16),
        pltpu.VMEM((2, 2, ROWS // 2, WIDTH), BF16),
        pltpu.VMEM((2, 8, 2, WIDTH, 256), BF16),
        pltpu.VMEM((3, 4096, WIDTH), BF16),
        pltpu.VMEM((2, 2, 6, ROWS // 2, 256), BF16),
        pltpu.VMEM((2, 2, 6, ROWS // 2, 256), BF16),
        pltpu.VMEM((ROWS, WIDTH), F32),
        pltpu.VMEM((8, 4, 128, WIDTH), BF16),
        pltpu.VMEM((ROWS, 2 * WIDTH), BF16),
        pltpu.VMEM((3, ROWS, WIDTH), F32),
        pltpu.VMEM((ROWS, LANES), F32),
        pltpu.VMEM((3, 16, WIDTH), BF16),
        pltpu.VMEM((3, 16, WIDTH), BF16),
        pltpu.VMEM((POLES * SEGS, WIDTH), F32),
        pltpu.VMEM((POLES * SEGS, WIDTH), F32),
        pltpu.VMEM((POLES * SEGS, WIDTH), F32),
        pltpu.VMEM((4 * SEGS, WIDTH), BF16),
        pltpu.VMEM((15, 4 * SEGS, WIDTH), BF16),
        pltpu.VMEM((4 * SEGS, WIDTH), F32),
        pltpu.VMEM((2, 256, WIDTH), BF16),
        pltpu.VMEM((2, 256, WIDTH), BF16),
        dma((4,)),
        dma((3,)),
        dma((3,)),
        dma((2, 3)),
        dma((2, 2, 4)),
        dma((2, 8)),
        dma((2, 8, 2)),
        dma((2, 2)),
        dma((2, 2)),
        dma((2, 2, 6)),
        dma((2, 2, 6)),
        dma((32,)),
        dma((8, 4)),
        dma((15,)),
        dma((15,)),
    ]
    return pl.pallas_call(
        kernel,
        out_shape=jax.ShapeDtypeStruct((2, 256, WIDTH), BF16),
        in_specs=[hbm, hbm, vmem, vmem, vmem, hbm, vmem, hbm, vmem, vmem, vmem, vmem, hbm],
        out_specs=hbm,
        scratch_shapes=scratch,
        compiler_params=pltpu.CompilerParams(
            collective_id=0, has_side_effects=True, vmem_limit_bytes=62 * 1024 * 1024
        ),
    )(
        residual_in,
        jnp.transpose(mr_qkv, (0, 2, 1, 3)),
        mr_short_w,
        mr_filter,
        mr_skip.reshape(1, WIDTH),
        mr_out_w,
        lr_gain.reshape(1, 8 * WIDTH),
        jnp.transpose(lr_in_w, (1, 0, 2)),
        lr_short_w,
        lr_rate,
        lr_res,
        lr_skip.reshape(1, WIDTH),
        lr_out_w,
    )


def solution(mesh):
    in_specs = (
        P(None, "ctx", "tp"),
        P(None, "ctx", None, "tp"),
        P(None, None, "tp"),
        P(None, "tp"),
        P("tp"),
        P("tp", "ctx"),
        P(),
        P(None, None, "tp"),
        P(None, None, "tp"),
        P(None, "tp"),
        P(None, "tp"),
        P("tp"),
        P("tp", "ctx"),
    )
    return jax.shard_map(local, mesh=mesh, in_specs=in_specs, out_specs=P(None, "ctx", "tp"), check_vma=False)
```

```python
import jax
import jax.numpy as jnp
from jax import lax
from jax.experimental import pallas as pl
from jax.experimental.pallas import tpu as pltpu
from jax.sharding import PartitionSpec as P

MESH = pl.DeviceIdType.MESH
F32 = jnp.float32
BF16 = jnp.bfloat16

SEGS = 8
STEPS = 64
ROWS = SEGS * STEPS
WIDTH = 512
TAPS = 128
POLES = 16
LANES = 128


def kernel(
    res_h, qkv_h, sw1, filt, skip1, wo1_h, gain, win_h, sw2, rate, resid, skip2, wo2_h,
    out_h,
    qkv_v, xtail, x32, q32, uext, ueven, uodd, fb, pk_s, pk_r, zo, zn, w, win, ps, pr, pacc, mid, scaled, acc, ssq,
    ltail_s, ltail, est, decays, weights, st_s, st_r, hin, obf, resv,
    loc, hs, hr, wsnd, fsnd, bsnd, wrecv, zs, zr, pss, prs, ags, agr, sts, strv,
):
    c = lax.axis_index("ctx")
    t = lax.axis_index("tp")
    core = c % 2
    m = c // 2
    y = m % 4
    xh = m // 4
    z = t // 2
    xl = t % 2
    sib = c + 1 - 2 * core
    xn = t + 1 - 2 * xl

    def ztp(dz, x):
        return ((z + dz) % 4) * 2 + x

    def remote(src, dst, ssem, rsem, ctx, tp):
        return pltpu.make_async_remote_copy(
            src_ref=src,
            dst_ref=dst,
            send_sem=ssem,
            recv_sem=rsem,
            device_id={"ctx": ctx, "tp": tp},
            device_id_type=MESH,
        )

    def arrived(ref, sem):
        pltpu.make_async_copy(ref, ref, sem).wait()

    load_qkv = pltpu.make_async_copy(qkv_h, qkv_v, loc.at[0])
    load_qkv.start()
    load_res = pltpu.make_async_copy(res_h, resv, loc.at[1])
    load_res.start()

    barrier = pltpu.get_barrier_semaphore()

    def greet(ctx, tp):
        pl.semaphore_signal(barrier, inc=1, device_id={"ctx": ctx, "tp": tp}, device_id_type=MESH)

    for d in range(1, 16):
        greet((c + d) % 16, t)
    greet(c, xn)
    greet((c + 8) % 16, xn)
    greet(c, ztp(1, xl))
    greet(c, ztp(3, xl))
    pl.semaphore_wait(barrier, 19)

    tail_copy = remote(qkv_h.at[:, :, 248:256, :], xtail, hs.at[0], hr.at[0], (c + 1) % 16, t)
    tail_copy.start()

    holder = (y + xl) % 2 == 0
    relay = (y + xl) % 2 == 1
    ups = ((y + 1) % 4, (y + 3) % 4)
    late_h = ((z + 2) % 4 // 2 + xh) % 2
    odd = z % 2

    def place_of(k, row):
        turn_h = (0, late_h, 1, 1 - late_h)[k]
        turn_l = (0, 1, 1 - late_h, late_h)[k]
        return (xl + turn_l) % 2 * 4 + (xh + turn_h) % 2 * 2 + row // 2

    def ctx_of(h, row):
        return (h * 4 + row) * 2 + core

    def weight_first(stage, source):
        mine = place_of(0, y)
        target = w.at[stage, mine, core]
        arrival = wrecv.at[stage, mine, core]
        home = pltpu.make_async_copy(source, target, arrival)
        along = [
            remote(source, target, wsnd.at[stage, 0], arrival, ctx_of(xh, ups[0]), t),
            remote(source, target, wsnd.at[stage, 1], arrival, ctx_of(xh, ups[1]), t),
            remote(source, target, wsnd.at[stage, 2], arrival, ctx_of(1 - xh, y), t),
        ]
        across = [
            remote(source, target, wsnd.at[stage, 0], arrival, c, xn),
            remote(source, target, wsnd.at[stage, 1], arrival, ctx_of(1 - xh, y), xn),
        ]
        return home, along, across

    def weight_start(stage, source):
        home, along, across = weight_first(stage, source)

        @pl.when(holder)
        def _():
            home.start()
            for copy in along:
                copy.start()

        @pl.when(relay)
        def _():
            for copy in across:
                copy.start()

    def weight_pass(stage, index, sem, ctx):
        block = w.at[stage, index, core]
        return remote(block, block, sem, wrecv.at[stage, index, core], ctx, t)

    def weight_pass_half(stage, index, half, sem, ctx):
        block = w.at[stage, index, core, 256 * half : 256 * (half + 1), :]
        return remote(block, block, sem, wrecv.at[stage, index, core], ctx, t)

    def weight_got(stage, index):
        arrived(w.at[stage, index, core], wrecv.at[stage, index, core])

    def weight_moves(stage, k):
        here, up, down, far = place_of(k, y), place_of(k, ups[0]), place_of(k, ups[1]), place_of(k, (y + 2) % 4)

        def sibling(index, n):
            return weight_pass(stage, index, bsnd.at[stage, n], sib)

        held = [sibling(here, k)]
        if k:
            held += [weight_pass(stage, here, fsnd.at[stage, n, k], ctx_of(xh, ups[n])) for n in range(2)]
        late = [sibling(far, 4 + k)]
        below = [sibling(down, k), weight_pass_half(stage, down, 0, fsnd.at[stage, 0, k], ctx_of(xh, ups[0]))]
        above = [sibling(up, 4 + k), weight_pass_half(stage, up, 1, fsnd.at[stage, 1, k], ctx_of(xh, ups[1]))]
        return (here, held), (far, late), (down, below), (up, above)

    def weight_hold(stage, *ks):
        @pl.when(holder)
        def _():
            for k in ks:
                first_ = weight_moves(stage, k)[0]
                weight_got(stage, first_[0])
                for copy in reversed(first_[1]):
                    copy.start()

    def weight_relay(stage, k):
        _, _, below, above = weight_moves(stage, k)

        @pl.when(relay)
        def _():
            for index, copies in (below, above):
                weight_got(stage, index)
                for copy in reversed(copies):
                    copy.start()

    def weight_late(stage, *ks):
        @pl.when(holder)
        def _():
            for k in ks:
                _, (index, copies), _, _ = weight_moves(stage, k)
                weight_got(stage, index)
                copies[0].start()

    def weight_sibling(stage, index):
        arrived(w.at[stage, index, 1 - core], wrecv.at[stage, index, 1 - core])

    def weight_drain(stage, source):
        _, along, across = weight_first(stage, source)

        @pl.when(holder)
        def _():
            for copy in along:
                copy.wait_send()
            for k in range(4):
                first_, late, _, _ = weight_moves(stage, k)
                for copy in first_[1] + late[1]:
                    copy.wait_send()

        @pl.when(relay)
        def _():
            for copy in across:
                copy.wait_send()
            for k in range(4):
                _, _, below, above = weight_moves(stage, k)
                for copy in below[1] + above[1]:
                    copy.wait_send()

    weight_start(0, wo1_h)
    load_win = pltpu.make_async_copy(win_h, win, loc.at[2])

    seg = lax.broadcasted_iota(jnp.int32, (SEGS, WIDTH), 0)
    seg1 = lax.broadcasted_iota(jnp.int32, (SEGS, LANES), 0)
    first = seg % 4 == 0
    live = jnp.where(c > 0, 1.0, 0.0).astype(F32)

    def rows(j, count=1):
        start = j * SEGS
        return pl.ds(start if isinstance(start, int) else pl.multiple_of(start, SEGS), count * SEGS)

    def lanes(lt):
        return pl.ds(pl.multiple_of(lt * LANES, LANES), LANES)

    @pl.loop(0, TAPS // 8)
    def _(i):
        taps = filt[pl.ds(pl.multiple_of(i * 8, 8), 8), :].astype(F32)
        for k in range(8):
            fb[pl.ds(pl.multiple_of((i * 8 + k) * 16, 16), 16), :] = jnp.broadcast_to(
                taps[k : k + 1, :], (16, WIDTH)
            ).astype(BF16)

    load_qkv.wait()
    for s in range(2):
        for p in range(3):

            @pl.loop(0, 16)
            def _(i, s=s, p=p):
                here = pl.ds(pl.multiple_of(i * 16, 16), 16)
                there = pl.ds(pl.multiple_of(s * 256 + i * 16, 16), 16)
                values = qkv_v[s, p, here, :].astype(F32)
                for k in range(WIDTH // LANES):
                    x32[p, k, there, :] = values[:, LANES * k : LANES * (k + 1)]

    def tap(ref, lag, p):
        return jnp.broadcast_to(ref[lag, p : p + 1, :], (SEGS, WIDTH))

    def strided3(p, j):
        return jnp.concatenate(
            [x32[p, k, pl.ds(j, SEGS, stride=STEPS), :] for k in range(WIDTH // LANES)], axis=1
        )

    def medium(j, now, before, before2):
        mixed = [tap(sw1, 0, p) * now[p] + tap(sw1, 1, p) * before[p] + tap(sw1, 2, p) * before2[p] for p in range(3)]
        q32[rows(j), :] = mixed[0]
        uext[rows(j + 128), :] = (mixed[1] * mixed[2]).astype(BF16).astype(F32)

    last = [strided3(p, 63) for p in range(3)]
    last2 = [strided3(p, 62) for p in range(3)]
    x0 = [strided3(p, 0) for p in range(3)]
    x1 = [strided3(p, 1) for p in range(3)]
    own1 = [jnp.where(first, 0.0, pltpu.roll(v, 1, 0)) for v in last]
    own2 = [jnp.where(first, 0.0, pltpu.roll(v, 1, 0)) for v in last2]
    medium(0, x0, own1, own2)
    medium(1, x1, x0, own1)

    def medium_step(j, carried):
        now = [strided3(p, j) for p in range(3)]
        before, before2 = carried
        medium(j, now, before, before2)
        return now, before

    lax.fori_loop(2, STEPS, medium_step, (x1, x0))

    @pl.loop(0, STEPS // 4)
    def _(i):
        packed = []
        for k in range(2):
            even = uext[rows(128 + 4 * i + 2 * k), :]
            odd = uext[rows(129 + 4 * i + 2 * k), :]
            packed.append(jnp.where(seg % 4 >= 2, even, pltpu.roll(odd, 6, 0)))
        pk_s[pl.ds(pl.multiple_of(i * 16, 16), 16), :] = jnp.concatenate(packed, axis=0).astype(BF16)

    u_copy = remote(pk_s, pk_r, hs.at[1], hr.at[1], (c + 1) % 16, t)
    u_copy.start()
    weight_hold(0, 0, 1)
    weight_relay(0, 0)

    arrived(xtail, hr.at[0])

    def halo(p, row):
        top = xtail[0, p].astype(F32)[row : row + 1, :] * live
        bottom = xtail[1, p].astype(F32)[row : row + 1, :] * live
        return jnp.where(seg < 4, jnp.broadcast_to(top, (SEGS, WIDTH)), jnp.broadcast_to(bottom, (SEGS, WIDTH)))

    full1 = [jnp.where(first, halo(p, 7), own1[p]) for p in range(3)]
    full2 = [jnp.where(first, halo(p, 6), own2[p]) for p in range(3)]
    medium(0, x0, full1, full2)
    medium(1, x1, x0, full1)

    load_win.start()
    arrived(pk_r, hr.at[1])

    @pl.loop(0, STEPS // 2)
    def _(i):
        both = pk_r[pl.ds(pl.multiple_of((i // 2) * 16, 16), 16), :].astype(F32) * live
        got = jnp.where(i % 2 == 0, both[:SEGS], both[SEGS:])
        even = uext[rows(128 + 2 * i), :]
        odd = uext[rows(129 + 2 * i), :]
        uext[rows(64 + 2 * i), :] = jnp.where(first, pltpu.roll(got, 5, 0), pltpu.roll(even, 1, 0))
        uext[rows(65 + 2 * i), :] = jnp.where(first, pltpu.roll(got, 7, 0), pltpu.roll(odd, 1, 0))
        uext[rows(2 * i), :] = jnp.where(seg % 4 < 2, pltpu.roll(got, 6, 0), pltpu.roll(even, 2, 0))
        uext[rows(1 + 2 * i), :] = jnp.where(seg % 4 < 2, got, pltpu.roll(odd, 2, 0))


    HALF = ROWS // 2

    def z_copy(stage, part):
        return remote(zo.at[stage, part], zn.at[stage, part], zs.at[stage, part], zr.at[stage, part], c, xn)

    def p_copy(stage, part, i):
        return remote(
            ps.at[stage, part, i],
            pr.at[stage, part, i],
            pss.at[stage, part, i],
            prs.at[stage, part, i],
            c,
            ztp(1 + 2 * (i % 2), xl),
        )

    def term(stage, part, d, half):
        dest = (z + d) % 4
        both = jnp.concatenate([zo[stage, part], zn[stage, part]], axis=1)
        weights = jnp.concatenate([w[stage, xl * 4 + dest, half], w[stage, (1 - xl) * 4 + dest, half]], axis=0)
        return jnp.dot(both, weights, preferred_element_type=F32)

    early = ((0, 2, 0), (1, 2, 1), (3 - odd, 3 - 2 * odd, odd))
    later = ((2 + odd, 1 + 2 * odd, 1 - odd),)
    passed = ((5 - odd, 3 - 2 * odd, 1 - odd), (4 + odd, 1 + 2 * odd, odd))

    def project_direct(stage, part, pieces):
        for i, d, half in pieces:
            ps[stage, part, i] = term(stage, part, d, half).astype(BF16)
            p_copy(stage, part, i).start()

    def project_relay(stage, part, pieces):
        for i, d, half in pieces:
            mine = term(stage, part, d, half)
            arrived(pr.at[stage, part, i - 4], prs.at[stage, part, i - 4])
            ps[stage, part, i] = (mine + pr[stage, part, i - 4].astype(F32)).astype(BF16)
            p_copy(stage, part, i).start()

    def project_own(stage, part):
        for own in range(2):
            pacc[HALF * part : HALF * (part + 1), 256 * own : 256 * (own + 1)] = term(stage, part, 0, own)

    def project_weights(stage, *offsets):
        for d in offsets:
            for source in range(2):
                weight_sibling(stage, source * 4 + (z + d) % 4)

    def project_end(stage):
        project_relay(stage, 0, passed)
        project_own(stage, 0)
        project_relay(stage, 1, passed)
        project_own(stage, 1)

    def project_wait(stage, part):
        for i in (2, 3, 4, 5):
            arrived(pr.at[stage, part, i], prs.at[stage, part, i])

    def project_drain(stage):
        for part in range(2):
            z_copy(stage, part).wait_send()
            for i in range(6):
                p_copy(stage, part, i).wait_send()

    def arrivals(stage, part, i):
        here = pl.ds(pl.multiple_of(i * 16, 16), 16)
        left = pr[stage, part, 3, here, :].astype(F32) + pr[stage, part, 4, here, :].astype(F32)
        right = pr[stage, part, 2, here, :].astype(F32) + pr[stage, part, 5, here, :].astype(F32)
        own = pacc[pl.ds(pl.multiple_of(part * HALF + i * 16, 16), 16), :]
        return own + jnp.concatenate([left, right], axis=1)

    def filter_blocks(first_block):
        @pl.loop(first_block, first_block + 2)
        def _(block):
            lane = lanes((block % 8) // 2)
            part = block // 8
            r0 = (block % 2) * 16
            j0 = part * 32 + r0

            def taps8(ib, totals):
                base = 64 + j0 // 2 - 4 * ib - 3
                window = pl.ds(pl.multiple_of(base * 16, 16), 11 * 16)
                even, odd_ = ueven[window, lane], uodd[window, lane]
                taps = fb[pl.ds(pl.multiple_of(ib * 128, 128), 128), lane]
                totals = list(totals)
                for a in range(8):
                    terms = []
                    for b in range(8):
                        k = 3 - b // 2 + a
                        u = (odd_ if b % 2 else even)[k * 16 : (k + 1) * 16]
                        terms.append(taps[b * 16 : (b + 1) * 16] * u)
                    while len(terms) > 1:
                        terms = [terms[n] + terms[n + 1] for n in range(0, len(terms), 2)]
                    totals[a] = totals[a] + terms[0].astype(F32)
                return tuple(totals)

            totals = lax.fori_loop(0, 16, taps8, tuple(jnp.zeros((16, LANES), F32) for _ in range(8)))
            skip = jnp.broadcast_to(skip1[:, lane], (16, LANES))
            for a in range(8):
                u = uext[rows(128 + j0 + 2 * a, 2), lane]
                value = q32[rows(j0 + 2 * a, 2), lane] * (totals[a] + skip * u)
                zo[0, part, pl.ds(pl.multiple_of((r0 + 2 * a) * SEGS, 16), 16), lane] = value.astype(BF16)

    def pairs(first_pair, last_pair):
        @pl.loop(first_pair, last_pair)
        def _(i):
            here = pl.ds(pl.multiple_of(i * 16, 16), 16)
            ueven[here, :] = uext[rows(2 * i, 2), :].astype(BF16)
            uodd[here, :] = uext[rows(2 * i - 1, 2), :].astype(BF16)

    pairs(1, 96)
    for first_block in range(0, 8, 2):
        filter_blocks(first_block)
    z_copy(0, 0).start()
    weight_hold(0, 2, 3)
    filter_blocks(8)
    filter_blocks(10)
    weight_relay(0, 1)
    filter_blocks(12)
    filter_blocks(14)
    z_copy(0, 1).start()
    weight_late(0, 0)

    load_res.wait()

    @pl.loop(0, 32)
    def _(i):
        s = i // 16
        r = (i % 16) * 16
        values = resv[s, pl.ds(pl.multiple_of(r, 16), 16), :].astype(F32)
        for k in range(WIDTH // LANES):
            x32[0, k, pl.ds(pl.multiple_of(i * 16, 16), 16), :] = values[:, LANES * k : LANES * (k + 1)]

    @pl.loop(0, STEPS)
    def _(j):
        for k in range(WIDTH // LANES):
            x32[1, k, rows(j), :] = x32[0, k, pl.ds(j, SEGS, stride=STEPS), :]

    weight_relay(0, 2)
    weight_late(0, 1, 2)
    project_weights(0, 2, 3 - 2 * odd)
    arrived(zn.at[0, 0], zr.at[0, 0])
    project_direct(0, 0, early)
    weight_relay(0, 3)
    arrived(zn.at[0, 1], zr.at[0, 1])
    project_direct(0, 1, early)
    weight_late(0, 3)
    weight_start(1, wo2_h)
    project_weights(0, 1 + 2 * odd, 0)
    project_direct(0, 0, later)
    project_direct(0, 1, later)
    project_end(0)
    weight_hold(1, 0, 1, 2)
    weight_relay(1, 0)

    sent = []

    def send(slot, quarter, tp):
        k = len(sent)
        copy = remote(
            mid.at[slot, quarter], mid.at[slot, quarter], ags.at[k], agr.at[slot, quarter], c, tp
        )
        copy.start()
        sent.append(copy)

    zp, zm, zz = ztp(1, xl), ztp(3, xl), ztp(2, xl)
    xp, xm, xz = ztp(1, 1 - xl), ztp(3, 1 - xl), ztp(2, 1 - xl)
    for part in range(2):
        project_wait(0, part)

        @pl.loop(0, 16)
        def _(i, part=part):
            here = pl.ds(pl.multiple_of(part * HALF + i * 16, 16), 16)
            before = jnp.concatenate([x32[1, k, here, :] for k in range(WIDTH // LANES)], axis=1)
            value = (before + arrivals(0, part, i)).astype(BF16)
            mid[t, part * 2 + i // 8, pl.ds(pl.multiple_of((i % 8) * 16, 16), 16), :] = value

        for quarter in (2 * part, 2 * part + 1):
            send(t, quarter, xn)
            send(t, quarter, zp)
            send(t, quarter, zm)

    def have(slot, *quarters):
        for quarter in quarters:
            arrived(mid.at[slot, quarter], agr.at[slot, quarter])

    load_win.wait()

    def absorb(*slots, fresh=False):
        count = len(slots)
        scales = [gain[:, pl.ds(pl.multiple_of(slot * WIDTH, WIDTH), WIDTH)] for slot in slots]

        @pl.loop(0, 16)
        def _(i):
            here = pl.ds(pl.multiple_of((i % 4) * 32, 32), 32)
            there = pl.ds(pl.multiple_of(i * 32, 32), 32)
            total = 0.0 if fresh else ssq[there, :]
            for k, slot in enumerate(slots):
                values = mid[slot, i // 4, here, :].astype(F32)
                square = values * values
                total += square[:, 0:128] + square[:, 128:256] + square[:, 256:384] + square[:, 384:512]
                scaled[there, WIDTH * k : WIDTH * (k + 1)] = (values * scales[k]).astype(BF16)
            ssq[there, :] = total

        @pl.loop(0, 6)
        def _(i):
            cols = pl.ds(pl.multiple_of((i % 2) * 256, 256), 256)
            weights = [win[i // 2, pl.ds(pl.multiple_of(slot * WIDTH, WIDTH), WIDTH), cols] for slot in slots]
            product = jnp.dot(
                scaled[:, 0 : WIDTH * count], jnp.concatenate(weights, axis=0), preferred_element_type=F32
            )
            acc[i // 2, :, cols] = product if fresh else acc[i // 2, :, cols] + product

    absorb(t, fresh=True)
    weight_hold(1, 3)
    weight_relay(1, 1)
    have(xn, 0, 1)
    for quarter in range(2):
        send(xn, quarter, zp)
        send(xn, quarter, zm)
    have(zm, 0, 1, 2, 3)
    send(zm, 0, zp)
    send(zm, 2, zp)
    send(zm, 2, xn)
    send(zm, 3, xn)
    have(zp, 0, 1, 2, 3)
    send(zp, 1, zm)
    send(zp, 3, zm)
    send(zp, 2, xn)
    send(zp, 3, xn)
    absorb(zm, zp)
    weight_relay(1, 2)
    have(xm, 0, 1)
    send(xm, 0, zp)
    have(xp, 0, 1)
    send(xp, 1, zm)
    have(zz, 0, 1, 2, 3)
    send(zz, 2, xn)
    send(zz, 3, xn)
    have(xn, 2, 3)
    absorb(xn, zz)
    weight_relay(1, 3)
    have(xm, 2, 3)
    have(xp, 2, 3)
    absorb(xm, xp)
    have(xz, 0, 1, 2, 3)
    absorb(xz)
    weight_late(1, 0, 1, 2, 3)

    def finish(i):
        here = pl.ds(i * 16 if isinstance(i, int) else pl.multiple_of(i * 16, 16), 16)
        meansq = jnp.sum(ssq[here, :], axis=1, keepdims=True) * (1.0 / 4096.0)
        factor = lax.rsqrt(meansq + 1e-6)
        values = [(acc[p, here, :] * factor).astype(BF16) for p in range(3)]
        for p in range(3):
            acc[p, here, :] = values[p].astype(F32)
        return values

    tails = finish(31)
    for p in range(3):
        ltail_s[p] = tails[p]
    l_copy = remote(ltail_s, ltail, hs.at[2], hr.at[2], (c + 1) % 16, t)
    l_copy.start()

    @pl.loop(0, 31)
    def _(i):
        finish(i)

    def longer(j, now, before, before2):
        mixed = [tap(sw2, 0, p) * now[p] + tap(sw2, 1, p) * before[p] + tap(sw2, 2, p) * before2[p] for p in range(3)]
        q32[rows(j), :] = mixed[0]
        uext[rows(j), :] = mixed[1] * mixed[2]

    @pl.loop(2, STEPS)
    def _(j):
        longer(
            j,
            [acc[p, rows(j), :] for p in range(3)],
            [acc[p, rows(j - 1), :] for p in range(3)],
            [acc[p, rows(j - 2), :] for p in range(3)],
        )

    arrived(ltail, hr.at[2])
    edge1, edge2 = [], []
    for p in range(3):
        got = ltail[p].astype(F32) * live
        edge2.append(jnp.where(first, pltpu.roll(got[:SEGS], 5, 0), pltpu.roll(acc[p, rows(62), :], 1, 0)))
        edge1.append(jnp.where(first, pltpu.roll(got[SEGS:], 5, 0), pltpu.roll(acc[p, rows(63), :], 1, 0)))
    y0 = [acc[p, rows(0), :] for p in range(3)]
    y1 = [acc[p, rows(1), :] for p in range(3)]
    longer(0, y0, edge1, edge2)
    longer(1, y1, y0, edge1)

    def row_of(ref, n, lane):
        return jnp.broadcast_to(ref[n : n + 1, lane], (SEGS, LANES))

    @pl.loop(0, WIDTH // LANES)
    def _(lt):
        lane = lanes(lt)
        decay = [jnp.exp(-row_of(rate, n, lane)) for n in range(POLES)]

        def step(i, states):
            for k in range(4):
                u = uext[rows(4 * i + k), lane]
                states = [decay[n] * states[n] + u for n in range(POLES)]
            return tuple(states)

        states = lax.fori_loop(0, STEPS // 4, step, tuple(jnp.zeros((SEGS, LANES), F32) for _ in range(POLES)))
        for n in range(POLES):
            est[rows(n), lane] = states[n]
            decays[rows(n), lane] = decay[n]

    place = seg1 % 4

    @pl.loop(0, WIDTH // LANES)
    def _(lt):
        lane = lanes(lt)
        for g in range(2):
            packed = []
            for h in range(2):
                total = jnp.zeros((SEGS, LANES), F32)
                for r in range(4):
                    n = g * 8 + h * 4 + r
                    span = jnp.exp(-float(STEPS) * row_of(rate, n, lane))
                    value = est[rows(n), lane]
                    value = value + span * jnp.where(place >= 1, pltpu.roll(value, 1, 0), 0.0)
                    value = value + span * span * jnp.where(place >= 2, pltpu.roll(value, 2, 0), 0.0)
                    est[rows(n), lane] = jnp.where(place >= 1, pltpu.roll(value, 1, 0), 0.0)
                    end = value if r == 3 else pltpu.roll(value, (r - 3) % 8, 0)
                    total = jnp.where(place == r, end, total)
                packed.append(total)
            st_s[pl.ds(g * 16, 16), lane] = jnp.concatenate(packed, axis=0).astype(BF16)

    def state_copy(d):
        return remote(st_s, st_r.at[d - 1], sts.at[d - 1], strv.at[d - 1], c + d, t)

    for d in range(15, 0, -1):

        @pl.when(c + d < 16)
        def _(d=d):
            state_copy(d).start()

    @pl.loop(0, WIDTH // LANES)
    def _(lt):
        lane = lanes(lt)
        for n in range(POLES):
            weights[rows(n), lane] = row_of(resid, n, lane) * jnp.sqrt(1.0 - jnp.exp(-2.0 * row_of(rate, n, lane)))

    packs = []
    for g in range(4):
        total = jnp.zeros((SEGS, WIDTH), F32)
        for r in range(4):
            n = g * 4 + r
            total = jnp.where(seg % 4 == r, jnp.broadcast_to(rate[n : n + 1, :], (SEGS, WIDTH)), total)
        packs.append(total)
    pack = jnp.concatenate(packs, axis=0)
    hin[...] = jnp.zeros((4 * SEGS, WIDTH), F32)
    for d in range(1, 16):

        @pl.when(c - d >= 0)
        def _(d=d):
            arrived(st_r.at[d - 1], strv.at[d - 1])
            hin[...] += jnp.exp(pack * (-256.0 * (d - 1))) * st_r[d - 1].astype(F32)

    for part in range(2):

        @pl.loop(0, WIDTH // LANES)
        def _(lt, part=part):
            lane = lanes(lt)
            decay, weight, states = [], [], []
            for n in range(POLES):
                decay.append(decays[rows(n), lane])
                weight.append(weights[rows(n), lane])
                state = est[rows(n), lane]
                if part == 0:
                    r = row_of(rate, n, lane)
                    k = (n // 4) * SEGS + n % 4
                    enter = jnp.where(
                        seg1 < 4,
                        jnp.broadcast_to(hin[k : k + 1, lane], (SEGS, LANES)),
                        jnp.broadcast_to(hin[k + 4 : k + 5, lane], (SEGS, LANES)),
                    )
                    state = state + jnp.exp(r * (place.astype(F32) * (-float(STEPS)))) * enter
                states.append(state)
            skip = jnp.broadcast_to(skip2[:, lane], (SEGS, LANES))

            def step(i, states):
                pair = []
                for k in range(2):
                    j = part * (STEPS // 2) + 2 * i + k
                    u = uext[rows(j), lane]
                    states = [decay[n] * states[n] + u for n in range(POLES)]
                    terms = [weight[n] * states[n] for n in range(POLES)]
                    while len(terms) > 1:
                        terms = [terms[a] + terms[a + 1] for a in range(0, len(terms), 2)]
                    pair.append(q32[rows(j), lane] * (terms[0] + skip * u))
                zo[1, part, pl.ds(pl.multiple_of(i * 16, 16), 16), lane] = jnp.concatenate(pair, axis=0).astype(BF16)
                return tuple(states)

            states = lax.fori_loop(0, STEPS // 4, step, tuple(states))
            if part == 0:
                for n in range(POLES):
                    est[rows(n), lane] = states[n]

        z_copy(1, part).start()

    project_weights(1, 0, 1, 2, 3)
    for part in range(2):
        arrived(zn.at[1, part], zr.at[1, part])
        project_direct(1, part, early + later)
    project_end(1)
    for part in range(2):
        project_wait(1, part)

        @pl.loop(0, 16)
        def _(i, part=part):
            base = mid[t, part * 2 + i // 8, pl.ds(pl.multiple_of((i % 8) * 16, 16), 16), :].astype(F32)
            value = base + arrivals(1, part, i)
            j = part * (STEPS // 2) + 2 * i
            for k in range(WIDTH // LANES):
                piece = value[:, LANES * k : LANES * (k + 1)]
                x32[2, k, pl.ds(j, SEGS, stride=STEPS), :] = piece[:SEGS]
                x32[2, k, pl.ds(j + 1, SEGS, stride=STEPS), :] = piece[SEGS:]

    @pl.loop(0, 32)
    def _(i):
        s = i // 16
        r = (i % 16) * 16
        here = pl.ds(pl.multiple_of(i * 16, 16), 16)
        value = jnp.concatenate([x32[2, k, here, :] for k in range(WIDTH // LANES)], axis=1)
        obf[s, pl.ds(pl.multiple_of(r, 16), 16), :] = value.astype(BF16)

    store = pltpu.make_async_copy(obf, out_h, loc.at[3])
    store.start()

    tail_copy.wait_send()
    u_copy.wait_send()
    l_copy.wait_send()
    weight_drain(0, wo1_h)
    weight_drain(1, wo2_h)
    project_drain(0)
    project_drain(1)
    for copy in sent:
        copy.wait_send()
    for d in range(1, 16):

        @pl.when(c + d < 16)
        def _(d=d):
            state_copy(d).wait_send()

    store.wait()


def local(
    residual_in, mr_qkv, mr_short_w, mr_filter, mr_skip, mr_out_w, lr_gain,
    lr_in_w, lr_short_w, lr_rate, lr_res, lr_skip, lr_out_w,
):
    vmem = pl.BlockSpec(memory_space=pltpu.VMEM)
    hbm = pl.BlockSpec(memory_space=pl.ANY)
    dma = pltpu.SemaphoreType.DMA
    scratch = [
        pltpu.VMEM((2, 3, 256, WIDTH), BF16),
        pltpu.VMEM((2, 3, 8, WIDTH), BF16),
        pltpu.VMEM((3, WIDTH // LANES, ROWS, LANES), F32),
        pltpu.VMEM((ROWS, WIDTH), F32),
        pltpu.VMEM((192 * SEGS, WIDTH), F32),
        pltpu.VMEM((96 * 16, WIDTH), BF16),
        pltpu.VMEM((96 * 16, WIDTH), BF16),
        pltpu.VMEM((TAPS * 16, WIDTH), BF16),
        pltpu.VMEM((256, WIDTH), BF16),
        pltpu.VMEM((256, WIDTH), BF16),
        pltpu.VMEM((2, 2, ROWS // 2, WIDTH), BF16),
        pltpu.VMEM((2, 2, ROWS // 2, WIDTH), BF16),
        pltpu.VMEM((2, 8, 2, WIDTH, 256), BF16),
        pltpu.VMEM((3, 4096, WIDTH), BF16),
        pltpu.VMEM((2, 2, 6, ROWS // 2, 256), BF16),
        pltpu.VMEM((2, 2, 6, ROWS // 2, 256), BF16),
        pltpu.VMEM((ROWS, WIDTH), F32),
        pltpu.VMEM((8, 4, 128, WIDTH), BF16),
        pltpu.VMEM((ROWS, 2 * WIDTH), BF16),
        pltpu.VMEM((3, ROWS, WIDTH), F32),
        pltpu.VMEM((ROWS, LANES), F32),
        pltpu.VMEM((3, 16, WIDTH), BF16),
        pltpu.VMEM((3, 16, WIDTH), BF16),
        pltpu.VMEM((POLES * SEGS, WIDTH), F32),
        pltpu.VMEM((POLES * SEGS, WIDTH), F32),
        pltpu.VMEM((POLES * SEGS, WIDTH), F32),
        pltpu.VMEM((4 * SEGS, WIDTH), BF16),
        pltpu.VMEM((15, 4 * SEGS, WIDTH), BF16),
        pltpu.VMEM((4 * SEGS, WIDTH), F32),
        pltpu.VMEM((2, 256, WIDTH), BF16),
        pltpu.VMEM((2, 256, WIDTH), BF16),
        dma((4,)),
        dma((3,)),
        dma((3,)),
        dma((2, 3)),
        dma((2, 2, 4)),
        dma((2, 8)),
        dma((2, 8, 2)),
        dma((2, 2)),
        dma((2, 2)),
        dma((2, 2, 6)),
        dma((2, 2, 6)),
        dma((32,)),
        dma((8, 4)),
        dma((15,)),
        dma((15,)),
    ]
    return pl.pallas_call(
        kernel,
        out_shape=jax.ShapeDtypeStruct((2, 256, WIDTH), BF16),
        in_specs=[hbm, hbm, vmem, vmem, vmem, hbm, vmem, hbm, vmem, vmem, vmem, vmem, hbm],
        out_specs=hbm,
        scratch_shapes=scratch,
        compiler_params=pltpu.CompilerParams(
            collective_id=0, has_side_effects=True, vmem_limit_bytes=62 * 1024 * 1024
        ),
    )(
        residual_in,
        jnp.transpose(mr_qkv, (0, 2, 1, 3)),
        mr_short_w,
        mr_filter,
        mr_skip.reshape(1, WIDTH),
        mr_out_w,
        lr_gain.reshape(1, 8 * WIDTH),
        jnp.transpose(lr_in_w, (1, 0, 2)),
        lr_short_w,
        lr_rate,
        lr_res,
        lr_skip.reshape(1, WIDTH),
        lr_out_w,
    )


def solution(mesh):
    in_specs = (
        P(None, "ctx", "tp"),
        P(None, "ctx", None, "tp"),
        P(None, None, "tp"),
        P(None, "tp"),
        P("tp"),
        P("tp", "ctx"),
        P(),
        P(None, None, "tp"),
        P(None, None, "tp"),
        P(None, "tp"),
        P(None, "tp"),
        P("tp"),
        P("tp", "ctx"),
    )
    return jax.shard_map(local, mesh=mesh, in_specs=in_specs, out_specs=P(None, "ctx", "tp"), check_vma=False)
```

```python
import jax
import jax.numpy as jnp
from jax import lax
from jax.experimental import pallas as pl
from jax.experimental.pallas import tpu as pltpu
from jax.sharding import PartitionSpec as P

MESH = pl.DeviceIdType.MESH
F32 = jnp.float32
BF16 = jnp.bfloat16

SEGS = 8
STEPS = 64
ROWS = SEGS * STEPS
WIDTH = 512
TAPS = 128
POLES = 16
LANES = 128


def kernel(
    res_h, qkv_h, sw1, filt, skip1, wo1_h, gain, win_h, sw2, rate, resid, skip2, wo2_h,
    out_h,
    qkv_v, xtail, x32, q32, uext, fb, pk_s, pk_r, zo, zn, w, win, ps, pr, pacc, mid, scaled, acc, ssq,
    ltail_s, ltail, est, decays, weights, st_s, st_r, hin, obf, resv,
    loc, hs, hr, wsnd, fsnd, bsnd, wrecv, zs, zr, pss, prs, ags, agr, sts, strv,
):
    c = lax.axis_index("ctx")
    t = lax.axis_index("tp")
    core = c % 2
    m = c // 2
    y = m % 4
    xh = m // 4
    z = t // 2
    xl = t % 2
    sib = c + 1 - 2 * core
    xn = t + 1 - 2 * xl

    def ztp(dz, x):
        return ((z + dz) % 4) * 2 + x

    def remote(src, dst, ssem, rsem, ctx, tp):
        return pltpu.make_async_remote_copy(
            src_ref=src,
            dst_ref=dst,
            send_sem=ssem,
            recv_sem=rsem,
            device_id={"ctx": ctx, "tp": tp},
            device_id_type=MESH,
        )

    def arrived(ref, sem):
        pltpu.make_async_copy(ref, ref, sem).wait()

    load_qkv = pltpu.make_async_copy(qkv_h, qkv_v, loc.at[0])
    load_qkv.start()
    load_res = pltpu.make_async_copy(res_h, resv, loc.at[1])
    load_res.start()

    barrier = pltpu.get_barrier_semaphore()

    def greet(ctx, tp):
        pl.semaphore_signal(barrier, inc=1, device_id={"ctx": ctx, "tp": tp}, device_id_type=MESH)

    for d in range(1, 16):
        greet((c + d) % 16, t)
    greet(c, xn)
    greet((c + 8) % 16, xn)
    greet(c, ztp(1, xl))
    greet(c, ztp(3, xl))
    pl.semaphore_wait(barrier, 19)

    tail_copy = remote(qkv_h.at[:, :, 248:256, :], xtail, hs.at[0], hr.at[0], (c + 1) % 16, t)
    tail_copy.start()

    holder = (y + xl) % 2 == 0
    relay = (y + xl) % 2 == 1
    ups = ((y + 1) % 4, (y + 3) % 4)

    def place_of(k, row):
        xs = (xl, 1 - xl, 1 - xl, xl)[k]
        xhs = (xh, xh, 1 - xh, 1 - xh)[k]
        return xs * 4 + xhs * 2 + row // 2

    def ctx_of(h, row):
        return (h * 4 + row) * 2 + core

    def weight_first(stage, source):
        mine = place_of(0, y)
        target = w.at[stage, mine, core]
        arrival = wrecv.at[stage, mine, core]
        home = pltpu.make_async_copy(source, target, arrival)
        along = [
            remote(source, target, wsnd.at[stage, 0], arrival, ctx_of(xh, ups[0]), t),
            remote(source, target, wsnd.at[stage, 1], arrival, ctx_of(xh, ups[1]), t),
            remote(source, target, wsnd.at[stage, 2], arrival, ctx_of(1 - xh, y), t),
        ]
        across = [
            remote(source, target, wsnd.at[stage, 0], arrival, c, xn),
            remote(source, target, wsnd.at[stage, 1], arrival, ctx_of(1 - xh, y), xn),
        ]
        return home, along, across

    def weight_start(stage, source):
        home, along, across = weight_first(stage, source)

        @pl.when(holder)
        def _():
            home.start()
            for copy in along:
                copy.start()

        @pl.when(relay)
        def _():
            for copy in across:
                copy.start()

    def weight_pass(stage, index, sem, ctx):
        block = w.at[stage, index, core]
        return remote(block, block, sem, wrecv.at[stage, index, core], ctx, t)

    def weight_pass_half(stage, index, half, sem, ctx):
        block = w.at[stage, index, core, 256 * half : 256 * (half + 1), :]
        return remote(block, block, sem, wrecv.at[stage, index, core], ctx, t)

    def weight_got(stage, index):
        arrived(w.at[stage, index, core], wrecv.at[stage, index, core])

    def weight_moves(stage, k):
        here, up, down, far = place_of(k, y), place_of(k, ups[0]), place_of(k, ups[1]), place_of(k, (y + 2) % 4)

        def sibling(index, n):
            return weight_pass(stage, index, bsnd.at[stage, n], sib)

        held = [sibling(here, k)]
        if k:
            held += [weight_pass(stage, here, fsnd.at[stage, n, k], ctx_of(xh, ups[n])) for n in range(2)]
        late = [sibling(far, 4 + k)]
        below = [sibling(down, k), weight_pass_half(stage, down, 0, fsnd.at[stage, 0, k], ctx_of(xh, ups[0]))]
        above = [sibling(up, 4 + k), weight_pass_half(stage, up, 1, fsnd.at[stage, 1, k], ctx_of(xh, ups[1]))]
        return (here, held), (far, late), (down, below), (up, above)

    def weight_hold(stage, *ks):
        @pl.when(holder)
        def _():
            for k in ks:
                first_ = weight_moves(stage, k)[0]
                weight_got(stage, first_[0])
                for copy in reversed(first_[1]):
                    copy.start()

    def weight_relay(stage, k):
        _, _, below, above = weight_moves(stage, k)

        @pl.when(relay)
        def _():
            for index, copies in (below, above):
                weight_got(stage, index)
                for copy in reversed(copies):
                    copy.start()

    def weight_late(stage, *ks):
        @pl.when(holder)
        def _():
            for k in ks:
                _, (index, copies), _, _ = weight_moves(stage, k)
                weight_got(stage, index)
                copies[0].start()

    def weight_sibling(stage, index):
        arrived(w.at[stage, index, 1 - core], wrecv.at[stage, index, 1 - core])

    def weight_drain(stage, source):
        _, along, across = weight_first(stage, source)

        @pl.when(holder)
        def _():
            for copy in along:
                copy.wait_send()
            for k in range(4):
                first_, late, _, _ = weight_moves(stage, k)
                for copy in first_[1] + late[1]:
                    copy.wait_send()

        @pl.when(relay)
        def _():
            for copy in across:
                copy.wait_send()
            for k in range(4):
                _, _, below, above = weight_moves(stage, k)
                for copy in below[1] + above[1]:
                    copy.wait_send()

    weight_start(0, wo1_h)
    load_win = pltpu.make_async_copy(win_h, win, loc.at[2])

    seg = lax.broadcasted_iota(jnp.int32, (SEGS, WIDTH), 0)
    seg1 = lax.broadcasted_iota(jnp.int32, (SEGS, LANES), 0)
    first = seg % 4 == 0
    live = jnp.where(c > 0, 1.0, 0.0).astype(F32)

    def rows(j, count=1):
        start = j * SEGS
        return pl.ds(start if isinstance(start, int) else pl.multiple_of(start, SEGS), count * SEGS)

    def lanes(lt):
        return pl.ds(pl.multiple_of(lt * LANES, LANES), LANES)

    @pl.loop(0, TAPS // 8)
    def _(i):
        taps = filt[pl.ds(pl.multiple_of(i * 8, 8), 8), :].astype(F32)
        for k in range(8):
            fb[rows(i * 8 + k), :] = jnp.broadcast_to(taps[k : k + 1, :], (SEGS, WIDTH))

    load_qkv.wait()
    for s in range(2):
        for p in range(3):

            @pl.loop(0, 16)
            def _(i, s=s, p=p):
                here = pl.ds(pl.multiple_of(i * 16, 16), 16)
                there = pl.ds(pl.multiple_of(s * 256 + i * 16, 16), 16)
                values = qkv_v[s, p, here, :].astype(F32)
                for k in range(WIDTH // LANES):
                    x32[p, k, there, :] = values[:, LANES * k : LANES * (k + 1)]

    def tap(ref, lag, p):
        return jnp.broadcast_to(ref[lag, p : p + 1, :], (SEGS, WIDTH))

    def strided3(p, j):
        return jnp.concatenate(
            [x32[p, k, pl.ds(j, SEGS, stride=STEPS), :] for k in range(WIDTH // LANES)], axis=1
        )

    def medium(j, now, before, before2):
        mixed = [tap(sw1, 0, p) * now[p] + tap(sw1, 1, p) * before[p] + tap(sw1, 2, p) * before2[p] for p in range(3)]
        q32[rows(j), :] = mixed[0]
        uext[rows(j + 128), :] = (mixed[1] * mixed[2]).astype(BF16).astype(F32)

    last = [strided3(p, 63) for p in range(3)]
    last2 = [strided3(p, 62) for p in range(3)]
    x0 = [strided3(p, 0) for p in range(3)]
    x1 = [strided3(p, 1) for p in range(3)]
    own1 = [jnp.where(first, 0.0, pltpu.roll(v, 1, 0)) for v in last]
    own2 = [jnp.where(first, 0.0, pltpu.roll(v, 1, 0)) for v in last2]
    medium(0, x0, own1, own2)
    medium(1, x1, x0, own1)

    def medium_step(j, carried):
        now = [strided3(p, j) for p in range(3)]
        before, before2 = carried
        medium(j, now, before, before2)
        return now, before

    lax.fori_loop(2, STEPS, medium_step, (x1, x0))

    @pl.loop(0, STEPS // 4)
    def _(i):
        packed = []
        for k in range(2):
            even = uext[rows(128 + 4 * i + 2 * k), :]
            odd = uext[rows(129 + 4 * i + 2 * k), :]
            packed.append(jnp.where(seg % 4 >= 2, even, pltpu.roll(odd, 6, 0)))
        pk_s[pl.ds(pl.multiple_of(i * 16, 16), 16), :] = jnp.concatenate(packed, axis=0).astype(BF16)

    u_copy = remote(pk_s, pk_r, hs.at[1], hr.at[1], (c + 1) % 16, t)
    u_copy.start()
    weight_hold(0, 0, 1, 2)
    weight_relay(0, 0)

    arrived(xtail, hr.at[0])

    def halo(p, row):
        top = xtail[0, p].astype(F32)[row : row + 1, :] * live
        bottom = xtail[1, p].astype(F32)[row : row + 1, :] * live
        return jnp.where(seg < 4, jnp.broadcast_to(top, (SEGS, WIDTH)), jnp.broadcast_to(bottom, (SEGS, WIDTH)))

    full1 = [jnp.where(first, halo(p, 7), own1[p]) for p in range(3)]
    full2 = [jnp.where(first, halo(p, 6), own2[p]) for p in range(3)]
    medium(0, x0, full1, full2)
    medium(1, x1, x0, full1)

    load_win.start()
    arrived(pk_r, hr.at[1])

    @pl.loop(0, STEPS // 2)
    def _(i):
        both = pk_r[pl.ds(pl.multiple_of((i // 2) * 16, 16), 16), :].astype(F32) * live
        got = jnp.where(i % 2 == 0, both[:SEGS], both[SEGS:])
        even = uext[rows(128 + 2 * i), :]
        odd = uext[rows(129 + 2 * i), :]
        uext[rows(64 + 2 * i), :] = jnp.where(first, pltpu.roll(got, 5, 0), pltpu.roll(even, 1, 0))
        uext[rows(65 + 2 * i), :] = jnp.where(first, pltpu.roll(got, 7, 0), pltpu.roll(odd, 1, 0))
        uext[rows(2 * i), :] = jnp.where(seg % 4 < 2, pltpu.roll(got, 6, 0), pltpu.roll(even, 2, 0))
        uext[rows(1 + 2 * i), :] = jnp.where(seg % 4 < 2, got, pltpu.roll(odd, 2, 0))


    HALF = ROWS // 2

    def z_copy(stage, part):
        return remote(zo.at[stage, part], zn.at[stage, part], zs.at[stage, part], zr.at[stage, part], c, xn)

    def p_copy(stage, part, i):
        return remote(
            ps.at[stage, part, i],
            pr.at[stage, part, i],
            pss.at[stage, part, i],
            prs.at[stage, part, i],
            c,
            ztp(1 if i % 2 == 0 else 3, xl),
        )

    def term(stage, part, d, half):
        dest = (z + d) % 4
        both = jnp.concatenate([zo[stage, part], zn[stage, part]], axis=1)
        weights = jnp.concatenate([w[stage, xl * 4 + dest, half], w[stage, (1 - xl) * 4 + dest, half]], axis=0)
        return jnp.dot(both, weights, preferred_element_type=F32)

    def project_first(stage, part):
        arrived(zn.at[stage, part], zr.at[stage, part])
        for i, d, half in ((0, 2, 0), (1, 2, 1), (2, 1, 1), (3, 3, 0)):
            if part == 0 and i in (0, 2, 3):
                for source in range(2):
                    weight_sibling(stage, source * 4 + (z + d) % 4)
            ps[stage, part, i] = term(stage, part, d, half).astype(BF16)
            p_copy(stage, part, i).start()

    def project_own(stage, part):
        if part == 0:
            for source in range(2):
                weight_sibling(stage, source * 4 + z)
        for own in range(2):
            pacc[HALF * part : HALF * (part + 1), 256 * own : 256 * (own + 1)] = term(stage, part, 0, own)

    def project_relay(stage, part):
        for i, d, half in ((4, 1, 0), (5, 3, 1)):
            mine = term(stage, part, d, half)
            arrived(pr.at[stage, part, i - 4], prs.at[stage, part, i - 4])
            ps[stage, part, i] = (mine + pr[stage, part, i - 4].astype(F32)).astype(BF16)
            p_copy(stage, part, i).start()

    def project(stage):
        project_first(stage, 0)
        project_first(stage, 1)
        project_relay(stage, 0)
        project_own(stage, 0)
        project_relay(stage, 1)
        project_own(stage, 1)

    def project_wait(stage, part):
        for i in (2, 3, 4, 5):
            arrived(pr.at[stage, part, i], prs.at[stage, part, i])

    def project_drain(stage):
        for part in range(2):
            z_copy(stage, part).wait_send()
            for i in range(6):
                p_copy(stage, part, i).wait_send()

    def arrivals(stage, part, i):
        here = pl.ds(pl.multiple_of(i * 16, 16), 16)
        left = pr[stage, part, 3, here, :].astype(F32) + pr[stage, part, 4, here, :].astype(F32)
        right = pr[stage, part, 2, here, :].astype(F32) + pr[stage, part, 5, here, :].astype(F32)
        own = pacc[pl.ds(pl.multiple_of(part * HALF + i * 16, 16), 16), :]
        return own + jnp.concatenate([left, right], axis=1)

    def filter_blocks(first_block):
        @pl.loop(first_block, first_block + 2)
        def _(block):
            lane = lanes((block % 8) // 2)
            part = block // 8
            r0 = (block % 2) * 16
            j0 = part * 32 + r0

            def taps8(ib, totals):
                base = 128 + j0 - 8 * ib - 7
                window = uext[pl.ds(pl.multiple_of(base * SEGS, SEGS), 23 * SEGS), lane]
                weights = fb[pl.ds(pl.multiple_of(ib * 64, 64), 64), lane]
                totals = list(totals)
                for b in range(8):
                    f = weights[b * SEGS : (b + 1) * SEGS]
                    for a in range(16):
                        k = a + 7 - b
                        totals[a] = totals[a] + f * window[k * SEGS : (k + 1) * SEGS]
                return tuple(totals)

            totals = lax.fori_loop(0, 16, taps8, tuple(jnp.zeros((SEGS, LANES), F32) for _ in range(16)))
            skip = jnp.broadcast_to(skip1[:, lane], (SEGS, LANES))
            for a in range(0, 16, 2):
                pair = []
                for k in (a, a + 1):
                    u = uext[rows(128 + j0 + k), lane]
                    pair.append(q32[rows(j0 + k), lane] * (totals[k] + skip * u))
                zo[0, part, pl.ds(pl.multiple_of((r0 + a) * SEGS, 16), 16), lane] = jnp.concatenate(
                    pair, axis=0
                ).astype(BF16)

    filter_blocks(0)
    filter_blocks(2)
    weight_hold(0, 3)
    weight_relay(0, 1)
    filter_blocks(4)
    filter_blocks(6)
    z_copy(0, 0).start()
    weight_late(0, 0)
    filter_blocks(8)
    weight_relay(0, 2)
    weight_late(0, 1)
    filter_blocks(10)
    filter_blocks(12)
    weight_relay(0, 3)
    weight_late(0, 2)
    filter_blocks(14)
    z_copy(0, 1).start()
    weight_late(0, 3)
    weight_start(1, wo2_h)

    load_res.wait()

    @pl.loop(0, 32)
    def _(i):
        s = i // 16
        r = (i % 16) * 16
        values = resv[s, pl.ds(pl.multiple_of(r, 16), 16), :].astype(F32)
        for k in range(WIDTH // LANES):
            x32[0, k, pl.ds(pl.multiple_of(i * 16, 16), 16), :] = values[:, LANES * k : LANES * (k + 1)]

    @pl.loop(0, STEPS)
    def _(j):
        for k in range(WIDTH // LANES):
            x32[1, k, rows(j), :] = x32[0, k, pl.ds(j, SEGS, stride=STEPS), :]

    project(0)
    weight_hold(1, 0, 1, 2)
    weight_relay(1, 0)

    sent = []

    def send(slot, quarter, tp):
        k = len(sent)
        copy = remote(
            mid.at[slot, quarter], mid.at[slot, quarter], ags.at[k], agr.at[slot, quarter], c, tp
        )
        copy.start()
        sent.append(copy)

    zp, zm, zz = ztp(1, xl), ztp(3, xl), ztp(2, xl)
    xp, xm, xz = ztp(1, 1 - xl), ztp(3, 1 - xl), ztp(2, 1 - xl)
    for part in range(2):
        project_wait(0, part)

        @pl.loop(0, 16)
        def _(i, part=part):
            here = pl.ds(pl.multiple_of(part * HALF + i * 16, 16), 16)
            before = jnp.concatenate([x32[1, k, here, :] for k in range(WIDTH // LANES)], axis=1)
            value = (before + arrivals(0, part, i)).astype(BF16)
            mid[t, part * 2 + i // 8, pl.ds(pl.multiple_of((i % 8) * 16, 16), 16), :] = value

        for quarter in (2 * part, 2 * part + 1):
            send(t, quarter, xn)
            send(t, quarter, zp)
            send(t, quarter, zm)

    def have(slot, *quarters):
        for quarter in quarters:
            arrived(mid.at[slot, quarter], agr.at[slot, quarter])

    load_win.wait()

    def absorb(*slots, fresh=False):
        count = len(slots)
        scales = [gain[:, pl.ds(pl.multiple_of(slot * WIDTH, WIDTH), WIDTH)] for slot in slots]

        @pl.loop(0, 16)
        def _(i):
            here = pl.ds(pl.multiple_of((i % 4) * 32, 32), 32)
            there = pl.ds(pl.multiple_of(i * 32, 32), 32)
            total = 0.0 if fresh else ssq[there, :]
            for k, slot in enumerate(slots):
                values = mid[slot, i // 4, here, :].astype(F32)
                square = values * values
                total += square[:, 0:128] + square[:, 128:256] + square[:, 256:384] + square[:, 384:512]
                scaled[there, WIDTH * k : WIDTH * (k + 1)] = (values * scales[k]).astype(BF16)
            ssq[there, :] = total

        @pl.loop(0, 6)
        def _(i):
            cols = pl.ds(pl.multiple_of((i % 2) * 256, 256), 256)
            weights = [win[i // 2, pl.ds(pl.multiple_of(slot * WIDTH, WIDTH), WIDTH), cols] for slot in slots]
            product = jnp.dot(
                scaled[:, 0 : WIDTH * count], jnp.concatenate(weights, axis=0), preferred_element_type=F32
            )
            acc[i // 2, :, cols] = product if fresh else acc[i // 2, :, cols] + product

    absorb(t, fresh=True)
    have(zm, 2, 3)
    send(zm, 2, xn)
    send(zm, 3, xn)
    send(zm, 2, zp)
    have(zp, 2, 3)
    send(zp, 2, xn)
    send(zp, 3, xn)
    send(zp, 3, zm)
    have(xn, 0, 1)
    for quarter in range(2):
        send(xn, quarter, zp)
        send(xn, quarter, zm)
    have(zm, 0, 1)
    send(zm, 0, zp)
    have(zp, 0, 1)
    send(zp, 1, zm)
    weight_hold(1, 3)
    absorb(zm, zp)
    have(zz, 2, 3)
    send(zz, 2, xn)
    send(zz, 3, xn)
    have(xm, 0, 1)
    send(xm, 0, zp)
    have(xp, 0, 1)
    send(xp, 1, zm)
    weight_relay(1, 1)
    have(zz, 0, 1)
    have(xn, 2, 3)
    absorb(xn, zz)
    weight_relay(1, 2)
    have(xm, 2, 3)
    have(xp, 2, 3)
    absorb(xm, xp)
    weight_relay(1, 3)
    have(xz, 0, 1, 2, 3)
    absorb(xz)

    def factors(start, count):
        here = pl.ds(start if isinstance(start, int) else pl.multiple_of(start, 64), count)
        meansq = jnp.sum(ssq[here, :], axis=1, keepdims=True) * (1.0 / 4096.0)
        ssq[here, :] = jnp.broadcast_to(lax.rsqrt(meansq + 1e-6), (count, LANES))

    def finish(i):
        here = pl.ds(i * 16 if isinstance(i, int) else pl.multiple_of(i * 16, 16), 16)
        factor = jnp.concatenate([ssq[here, :]] * (WIDTH // LANES), axis=1)
        values = [(acc[p, here, :] * factor).astype(BF16) for p in range(3)]
        for p in range(3):
            acc[p, here, :] = values[p].astype(F32)
        return values

    factors(448, 64)
    tails = finish(31)
    for p in range(3):
        ltail_s[p] = tails[p]
    l_copy = remote(ltail_s, ltail, hs.at[2], hr.at[2], (c + 1) % 16, t)
    l_copy.start()

    @pl.loop(0, 7)
    def _(i):
        factors(i * 64, 64)

    @pl.loop(0, 31)
    def _(i):
        finish(i)

    weight_late(1, 0, 1, 2, 3)

    def longer(j, now, before, before2):
        mixed = [tap(sw2, 0, p) * now[p] + tap(sw2, 1, p) * before[p] + tap(sw2, 2, p) * before2[p] for p in range(3)]
        q32[rows(j), :] = mixed[0]
        uext[rows(j), :] = mixed[1] * mixed[2]

    @pl.loop(2, STEPS)
    def _(j):
        longer(
            j,
            [acc[p, rows(j), :] for p in range(3)],
            [acc[p, rows(j - 1), :] for p in range(3)],
            [acc[p, rows(j - 2), :] for p in range(3)],
        )

    arrived(ltail, hr.at[2])
    edge1, edge2 = [], []
    for p in range(3):
        got = ltail[p].astype(F32) * live
        edge2.append(jnp.where(first, pltpu.roll(got[:SEGS], 5, 0), pltpu.roll(acc[p, rows(62), :], 1, 0)))
        edge1.append(jnp.where(first, pltpu.roll(got[SEGS:], 5, 0), pltpu.roll(acc[p, rows(63), :], 1, 0)))
    y0 = [acc[p, rows(0), :] for p in range(3)]
    y1 = [acc[p, rows(1), :] for p in range(3)]
    longer(0, y0, edge1, edge2)
    longer(1, y1, y0, edge1)

    def row_of(ref, n, lane):
        return jnp.broadcast_to(ref[n : n + 1, lane], (SEGS, LANES))

    @pl.loop(0, WIDTH // LANES)
    def _(lt):
        lane = lanes(lt)
        decay = [jnp.exp(-row_of(rate, n, lane)) for n in range(POLES)]

        def step(i, states):
            for k in range(4):
                u = uext[rows(4 * i + k), lane]
                states = [decay[n] * states[n] + u for n in range(POLES)]
            return tuple(states)

        states = lax.fori_loop(0, STEPS // 4, step, tuple(jnp.zeros((SEGS, LANES), F32) for _ in range(POLES)))
        for n in range(POLES):
            est[rows(n), lane] = states[n]
            decays[rows(n), lane] = decay[n]

    place = seg1 % 4

    @pl.loop(0, WIDTH // LANES)
    def _(lt):
        lane = lanes(lt)
        for g in range(2):
            packed = []
            for h in range(2):
                total = jnp.zeros((SEGS, LANES), F32)
                for r in range(4):
                    n = g * 8 + h * 4 + r
                    span = jnp.exp(-float(STEPS) * row_of(rate, n, lane))
                    value = est[rows(n), lane]
                    value = value + span * jnp.where(place >= 1, pltpu.roll(value, 1, 0), 0.0)
                    value = value + span * span * jnp.where(place >= 2, pltpu.roll(value, 2, 0), 0.0)
                    est[rows(n), lane] = jnp.where(place >= 1, pltpu.roll(value, 1, 0), 0.0)
                    end = value if r == 3 else pltpu.roll(value, (r - 3) % 8, 0)
                    total = jnp.where(place == r, end, total)
                packed.append(total)
            st_s[pl.ds(g * 16, 16), lane] = jnp.concatenate(packed, axis=0).astype(BF16)

    def state_copy(d):
        return remote(st_s, st_r.at[d - 1], sts.at[d - 1], strv.at[d - 1], c + d, t)

    for d in range(15, 0, -1):

        @pl.when(c + d < 16)
        def _(d=d):
            state_copy(d).start()

    @pl.loop(0, WIDTH // LANES)
    def _(lt):
        lane = lanes(lt)
        for n in range(POLES):
            weights[rows(n), lane] = row_of(resid, n, lane) * jnp.sqrt(1.0 - jnp.exp(-2.0 * row_of(rate, n, lane)))

    packs = []
    for g in range(4):
        total = jnp.zeros((SEGS, WIDTH), F32)
        for r in range(4):
            n = g * 4 + r
            total = jnp.where(seg % 4 == r, jnp.broadcast_to(rate[n : n + 1, :], (SEGS, WIDTH)), total)
        packs.append(total)
    pack = jnp.concatenate(packs, axis=0)
    hin[...] = jnp.zeros((4 * SEGS, WIDTH), F32)
    for d in range(1, 16):

        @pl.when(c - d >= 0)
        def _(d=d):
            arrived(st_r.at[d - 1], strv.at[d - 1])
            hin[...] += jnp.exp(pack * (-256.0 * (d - 1))) * st_r[d - 1].astype(F32)

    for part in range(2):

        @pl.loop(0, WIDTH // LANES)
        def _(lt, part=part):
            lane = lanes(lt)
            decay, weight, states = [], [], []
            for n in range(POLES):
                decay.append(decays[rows(n), lane])
                weight.append(weights[rows(n), lane])
                state = est[rows(n), lane]
                if part == 0:
                    r = row_of(rate, n, lane)
                    k = (n // 4) * SEGS + n % 4
                    enter = jnp.where(
                        seg1 < 4,
                        jnp.broadcast_to(hin[k : k + 1, lane], (SEGS, LANES)),
                        jnp.broadcast_to(hin[k + 4 : k + 5, lane], (SEGS, LANES)),
                    )
                    state = state + jnp.exp(r * (place.astype(F32) * (-float(STEPS)))) * enter
                states.append(state)
            skip = jnp.broadcast_to(skip2[:, lane], (SEGS, LANES))

            def step(i, states):
                pair = []
                for k in range(2):
                    j = part * (STEPS // 2) + 2 * i + k
                    u = uext[rows(j), lane]
                    states = [decay[n] * states[n] + u for n in range(POLES)]
                    terms = [weight[n] * states[n] for n in range(POLES)]
                    while len(terms) > 1:
                        terms = [terms[a] + terms[a + 1] for a in range(0, len(terms), 2)]
                    pair.append(q32[rows(j), lane] * (terms[0] + skip * u))
                zo[1, part, pl.ds(pl.multiple_of(i * 16, 16), 16), lane] = jnp.concatenate(pair, axis=0).astype(BF16)
                return tuple(states)

            states = lax.fori_loop(0, STEPS // 4, step, tuple(states))
            if part == 0:
                for n in range(POLES):
                    est[rows(n), lane] = states[n]

        z_copy(1, part).start()

    project(1)
    for part in range(2):
        project_wait(1, part)

        @pl.loop(0, 16)
        def _(i, part=part):
            base = mid[t, part * 2 + i // 8, pl.ds(pl.multiple_of((i % 8) * 16, 16), 16), :].astype(F32)
            value = base + arrivals(1, part, i)
            j = part * (STEPS // 2) + 2 * i
            for k in range(WIDTH // LANES):
                piece = value[:, LANES * k : LANES * (k + 1)]
                x32[2, k, pl.ds(j, SEGS, stride=STEPS), :] = piece[:SEGS]
                x32[2, k, pl.ds(j + 1, SEGS, stride=STEPS), :] = piece[SEGS:]

    @pl.loop(0, 32)
    def _(i):
        s = i // 16
        r = (i % 16) * 16
        here = pl.ds(pl.multiple_of(i * 16, 16), 16)
        value = jnp.concatenate([x32[2, k, here, :] for k in range(WIDTH // LANES)], axis=1)
        obf[s, pl.ds(pl.multiple_of(r, 16), 16), :] = value.astype(BF16)

    store = pltpu.make_async_copy(obf, out_h, loc.at[3])
    store.start()

    tail_copy.wait_send()
    u_copy.wait_send()
    l_copy.wait_send()
    weight_drain(0, wo1_h)
    weight_drain(1, wo2_h)
    project_drain(0)
    project_drain(1)
    for copy in sent:
        copy.wait_send()
    for d in range(1, 16):

        @pl.when(c + d < 16)
        def _(d=d):
            state_copy(d).wait_send()

    store.wait()


def local(
    residual_in, mr_qkv, mr_short_w, mr_filter, mr_skip, mr_out_w, lr_gain,
    lr_in_w, lr_short_w, lr_rate, lr_res, lr_skip, lr_out_w,
):
    vmem = pl.BlockSpec(memory_space=pltpu.VMEM)
    hbm = pl.BlockSpec(memory_space=pl.ANY)
    dma = pltpu.SemaphoreType.DMA
    scratch = [
        pltpu.VMEM((2, 3, 256, WIDTH), BF16),
        pltpu.VMEM((2, 3, 8, WIDTH), BF16),
        pltpu.VMEM((3, WIDTH // LANES, ROWS, LANES), F32),
        pltpu.VMEM((ROWS, WIDTH), F32),
        pltpu.VMEM((192 * SEGS, WIDTH), F32),
        pltpu.VMEM((TAPS * SEGS, WIDTH), F32),
        pltpu.VMEM((256, WIDTH), BF16),
        pltpu.VMEM((256, WIDTH), BF16),
        pltpu.VMEM((2, 2, ROWS // 2, WIDTH), BF16),
        pltpu.VMEM((2, 2, ROWS // 2, WIDTH), BF16),
        pltpu.VMEM((2, 8, 2, WIDTH, 256), BF16),
        pltpu.VMEM((3, 4096, WIDTH), BF16),
        pltpu.VMEM((2, 2, 6, ROWS // 2, 256), BF16),
        pltpu.VMEM((2, 2, 6, ROWS // 2, 256), BF16),
        pltpu.VMEM((ROWS, WIDTH), F32),
        pltpu.VMEM((8, 4, 128, WIDTH), BF16),
        pltpu.VMEM((ROWS, 2 * WIDTH), BF16),
        pltpu.VMEM((3, ROWS, WIDTH), F32),
        pltpu.VMEM((ROWS, LANES), F32),
        pltpu.VMEM((3, 16, WIDTH), BF16),
        pltpu.VMEM((3, 16, WIDTH), BF16),
        pltpu.VMEM((POLES * SEGS, WIDTH), F32),
        pltpu.VMEM((POLES * SEGS, WIDTH), F32),
        pltpu.VMEM((POLES * SEGS, WIDTH), F32),
        pltpu.VMEM((4 * SEGS, WIDTH), BF16),
        pltpu.VMEM((15, 4 * SEGS, WIDTH), BF16),
        pltpu.VMEM((4 * SEGS, WIDTH), F32),
        pltpu.VMEM((2, 256, WIDTH), BF16),
        pltpu.VMEM((2, 256, WIDTH), BF16),
        dma((4,)),
        dma((3,)),
        dma((3,)),
        dma((2, 3)),
        dma((2, 2, 4)),
        dma((2, 8)),
        dma((2, 8, 2)),
        dma((2, 2)),
        dma((2, 2)),
        dma((2, 2, 6)),
        dma((2, 2, 6)),
        dma((32,)),
        dma((8, 4)),
        dma((15,)),
        dma((15,)),
    ]
    return pl.pallas_call(
        kernel,
        out_shape=jax.ShapeDtypeStruct((2, 256, WIDTH), BF16),
        in_specs=[hbm, hbm, vmem, vmem, vmem, hbm, vmem, hbm, vmem, vmem, vmem, vmem, hbm],
        out_specs=hbm,
        scratch_shapes=scratch,
        compiler_params=pltpu.CompilerParams(
            collective_id=0, has_side_effects=True, vmem_limit_bytes=62 * 1024 * 1024
        ),
    )(
        residual_in,
        jnp.transpose(mr_qkv, (0, 2, 1, 3)),
        mr_short_w,
        mr_filter,
        mr_skip.reshape(1, WIDTH),
        mr_out_w,
        lr_gain.reshape(1, 8 * WIDTH),
        jnp.transpose(lr_in_w, (1, 0, 2)),
        lr_short_w,
        lr_rate,
        lr_res,
        lr_skip.reshape(1, WIDTH),
        lr_out_w,
    )


def solution(mesh):
    in_specs = (
        P(None, "ctx", "tp"),
        P(None, "ctx", None, "tp"),
        P(None, None, "tp"),
        P(None, "tp"),
        P("tp"),
        P("tp", "ctx"),
        P(),
        P(None, None, "tp"),
        P(None, None, "tp"),
        P(None, "tp"),
        P(None, "tp"),
        P("tp"),
        P("tp", "ctx"),
    )
    return jax.shard_map(local, mesh=mesh, in_specs=in_specs, out_specs=P(None, "ctx", "tp"), check_vma=False)
```

```python
import jax
import jax.numpy as jnp
from jax import lax
from jax.experimental import pallas as pl
from jax.experimental.pallas import tpu as pltpu
from jax.sharding import PartitionSpec as P

MESH = pl.DeviceIdType.MESH
F32 = jnp.float32
BF16 = jnp.bfloat16

SEGS = 8
STEPS = 64
ROWS = SEGS * STEPS
WIDTH = 512
TAPS = 128
POLES = 16
LANES = 128


def kernel(
    res_h, qkv_h, sw1, filt, skip1, wo1_h, gain, win_h, sw2, rate, resid, skip2, wo2_h,
    out_h,
    qkv_v, xtail, x32, q32, uext, fb, pk_s, pk_r, zo, zn, w, win, ps, pr, pacc, mid, scaled, acc, ssq,
    ltail_s, ltail, est, decays, weights, st_s, st_r, hin, obf, resv,
    loc, hs, hr, wsnd, fsnd, bsnd, wrecv, zs, zr, pss, prs, ags, agr, sts, strv,
):
    c = lax.axis_index("ctx")
    t = lax.axis_index("tp")
    core = c % 2
    m = c // 2
    y = m % 4
    xh = m // 4
    z = t // 2
    xl = t % 2
    sib = c + 1 - 2 * core
    xn = t + 1 - 2 * xl

    def ztp(dz, x):
        return ((z + dz) % 4) * 2 + x

    def remote(src, dst, ssem, rsem, ctx, tp):
        return pltpu.make_async_remote_copy(
            src_ref=src,
            dst_ref=dst,
            send_sem=ssem,
            recv_sem=rsem,
            device_id={"ctx": ctx, "tp": tp},
            device_id_type=MESH,
        )

    def arrived(ref, sem):
        pltpu.make_async_copy(ref, ref, sem).wait()

    load_qkv = pltpu.make_async_copy(qkv_h, qkv_v, loc.at[0])
    load_qkv.start()
    load_res = pltpu.make_async_copy(res_h, resv, loc.at[1])
    load_res.start()

    barrier = pltpu.get_barrier_semaphore()

    def greet(ctx, tp):
        pl.semaphore_signal(barrier, inc=1, device_id={"ctx": ctx, "tp": tp}, device_id_type=MESH)

    for d in range(1, 16):
        greet((c + d) % 16, t)
    greet(c, xn)
    greet((c + 8) % 16, xn)
    greet(c, ztp(1, xl))
    greet(c, ztp(3, xl))
    pl.semaphore_wait(barrier, 19)

    tail_copy = remote(qkv_h.at[:, :, 248:256, :], xtail, hs.at[0], hr.at[0], (c + 1) % 16, t)
    tail_copy.start()

    holder = (y + xl) % 2 == 0
    relay = (y + xl) % 2 == 1
    ups = ((y + 1) % 4, (y + 3) % 4)

    def place_of(k, row):
        xs = (xl, 1 - xl, 1 - xl, xl)[k]
        xhs = (xh, xh, 1 - xh, 1 - xh)[k]
        return xs * 4 + xhs * 2 + row // 2

    def ctx_of(h, row):
        return (h * 4 + row) * 2 + core

    def weight_first(stage, source):
        mine = place_of(0, y)
        target = w.at[stage, mine, core]
        arrival = wrecv.at[stage, mine, core]
        home = pltpu.make_async_copy(source, target, arrival)
        along = [
            remote(source, target, wsnd.at[stage, 0], arrival, ctx_of(xh, ups[0]), t),
            remote(source, target, wsnd.at[stage, 1], arrival, ctx_of(xh, ups[1]), t),
            remote(source, target, wsnd.at[stage, 2], arrival, ctx_of(1 - xh, y), t),
        ]
        across = [
            remote(source, target, wsnd.at[stage, 0], arrival, c, xn),
            remote(source, target, wsnd.at[stage, 1], arrival, ctx_of(1 - xh, y), xn),
        ]
        return home, along, across

    def weight_start(stage, source):
        home, along, across = weight_first(stage, source)

        @pl.when(holder)
        def _():
            home.start()
            for copy in along:
                copy.start()

        @pl.when(relay)
        def _():
            for copy in across:
                copy.start()

    def weight_pass(stage, index, sem, ctx):
        block = w.at[stage, index, core]
        return remote(block, block, sem, wrecv.at[stage, index, core], ctx, t)

    def weight_pass_half(stage, index, half, sem, ctx):
        block = w.at[stage, index, core, 256 * half : 256 * (half + 1), :]
        return remote(block, block, sem, wrecv.at[stage, index, core], ctx, t)

    def weight_got(stage, index):
        arrived(w.at[stage, index, core], wrecv.at[stage, index, core])

    def weight_moves(stage, k):
        here, up, down, far = place_of(k, y), place_of(k, ups[0]), place_of(k, ups[1]), place_of(k, (y + 2) % 4)

        def sibling(index, n):
            return weight_pass(stage, index, bsnd.at[stage, n], sib)

        held = [sibling(here, k)]
        if k:
            held += [weight_pass(stage, here, fsnd.at[stage, n, k], ctx_of(xh, ups[n])) for n in range(2)]
        late = [sibling(far, 4 + k)]
        below = [sibling(down, k), weight_pass_half(stage, down, 0, fsnd.at[stage, 0, k], ctx_of(xh, ups[0]))]
        above = [sibling(up, 4 + k), weight_pass_half(stage, up, 1, fsnd.at[stage, 1, k], ctx_of(xh, ups[1]))]
        return (here, held), (far, late), (down, below), (up, above)

    def weight_hold(stage, *ks):
        @pl.when(holder)
        def _():
            for k in ks:
                first_ = weight_moves(stage, k)[0]
                weight_got(stage, first_[0])
                for copy in reversed(first_[1]):
                    copy.start()

    def weight_relay(stage, k):
        _, _, below, above = weight_moves(stage, k)

        @pl.when(relay)
        def _():
            for index, copies in (below, above):
                weight_got(stage, index)
                for copy in reversed(copies):
                    copy.start()

    def weight_late(stage, *ks):
        @pl.when(holder)
        def _():
            for k in ks:
                _, (index, copies), _, _ = weight_moves(stage, k)
                weight_got(stage, index)
                copies[0].start()

    def weight_sibling(stage, index):
        arrived(w.at[stage, index, 1 - core], wrecv.at[stage, index, 1 - core])

    def weight_drain(stage, source):
        _, along, across = weight_first(stage, source)

        @pl.when(holder)
        def _():
            for copy in along:
                copy.wait_send()
            for k in range(4):
                first_, late, _, _ = weight_moves(stage, k)
                for copy in first_[1] + late[1]:
                    copy.wait_send()

        @pl.when(relay)
        def _():
            for copy in across:
                copy.wait_send()
            for k in range(4):
                _, _, below, above = weight_moves(stage, k)
                for copy in below[1] + above[1]:
                    copy.wait_send()

    weight_start(0, wo1_h)
    load_win = pltpu.make_async_copy(win_h, win, loc.at[2])

    seg = lax.broadcasted_iota(jnp.int32, (SEGS, WIDTH), 0)
    seg1 = lax.broadcasted_iota(jnp.int32, (SEGS, LANES), 0)
    first = seg % 4 == 0
    live = jnp.where(c > 0, 1.0, 0.0).astype(F32)

    def rows(j, count=1):
        start = j * SEGS
        return pl.ds(start if isinstance(start, int) else pl.multiple_of(start, SEGS), count * SEGS)

    def lanes(lt):
        return pl.ds(pl.multiple_of(lt * LANES, LANES), LANES)

    @pl.loop(0, TAPS // 8)
    def _(i):
        taps = filt[pl.ds(pl.multiple_of(i * 8, 8), 8), :].astype(F32)
        for k in range(8):
            fb[rows(i * 8 + k), :] = jnp.broadcast_to(taps[k : k + 1, :], (SEGS, WIDTH))

    load_qkv.wait()
    for s in range(2):
        for p in range(3):

            @pl.loop(0, 16)
            def _(i, s=s, p=p):
                here = pl.ds(pl.multiple_of(i * 16, 16), 16)
                there = pl.ds(pl.multiple_of(s * 256 + i * 16, 16), 16)
                values = qkv_v[s, p, here, :].astype(F32)
                for k in range(WIDTH // LANES):
                    x32[p, k, there, :] = values[:, LANES * k : LANES * (k + 1)]

    def tap(ref, lag, p):
        return jnp.broadcast_to(ref[lag, p : p + 1, :], (SEGS, WIDTH))

    def strided3(p, j):
        return jnp.concatenate(
            [x32[p, k, pl.ds(j, SEGS, stride=STEPS), :] for k in range(WIDTH // LANES)], axis=1
        )

    def medium(j, now, before, before2):
        mixed = [tap(sw1, 0, p) * now[p] + tap(sw1, 1, p) * before[p] + tap(sw1, 2, p) * before2[p] for p in range(3)]
        q32[rows(j), :] = mixed[0]
        uext[rows(j + 128), :] = (mixed[1] * mixed[2]).astype(BF16).astype(F32)

    last = [strided3(p, 63) for p in range(3)]
    last2 = [strided3(p, 62) for p in range(3)]
    x0 = [strided3(p, 0) for p in range(3)]
    x1 = [strided3(p, 1) for p in range(3)]
    own1 = [jnp.where(first, 0.0, pltpu.roll(v, 1, 0)) for v in last]
    own2 = [jnp.where(first, 0.0, pltpu.roll(v, 1, 0)) for v in last2]
    medium(0, x0, own1, own2)
    medium(1, x1, x0, own1)

    def medium_step(j, carried):
        now = [strided3(p, j) for p in range(3)]
        before, before2 = carried
        medium(j, now, before, before2)
        return now, before

    lax.fori_loop(2, STEPS, medium_step, (x1, x0))

    @pl.loop(0, STEPS // 4)
    def _(i):
        packed = []
        for k in range(2):
            even = uext[rows(128 + 4 * i + 2 * k), :]
            odd = uext[rows(129 + 4 * i + 2 * k), :]
            packed.append(jnp.where(seg % 4 >= 2, even, pltpu.roll(odd, 6, 0)))
        pk_s[pl.ds(pl.multiple_of(i * 16, 16), 16), :] = jnp.concatenate(packed, axis=0).astype(BF16)

    u_copy = remote(pk_s, pk_r, hs.at[1], hr.at[1], (c + 1) % 16, t)
    u_copy.start()
    weight_hold(0, 0, 1, 2)
    weight_relay(0, 0)

    arrived(xtail, hr.at[0])

    def halo(p, row):
        top = xtail[0, p].astype(F32)[row : row + 1, :] * live
        bottom = xtail[1, p].astype(F32)[row : row + 1, :] * live
        return jnp.where(seg < 4, jnp.broadcast_to(top, (SEGS, WIDTH)), jnp.broadcast_to(bottom, (SEGS, WIDTH)))

    full1 = [jnp.where(first, halo(p, 7), own1[p]) for p in range(3)]
    full2 = [jnp.where(first, halo(p, 6), own2[p]) for p in range(3)]
    medium(0, x0, full1, full2)
    medium(1, x1, x0, full1)

    load_win.start()
    arrived(pk_r, hr.at[1])

    @pl.loop(0, STEPS // 2)
    def _(i):
        both = pk_r[pl.ds(pl.multiple_of((i // 2) * 16, 16), 16), :].astype(F32) * live
        got = jnp.where(i % 2 == 0, both[:SEGS], both[SEGS:])
        even = uext[rows(128 + 2 * i), :]
        odd = uext[rows(129 + 2 * i), :]
        uext[rows(64 + 2 * i), :] = jnp.where(first, pltpu.roll(got, 5, 0), pltpu.roll(even, 1, 0))
        uext[rows(65 + 2 * i), :] = jnp.where(first, pltpu.roll(got, 7, 0), pltpu.roll(odd, 1, 0))
        uext[rows(2 * i), :] = jnp.where(seg % 4 < 2, pltpu.roll(got, 6, 0), pltpu.roll(even, 2, 0))
        uext[rows(1 + 2 * i), :] = jnp.where(seg % 4 < 2, got, pltpu.roll(odd, 2, 0))


    HALF = ROWS // 2

    def z_copy(stage, part):
        return remote(zo.at[stage, part], zn.at[stage, part], zs.at[stage, part], zr.at[stage, part], c, xn)

    def p_copy(stage, part, i):
        return remote(
            ps.at[stage, part, i],
            pr.at[stage, part, i],
            pss.at[stage, part, i],
            prs.at[stage, part, i],
            c,
            ztp(1 if i % 2 == 0 else 3, xl),
        )

    def term(stage, part, d, half):
        dest = (z + d) % 4
        both = jnp.concatenate([zo[stage, part], zn[stage, part]], axis=1)
        weights = jnp.concatenate([w[stage, xl * 4 + dest, half], w[stage, (1 - xl) * 4 + dest, half]], axis=0)
        return jnp.dot(both, weights, preferred_element_type=F32)

    def project_first(stage, part):
        arrived(zn.at[stage, part], zr.at[stage, part])
        for i, d, half in ((0, 2, 0), (1, 2, 1), (2, 1, 1), (3, 3, 0)):
            if part == 0 and i in (0, 2, 3):
                for source in range(2):
                    weight_sibling(stage, source * 4 + (z + d) % 4)
            ps[stage, part, i] = term(stage, part, d, half).astype(BF16)
            p_copy(stage, part, i).start()

    def project_own(stage, part):
        if part == 0:
            for source in range(2):
                weight_sibling(stage, source * 4 + z)
        for own in range(2):
            pacc[HALF * part : HALF * (part + 1), 256 * own : 256 * (own + 1)] = term(stage, part, 0, own)

    def project_relay(stage, part):
        for i, d, half in ((4, 1, 0), (5, 3, 1)):
            mine = term(stage, part, d, half)
            arrived(pr.at[stage, part, i - 4], prs.at[stage, part, i - 4])
            ps[stage, part, i] = (mine + pr[stage, part, i - 4].astype(F32)).astype(BF16)
            p_copy(stage, part, i).start()

    def project(stage):
        project_first(stage, 0)
        project_first(stage, 1)
        project_relay(stage, 0)
        project_own(stage, 0)
        project_relay(stage, 1)
        project_own(stage, 1)

    def project_wait(stage, part):
        for i in (2, 3, 4, 5):
            arrived(pr.at[stage, part, i], prs.at[stage, part, i])

    def project_drain(stage):
        for part in range(2):
            z_copy(stage, part).wait_send()
            for i in range(6):
                p_copy(stage, part, i).wait_send()

    def arrivals(stage, part, i):
        here = pl.ds(pl.multiple_of(i * 16, 16), 16)
        left = pr[stage, part, 3, here, :].astype(F32) + pr[stage, part, 4, here, :].astype(F32)
        right = pr[stage, part, 2, here, :].astype(F32) + pr[stage, part, 5, here, :].astype(F32)
        own = pacc[pl.ds(pl.multiple_of(part * HALF + i * 16, 16), 16), :]
        return own + jnp.concatenate([left, right], axis=1)

    def filter_blocks(first_block):
        @pl.loop(first_block, first_block + 2)
        def _(block):
            lane = lanes((block % 8) // 2)
            part = block // 8
            r0 = (block % 2) * 16
            j0 = part * 32 + r0

            def taps8(ib, totals):
                base = 128 + j0 - 8 * ib - 7
                window = uext[pl.ds(pl.multiple_of(base * SEGS, SEGS), 23 * SEGS), lane]
                weights = fb[pl.ds(pl.multiple_of(ib * 64, 64), 64), lane]
                totals = list(totals)
                for b in range(8):
                    f = weights[b * SEGS : (b + 1) * SEGS]
                    for a in range(16):
                        k = a + 7 - b
                        totals[a] = totals[a] + f * window[k * SEGS : (k + 1) * SEGS]
                return tuple(totals)

            totals = lax.fori_loop(0, 16, taps8, tuple(jnp.zeros((SEGS, LANES), F32) for _ in range(16)))
            skip = jnp.broadcast_to(skip1[:, lane], (SEGS, LANES))
            for a in range(0, 16, 2):
                pair = []
                for k in (a, a + 1):
                    u = uext[rows(128 + j0 + k), lane]
                    pair.append(q32[rows(j0 + k), lane] * (totals[k] + skip * u))
                zo[0, part, pl.ds(pl.multiple_of((r0 + a) * SEGS, 16), 16), lane] = jnp.concatenate(
                    pair, axis=0
                ).astype(BF16)

    filter_blocks(0)
    filter_blocks(2)
    weight_hold(0, 3)
    weight_relay(0, 1)
    filter_blocks(4)
    filter_blocks(6)
    z_copy(0, 0).start()
    weight_late(0, 0)
    filter_blocks(8)
    weight_relay(0, 2)
    weight_late(0, 1)
    filter_blocks(10)
    filter_blocks(12)
    weight_relay(0, 3)
    weight_late(0, 2)
    filter_blocks(14)
    z_copy(0, 1).start()
    weight_late(0, 3)
    weight_start(1, wo2_h)

    load_res.wait()

    @pl.loop(0, 32)
    def _(i):
        s = i // 16
        r = (i % 16) * 16
        values = resv[s, pl.ds(pl.multiple_of(r, 16), 16), :].astype(F32)
        for k in range(WIDTH // LANES):
            x32[0, k, pl.ds(pl.multiple_of(i * 16, 16), 16), :] = values[:, LANES * k : LANES * (k + 1)]

    @pl.loop(0, STEPS)
    def _(j):
        for k in range(WIDTH // LANES):
            x32[1, k, rows(j), :] = x32[0, k, pl.ds(j, SEGS, stride=STEPS), :]

    project(0)
    weight_hold(1, 0, 1, 2)
    weight_relay(1, 0)

    sent = []

    def send(slot, quarter, tp):
        k = len(sent)
        copy = remote(
            mid.at[slot, quarter], mid.at[slot, quarter], ags.at[k], agr.at[slot, quarter], c, tp
        )
        copy.start()
        sent.append(copy)

    zp, zm, zz = ztp(1, xl), ztp(3, xl), ztp(2, xl)
    xp, xm, xz = ztp(1, 1 - xl), ztp(3, 1 - xl), ztp(2, 1 - xl)
    for part in range(2):
        project_wait(0, part)

        @pl.loop(0, 16)
        def _(i, part=part):
            here = pl.ds(pl.multiple_of(part * HALF + i * 16, 16), 16)
            before = jnp.concatenate([x32[1, k, here, :] for k in range(WIDTH // LANES)], axis=1)
            value = (before + arrivals(0, part, i)).astype(BF16)
            mid[t, part * 2 + i // 8, pl.ds(pl.multiple_of((i % 8) * 16, 16), 16), :] = value

        for quarter in (2 * part, 2 * part + 1):
            send(t, quarter, xn)
            send(t, quarter, zp)
            send(t, quarter, zm)

    def have(slot, *quarters):
        for quarter in quarters:
            arrived(mid.at[slot, quarter], agr.at[slot, quarter])

    load_win.wait()

    def absorb(*slots, fresh=False):
        count = len(slots)
        scales = [gain[:, pl.ds(pl.multiple_of(slot * WIDTH, WIDTH), WIDTH)] for slot in slots]

        @pl.loop(0, 16)
        def _(i):
            here = pl.ds(pl.multiple_of((i % 4) * 32, 32), 32)
            there = pl.ds(pl.multiple_of(i * 32, 32), 32)
            total = 0.0 if fresh else ssq[there, :]
            for k, slot in enumerate(slots):
                values = mid[slot, i // 4, here, :].astype(F32)
                square = values * values
                total += square[:, 0:128] + square[:, 128:256] + square[:, 256:384] + square[:, 384:512]
                scaled[there, WIDTH * k : WIDTH * (k + 1)] = (values * scales[k]).astype(BF16)
            ssq[there, :] = total

        @pl.loop(0, 6)
        def _(i):
            cols = pl.ds(pl.multiple_of((i % 2) * 256, 256), 256)
            weights = [win[i // 2, pl.ds(pl.multiple_of(slot * WIDTH, WIDTH), WIDTH), cols] for slot in slots]
            product = jnp.dot(
                scaled[:, 0 : WIDTH * count], jnp.concatenate(weights, axis=0), preferred_element_type=F32
            )
            acc[i // 2, :, cols] = product if fresh else acc[i // 2, :, cols] + product

    absorb(t, fresh=True)
    weight_hold(1, 3)
    weight_relay(1, 1)
    have(xn, 0, 1)
    for quarter in range(2):
        send(xn, quarter, zp)
        send(xn, quarter, zm)
    have(zm, 0, 1, 2, 3)
    send(zm, 0, zp)
    send(zm, 2, zp)
    send(zm, 2, xn)
    send(zm, 3, xn)
    have(zp, 0, 1, 2, 3)
    send(zp, 1, zm)
    send(zp, 3, zm)
    send(zp, 2, xn)
    send(zp, 3, xn)
    absorb(zm, zp)
    weight_relay(1, 2)
    have(xm, 0, 1)
    send(xm, 0, zp)
    have(xp, 0, 1)
    send(xp, 1, zm)
    have(zz, 0, 1, 2, 3)
    send(zz, 2, xn)
    send(zz, 3, xn)
    have(xn, 2, 3)
    absorb(xn, zz)
    weight_relay(1, 3)
    have(xm, 2, 3)
    have(xp, 2, 3)
    absorb(xm, xp)
    have(xz, 0, 1, 2, 3)
    absorb(xz)
    weight_late(1, 0, 1, 2, 3)

    def finish(i):
        here = pl.ds(i * 16 if isinstance(i, int) else pl.multiple_of(i * 16, 16), 16)
        meansq = jnp.sum(ssq[here, :], axis=1, keepdims=True) * (1.0 / 4096.0)
        factor = lax.rsqrt(meansq + 1e-6)
        values = [(acc[p, here, :] * factor).astype(BF16) for p in range(3)]
        for p in range(3):
            acc[p, here, :] = values[p].astype(F32)
        return values

    tails = finish(31)
    for p in range(3):
        ltail_s[p] = tails[p]
    l_copy = remote(ltail_s, ltail, hs.at[2], hr.at[2], (c + 1) % 16, t)
    l_copy.start()

    @pl.loop(0, 31)
    def _(i):
        finish(i)

    def longer(j, now, before, before2):
        mixed = [tap(sw2, 0, p) * now[p] + tap(sw2, 1, p) * before[p] + tap(sw2, 2, p) * before2[p] for p in range(3)]
        q32[rows(j), :] = mixed[0]
        uext[rows(j), :] = mixed[1] * mixed[2]

    @pl.loop(2, STEPS)
    def _(j):
        longer(
            j,
            [acc[p, rows(j), :] for p in range(3)],
            [acc[p, rows(j - 1), :] for p in range(3)],
            [acc[p, rows(j - 2), :] for p in range(3)],
        )

    arrived(ltail, hr.at[2])
    edge1, edge2 = [], []
    for p in range(3):
        got = ltail[p].astype(F32) * live
        edge2.append(jnp.where(first, pltpu.roll(got[:SEGS], 5, 0), pltpu.roll(acc[p, rows(62), :], 1, 0)))
        edge1.append(jnp.where(first, pltpu.roll(got[SEGS:], 5, 0), pltpu.roll(acc[p, rows(63), :], 1, 0)))
    y0 = [acc[p, rows(0), :] for p in range(3)]
    y1 = [acc[p, rows(1), :] for p in range(3)]
    longer(0, y0, edge1, edge2)
    longer(1, y1, y0, edge1)

    def row_of(ref, n, lane):
        return jnp.broadcast_to(ref[n : n + 1, lane], (SEGS, LANES))

    @pl.loop(0, WIDTH // LANES)
    def _(lt):
        lane = lanes(lt)
        decay = [jnp.exp(-row_of(rate, n, lane)) for n in range(POLES)]

        def step(i, states):
            for k in range(4):
                u = uext[rows(4 * i + k), lane]
                states = [decay[n] * states[n] + u for n in range(POLES)]
            return tuple(states)

        states = lax.fori_loop(0, STEPS // 4, step, tuple(jnp.zeros((SEGS, LANES), F32) for _ in range(POLES)))
        for n in range(POLES):
            est[rows(n), lane] = states[n]
            decays[rows(n), lane] = decay[n]

    place = seg1 % 4

    @pl.loop(0, WIDTH // LANES)
    def _(lt):
        lane = lanes(lt)
        for g in range(2):
            packed = []
            for h in range(2):
                total = jnp.zeros((SEGS, LANES), F32)
                for r in range(4):
                    n = g * 8 + h * 4 + r
                    span = jnp.exp(-float(STEPS) * row_of(rate, n, lane))
                    value = est[rows(n), lane]
                    value = value + span * jnp.where(place >= 1, pltpu.roll(value, 1, 0), 0.0)
                    value = value + span * span * jnp.where(place >= 2, pltpu.roll(value, 2, 0), 0.0)
                    est[rows(n), lane] = jnp.where(place >= 1, pltpu.roll(value, 1, 0), 0.0)
                    end = value if r == 3 else pltpu.roll(value, (r - 3) % 8, 0)
                    total = jnp.where(place == r, end, total)
                packed.append(total)
            st_s[pl.ds(g * 16, 16), lane] = jnp.concatenate(packed, axis=0).astype(BF16)

    def state_copy(d):
        return remote(st_s, st_r.at[d - 1], sts.at[d - 1], strv.at[d - 1], c + d, t)

    for d in range(15, 0, -1):

        @pl.when(c + d < 16)
        def _(d=d):
            state_copy(d).start()

    @pl.loop(0, WIDTH // LANES)
    def _(lt):
        lane = lanes(lt)
        for n in range(POLES):
            weights[rows(n), lane] = row_of(resid, n, lane) * jnp.sqrt(1.0 - jnp.exp(-2.0 * row_of(rate, n, lane)))

    packs = []
    for g in range(4):
        total = jnp.zeros((SEGS, WIDTH), F32)
        for r in range(4):
            n = g * 4 + r
            total = jnp.where(seg % 4 == r, jnp.broadcast_to(rate[n : n + 1, :], (SEGS, WIDTH)), total)
        packs.append(total)
    pack = jnp.concatenate(packs, axis=0)
    hin[...] = jnp.zeros((4 * SEGS, WIDTH), F32)
    for d in range(1, 16):

        @pl.when(c - d >= 0)
        def _(d=d):
            arrived(st_r.at[d - 1], strv.at[d - 1])
            hin[...] += jnp.exp(pack * (-256.0 * (d - 1))) * st_r[d - 1].astype(F32)

    for part in range(2):

        @pl.loop(0, WIDTH // LANES)
        def _(lt, part=part):
            lane = lanes(lt)
            decay, weight, states = [], [], []
            for n in range(POLES):
                decay.append(decays[rows(n), lane])
                weight.append(weights[rows(n), lane])
                state = est[rows(n), lane]
                if part == 0:
                    r = row_of(rate, n, lane)
                    k = (n // 4) * SEGS + n % 4
                    enter = jnp.where(
                        seg1 < 4,
                        jnp.broadcast_to(hin[k : k + 1, lane], (SEGS, LANES)),
                        jnp.broadcast_to(hin[k + 4 : k + 5, lane], (SEGS, LANES)),
                    )
                    state = state + jnp.exp(r * (place.astype(F32) * (-float(STEPS)))) * enter
                states.append(state)
            skip = jnp.broadcast_to(skip2[:, lane], (SEGS, LANES))

            def step(i, states):
                values = []
                for k in range(4):
                    j = part * (STEPS // 2) + 4 * i + k
                    u = uext[rows(j), lane]
                    states = [decay[n] * states[n] + u for n in range(POLES)]
                    terms = [weight[n] * states[n] for n in range(POLES)]
                    while len(terms) > 1:
                        terms = [terms[a] + terms[a + 1] for a in range(0, len(terms), 2)]
                    values.append(q32[rows(j), lane] * (terms[0] + skip * u))
                zo[1, part, pl.ds(pl.multiple_of(i * 32, 32), 32), lane] = jnp.concatenate(values, axis=0).astype(BF16)
                return tuple(states)

            states = lax.fori_loop(0, STEPS // 8, step, tuple(states))
            if part == 0:
                for n in range(POLES):
                    est[rows(n), lane] = states[n]

        z_copy(1, part).start()

    project(1)
    for part in range(2):
        project_wait(1, part)

        @pl.loop(0, 16)
        def _(i, part=part):
            base = mid[t, part * 2 + i // 8, pl.ds(pl.multiple_of((i % 8) * 16, 16), 16), :].astype(F32)
            value = base + arrivals(1, part, i)
            j = part * (STEPS // 2) + 2 * i
            for k in range(WIDTH // LANES):
                piece = value[:, LANES * k : LANES * (k + 1)]
                x32[2, k, pl.ds(j, SEGS, stride=STEPS), :] = piece[:SEGS]
                x32[2, k, pl.ds(j + 1, SEGS, stride=STEPS), :] = piece[SEGS:]

        @pl.loop(0, 8)
        def _(i, part=part):
            here = pl.ds(pl.multiple_of(i * STEPS + part * 32, 32), 32)
            there = pl.ds(pl.multiple_of(i % 4 * STEPS + part * 32, 32), 32)
            value = jnp.concatenate([x32[2, k, here, :] for k in range(WIDTH // LANES)], axis=1)
            obf[i // 4, there, :] = value.astype(BF16)

    store = pltpu.make_async_copy(obf, out_h, loc.at[3])
    store.start()

    tail_copy.wait_send()
    u_copy.wait_send()
    l_copy.wait_send()
    weight_drain(0, wo1_h)
    weight_drain(1, wo2_h)
    project_drain(0)
    project_drain(1)
    for copy in sent:
        copy.wait_send()
    for d in range(1, 16):

        @pl.when(c + d < 16)
        def _(d=d):
            state_copy(d).wait_send()

    store.wait()


def local(
    residual_in, mr_qkv, mr_short_w, mr_filter, mr_skip, mr_out_w, lr_gain,
    lr_in_w, lr_short_w, lr_rate, lr_res, lr_skip, lr_out_w,
):
    vmem = pl.BlockSpec(memory_space=pltpu.VMEM)
    hbm = pl.BlockSpec(memory_space=pl.ANY)
    dma = pltpu.SemaphoreType.DMA
    scratch = [
        pltpu.VMEM((2, 3, 256, WIDTH), BF16),
        pltpu.VMEM((2, 3, 8, WIDTH), BF16),
        pltpu.VMEM((3, WIDTH // LANES, ROWS, LANES), F32),
        pltpu.VMEM((ROWS, WIDTH), F32),
        pltpu.VMEM((192 * SEGS, WIDTH), F32),
        pltpu.VMEM((TAPS * SEGS, WIDTH), F32),
        pltpu.VMEM((256, WIDTH), BF16),
        pltpu.VMEM((256, WIDTH), BF16),
        pltpu.VMEM((2, 2, ROWS // 2, WIDTH), BF16),
        pltpu.VMEM((2, 2, ROWS // 2, WIDTH), BF16),
        pltpu.VMEM((2, 8, 2, WIDTH, 256), BF16),
        pltpu.VMEM((3, 4096, WIDTH), BF16),
        pltpu.VMEM((2, 2, 6, ROWS // 2, 256), BF16),
        pltpu.VMEM((2, 2, 6, ROWS // 2, 256), BF16),
        pltpu.VMEM((ROWS, WIDTH), F32),
        pltpu.VMEM((8, 4, 128, WIDTH), BF16),
        pltpu.VMEM((ROWS, 2 * WIDTH), BF16),
        pltpu.VMEM((3, ROWS, WIDTH), F32),
        pltpu.VMEM((ROWS, LANES), F32),
        pltpu.VMEM((3, 16, WIDTH), BF16),
        pltpu.VMEM((3, 16, WIDTH), BF16),
        pltpu.VMEM((POLES * SEGS, WIDTH), F32),
        pltpu.VMEM((POLES * SEGS, WIDTH), F32),
        pltpu.VMEM((POLES * SEGS, WIDTH), F32),
        pltpu.VMEM((4 * SEGS, WIDTH), BF16),
        pltpu.VMEM((15, 4 * SEGS, WIDTH), BF16),
        pltpu.VMEM((4 * SEGS, WIDTH), F32),
        pltpu.VMEM((2, 256, WIDTH), BF16),
        pltpu.VMEM((2, 256, WIDTH), BF16),
        dma((4,)),
        dma((3,)),
        dma((3,)),
        dma((2, 3)),
        dma((2, 2, 4)),
        dma((2, 8)),
        dma((2, 8, 2)),
        dma((2, 2)),
        dma((2, 2)),
        dma((2, 2, 6)),
        dma((2, 2, 6)),
        dma((32,)),
        dma((8, 4)),
        dma((15,)),
        dma((15,)),
    ]
    return pl.pallas_call(
        kernel,
        out_shape=jax.ShapeDtypeStruct((2, 256, WIDTH), BF16),
        in_specs=[hbm, hbm, vmem, vmem, vmem, hbm, vmem, hbm, vmem, vmem, vmem, vmem, hbm],
        out_specs=hbm,
        scratch_shapes=scratch,
        compiler_params=pltpu.CompilerParams(
            collective_id=0, has_side_effects=True, vmem_limit_bytes=62 * 1024 * 1024
        ),
    )(
        residual_in,
        jnp.transpose(mr_qkv, (0, 2, 1, 3)),
        mr_short_w,
        mr_filter,
        mr_skip.reshape(1, WIDTH),
        mr_out_w,
        lr_gain.reshape(1, 8 * WIDTH),
        jnp.transpose(lr_in_w, (1, 0, 2)),
        lr_short_w,
        lr_rate,
        lr_res,
        lr_skip.reshape(1, WIDTH),
        lr_out_w,
    )


def solution(mesh):
    in_specs = (
        P(None, "ctx", "tp"),
        P(None, "ctx", None, "tp"),
        P(None, None, "tp"),
        P(None, "tp"),
        P("tp"),
        P("tp", "ctx"),
        P(),
        P(None, None, "tp"),
        P(None, None, "tp"),
        P(None, "tp"),
        P(None, "tp"),
        P("tp"),
        P("tp", "ctx"),
    )
    return jax.shard_map(local, mesh=mesh, in_specs=in_specs, out_specs=P(None, "ctx", "tp"), check_vma=False)
```

```python
import jax
import jax.numpy as jnp
from jax import lax
from jax.experimental import pallas as pl
from jax.experimental.pallas import tpu as pltpu
from jax.sharding import PartitionSpec as P

MESH = pl.DeviceIdType.MESH
F32 = jnp.float32
BF16 = jnp.bfloat16

SEGS = 8
STEPS = 64
ROWS = SEGS * STEPS
WIDTH = 512
TAPS = 128
POLES = 16
LANES = 128


def kernel(
    res_h, qkv_h, sw1, filt, skip1, wo1_h, gain, win_h, sw2, rate, resid, skip2, wo2_h,
    out_h,
    qkv_v, xtail, x32, q32, uext, fb, pk_s, pk_r, zo, zn, w, win, ps, pr, pacc, mid, scaled, acc, ssq,
    ltail_s, ltail, est, decays, weights, st_s, st_r, hin, obf, resv,
    loc, hs, hr, wsnd, fsnd, bsnd, wrecv, zs, zr, pss, prs, ags, agr, sts, strv,
):
    c = lax.axis_index("ctx")
    t = lax.axis_index("tp")
    core = c % 2
    m = c // 2
    y = m % 4
    xh = m // 4
    z = t // 2
    xl = t % 2
    sib = c + 1 - 2 * core
    xn = t + 1 - 2 * xl

    def ztp(dz, x):
        return ((z + dz) % 4) * 2 + x

    def remote(src, dst, ssem, rsem, ctx, tp):
        return pltpu.make_async_remote_copy(
            src_ref=src,
            dst_ref=dst,
            send_sem=ssem,
            recv_sem=rsem,
            device_id={"ctx": ctx, "tp": tp},
            device_id_type=MESH,
        )

    def arrived(ref, sem):
        pltpu.make_async_copy(ref, ref, sem).wait()

    load_qkv = pltpu.make_async_copy(qkv_h, qkv_v, loc.at[0])
    load_qkv.start()
    load_res = pltpu.make_async_copy(res_h, resv, loc.at[1])
    load_res.start()

    barrier = pltpu.get_barrier_semaphore()

    def greet(ctx, tp):
        pl.semaphore_signal(barrier, inc=1, device_id={"ctx": ctx, "tp": tp}, device_id_type=MESH)

    for d in range(1, 16):
        greet((c + d) % 16, t)
    greet(c, xn)
    greet((c + 8) % 16, xn)
    greet(c, ztp(1, xl))
    greet(c, ztp(3, xl))
    pl.semaphore_wait(barrier, 19)

    tail_copy = remote(qkv_h.at[:, :, 248:256, :], xtail, hs.at[0], hr.at[0], (c + 1) % 16, t)
    tail_copy.start()

    holder = (y + xl) % 2 == 0
    relay = (y + xl) % 2 == 1
    ups = ((y + 1) % 4, (y + 3) % 4)

    def place_of(k, row):
        xs = (xl, 1 - xl, 1 - xl, xl)[k]
        xhs = (xh, xh, 1 - xh, 1 - xh)[k]
        return xs * 4 + xhs * 2 + row // 2

    def ctx_of(h, row):
        return (h * 4 + row) * 2 + core

    def weight_first(stage, source):
        mine = place_of(0, y)
        target = w.at[stage, mine, core]
        arrival = wrecv.at[stage, mine, core]
        home = pltpu.make_async_copy(source, target, arrival)
        along = [
            remote(source, target, wsnd.at[stage, 0], arrival, ctx_of(xh, ups[0]), t),
            remote(source, target, wsnd.at[stage, 1], arrival, ctx_of(xh, ups[1]), t),
            remote(source, target, wsnd.at[stage, 2], arrival, ctx_of(1 - xh, y), t),
        ]
        across = [
            remote(source, target, wsnd.at[stage, 0], arrival, c, xn),
            remote(source, target, wsnd.at[stage, 1], arrival, ctx_of(1 - xh, y), xn),
        ]
        return home, along, across

    def weight_start(stage, source):
        home, along, across = weight_first(stage, source)

        @pl.when(holder)
        def _():
            home.start()
            for copy in along:
                copy.start()

        @pl.when(relay)
        def _():
            for copy in across:
                copy.start()

    def weight_pass(stage, index, sem, ctx):
        block = w.at[stage, index, core]
        return remote(block, block, sem, wrecv.at[stage, index, core], ctx, t)

    def weight_pass_half(stage, index, half, sem, ctx):
        block = w.at[stage, index, core, 256 * half : 256 * (half + 1), :]
        return remote(block, block, sem, wrecv.at[stage, index, core], ctx, t)

    def weight_got(stage, index):
        arrived(w.at[stage, index, core], wrecv.at[stage, index, core])

    def weight_moves(stage, k):
        here, up, down, far = place_of(k, y), place_of(k, ups[0]), place_of(k, ups[1]), place_of(k, (y + 2) % 4)

        def sibling(index, n):
            return weight_pass(stage, index, bsnd.at[stage, n], sib)

        held = [sibling(here, k)]
        if k:
            held += [weight_pass(stage, here, fsnd.at[stage, n, k], ctx_of(xh, ups[n])) for n in range(2)]
        late = [sibling(far, 4 + k)]
        below = [sibling(down, k), weight_pass_half(stage, down, 0, fsnd.at[stage, 0, k], ctx_of(xh, ups[0]))]
        above = [sibling(up, 4 + k), weight_pass_half(stage, up, 1, fsnd.at[stage, 1, k], ctx_of(xh, ups[1]))]
        return (here, held), (far, late), (down, below), (up, above)

    def weight_hold(stage, *ks):
        @pl.when(holder)
        def _():
            for k in ks:
                first_ = weight_moves(stage, k)[0]
                weight_got(stage, first_[0])
                for copy in reversed(first_[1]):
                    copy.start()

    def weight_relay(stage, k):
        _, _, below, above = weight_moves(stage, k)

        @pl.when(relay)
        def _():
            for index, copies in (below, above):
                weight_got(stage, index)
                for copy in reversed(copies):
                    copy.start()

    def weight_late(stage, *ks):
        @pl.when(holder)
        def _():
            for k in ks:
                _, (index, copies), _, _ = weight_moves(stage, k)
                weight_got(stage, index)
                copies[0].start()

    def weight_sibling(stage, index):
        arrived(w.at[stage, index, 1 - core], wrecv.at[stage, index, 1 - core])

    def weight_drain(stage, source):
        _, along, across = weight_first(stage, source)

        @pl.when(holder)
        def _():
            for copy in along:
                copy.wait_send()
            for k in range(4):
                first_, late, _, _ = weight_moves(stage, k)
                for copy in first_[1] + late[1]:
                    copy.wait_send()

        @pl.when(relay)
        def _():
            for copy in across:
                copy.wait_send()
            for k in range(4):
                _, _, below, above = weight_moves(stage, k)
                for copy in below[1] + above[1]:
                    copy.wait_send()

    weight_start(0, wo1_h)
    load_win = pltpu.make_async_copy(win_h, win, loc.at[2])

    seg = lax.broadcasted_iota(jnp.int32, (SEGS, WIDTH), 0)
    seg1 = lax.broadcasted_iota(jnp.int32, (SEGS, LANES), 0)
    first = seg % 4 == 0
    live = jnp.where(c > 0, 1.0, 0.0).astype(F32)

    def rows(j, count=1):
        start = j * SEGS
        return pl.ds(start if isinstance(start, int) else pl.multiple_of(start, SEGS), count * SEGS)

    def lanes(lt):
        return pl.ds(pl.multiple_of(lt * LANES, LANES), LANES)

    @pl.loop(0, TAPS // 8)
    def _(i):
        taps = filt[pl.ds(pl.multiple_of(i * 8, 8), 8), :].astype(F32)
        for k in range(8):
            fb[rows(i * 8 + k), :] = jnp.broadcast_to(taps[k : k + 1, :], (SEGS, WIDTH))

    load_qkv.wait()
    for s in range(2):
        for p in range(3):

            @pl.loop(0, 16)
            def _(i, s=s, p=p):
                here = pl.ds(pl.multiple_of(i * 16, 16), 16)
                there = pl.ds(pl.multiple_of(s * 256 + i * 16, 16), 16)
                values = qkv_v[s, p, here, :].astype(F32)
                for k in range(WIDTH // LANES):
                    x32[p, k, there, :] = values[:, LANES * k : LANES * (k + 1)]

    def tap(ref, lag, p):
        return jnp.broadcast_to(ref[lag, p : p + 1, :], (SEGS, WIDTH))

    def strided3(p, j):
        return jnp.concatenate(
            [x32[p, k, pl.ds(j, SEGS, stride=STEPS), :] for k in range(WIDTH // LANES)], axis=1
        )

    def medium(j, now, before, before2):
        mixed = [tap(sw1, 0, p) * now[p] + tap(sw1, 1, p) * before[p] + tap(sw1, 2, p) * before2[p] for p in range(3)]
        q32[rows(j), :] = mixed[0]
        uext[rows(j + 128), :] = (mixed[1] * mixed[2]).astype(BF16).astype(F32)

    last = [strided3(p, 63) for p in range(3)]
    last2 = [strided3(p, 62) for p in range(3)]
    x0 = [strided3(p, 0) for p in range(3)]
    x1 = [strided3(p, 1) for p in range(3)]
    own1 = [jnp.where(first, 0.0, pltpu.roll(v, 1, 0)) for v in last]
    own2 = [jnp.where(first, 0.0, pltpu.roll(v, 1, 0)) for v in last2]
    medium(0, x0, own1, own2)
    medium(1, x1, x0, own1)

    def medium_step(j, carried):
        now = [strided3(p, j) for p in range(3)]
        before, before2 = carried
        medium(j, now, before, before2)
        return now, before

    lax.fori_loop(2, STEPS, medium_step, (x1, x0))

    @pl.loop(0, STEPS // 4)
    def _(i):
        packed = []
        for k in range(2):
            even = uext[rows(128 + 4 * i + 2 * k), :]
            odd = uext[rows(129 + 4 * i + 2 * k), :]
            packed.append(jnp.where(seg % 4 >= 2, even, pltpu.roll(odd, 6, 0)))
        pk_s[pl.ds(pl.multiple_of(i * 16, 16), 16), :] = jnp.concatenate(packed, axis=0).astype(BF16)

    u_copy = remote(pk_s, pk_r, hs.at[1], hr.at[1], (c + 1) % 16, t)
    u_copy.start()
    weight_hold(0, 0, 1, 2)
    weight_relay(0, 0)

    arrived(xtail, hr.at[0])

    def halo(p, row):
        top = xtail[0, p].astype(F32)[row : row + 1, :] * live
        bottom = xtail[1, p].astype(F32)[row : row + 1, :] * live
        return jnp.where(seg < 4, jnp.broadcast_to(top, (SEGS, WIDTH)), jnp.broadcast_to(bottom, (SEGS, WIDTH)))

    full1 = [jnp.where(first, halo(p, 7), own1[p]) for p in range(3)]
    full2 = [jnp.where(first, halo(p, 6), own2[p]) for p in range(3)]
    medium(0, x0, full1, full2)
    medium(1, x1, x0, full1)

    load_win.start()
    arrived(pk_r, hr.at[1])

    @pl.loop(0, STEPS // 2)
    def _(i):
        both = pk_r[pl.ds(pl.multiple_of((i // 2) * 16, 16), 16), :].astype(F32) * live
        got = jnp.where(i % 2 == 0, both[:SEGS], both[SEGS:])
        even = uext[rows(128 + 2 * i), :]
        odd = uext[rows(129 + 2 * i), :]
        uext[rows(64 + 2 * i), :] = jnp.where(first, pltpu.roll(got, 5, 0), pltpu.roll(even, 1, 0))
        uext[rows(65 + 2 * i), :] = jnp.where(first, pltpu.roll(got, 7, 0), pltpu.roll(odd, 1, 0))
        uext[rows(2 * i), :] = jnp.where(seg % 4 < 2, pltpu.roll(got, 6, 0), pltpu.roll(even, 2, 0))
        uext[rows(1 + 2 * i), :] = jnp.where(seg % 4 < 2, got, pltpu.roll(odd, 2, 0))


    HALF = ROWS // 2

    def z_copy(stage, part):
        return remote(zo.at[stage, part], zn.at[stage, part], zs.at[stage, part], zr.at[stage, part], c, xn)

    def p_copy(stage, part, i):
        return remote(
            ps.at[stage, part, i],
            pr.at[stage, part, i],
            pss.at[stage, part, i],
            prs.at[stage, part, i],
            c,
            ztp(1 if i % 2 == 0 else 3, xl),
        )

    def term(stage, part, d, half):
        dest = (z + d) % 4
        both = jnp.concatenate([zo[stage, part], zn[stage, part]], axis=1)
        weights = jnp.concatenate([w[stage, xl * 4 + dest, half], w[stage, (1 - xl) * 4 + dest, half]], axis=0)
        return jnp.dot(both, weights, preferred_element_type=F32)

    def project_first(stage, part):
        arrived(zn.at[stage, part], zr.at[stage, part])
        for i, d, half in ((0, 2, 0), (1, 2, 1), (2, 1, 1), (3, 3, 0)):
            if part == 0 and i in (0, 2, 3):
                for source in range(2):
                    weight_sibling(stage, source * 4 + (z + d) % 4)
            ps[stage, part, i] = term(stage, part, d, half).astype(BF16)
            p_copy(stage, part, i).start()

    def project_own(stage, part):
        if part == 0:
            for source in range(2):
                weight_sibling(stage, source * 4 + z)
        for own in range(2):
            pacc[HALF * part : HALF * (part + 1), 256 * own : 256 * (own + 1)] = term(stage, part, 0, own)

    def project_relay(stage, part):
        for i, d, half in ((4, 1, 0), (5, 3, 1)):
            mine = term(stage, part, d, half)
            arrived(pr.at[stage, part, i - 4], prs.at[stage, part, i - 4])
            ps[stage, part, i] = (mine + pr[stage, part, i - 4].astype(F32)).astype(BF16)
            p_copy(stage, part, i).start()

    def project(stage):
        project_first(stage, 0)
        project_first(stage, 1)
        project_relay(stage, 0)
        project_own(stage, 0)
        project_relay(stage, 1)
        project_own(stage, 1)

    def project_wait(stage, part):
        for i in (2, 3, 4, 5):
            arrived(pr.at[stage, part, i], prs.at[stage, part, i])

    def project_drain(stage):
        for part in range(2):
            z_copy(stage, part).wait_send()
            for i in range(6):
                p_copy(stage, part, i).wait_send()

    def arrivals(stage, part, i):
        here = pl.ds(pl.multiple_of(i * 16, 16), 16)
        left = pr[stage, part, 3, here, :].astype(F32) + pr[stage, part, 4, here, :].astype(F32)
        right = pr[stage, part, 2, here, :].astype(F32) + pr[stage, part, 5, here, :].astype(F32)
        own = pacc[pl.ds(pl.multiple_of(part * HALF + i * 16, 16), 16), :]
        return own + jnp.concatenate([left, right], axis=1)

    def filter_blocks(first_block):
        @pl.loop(first_block, first_block + 2)
        def _(block):
            lane = lanes((block % 8) // 2)
            part = block // 8
            r0 = (block % 2) * 16
            j0 = part * 32 + r0

            def taps8(ib, totals):
                base = 128 + j0 - 8 * ib - 7
                window = uext[pl.ds(pl.multiple_of(base * SEGS, SEGS), 23 * SEGS), lane]
                weights = fb[pl.ds(pl.multiple_of(ib * 64, 64), 64), lane]
                totals = list(totals)
                for b in range(8):
                    f = weights[b * SEGS : (b + 1) * SEGS]
                    for a in range(16):
                        k = a + 7 - b
                        totals[a] = totals[a] + f * window[k * SEGS : (k + 1) * SEGS]
                return tuple(totals)

            totals = lax.fori_loop(0, 16, taps8, tuple(jnp.zeros((SEGS, LANES), F32) for _ in range(16)))
            skip = jnp.broadcast_to(skip1[:, lane], (SEGS, LANES))
            for a in range(0, 16, 2):
                pair = []
                for k in (a, a + 1):
                    u = uext[rows(128 + j0 + k), lane]
                    pair.append(q32[rows(j0 + k), lane] * (totals[k] + skip * u))
                zo[0, part, pl.ds(pl.multiple_of((r0 + a) * SEGS, 16), 16), lane] = jnp.concatenate(
                    pair, axis=0
                ).astype(BF16)

    filter_blocks(0)
    filter_blocks(2)
    weight_hold(0, 3)
    weight_relay(0, 1)
    filter_blocks(4)
    filter_blocks(6)
    z_copy(0, 0).start()
    weight_late(0, 0)
    filter_blocks(8)
    weight_relay(0, 2)
    weight_late(0, 1)
    filter_blocks(10)
    filter_blocks(12)
    filter_blocks(14)
    z_copy(0, 1).start()
    weight_relay(0, 3)
    weight_late(0, 2, 3)
    weight_start(1, wo2_h)

    load_res.wait()

    @pl.loop(0, 32)
    def _(i):
        s = i // 16
        r = (i % 16) * 16
        values = resv[s, pl.ds(pl.multiple_of(r, 16), 16), :].astype(F32)
        for k in range(WIDTH // LANES):
            x32[0, k, pl.ds(pl.multiple_of(i * 16, 16), 16), :] = values[:, LANES * k : LANES * (k + 1)]

    @pl.loop(0, STEPS)
    def _(j):
        for k in range(WIDTH // LANES):
            x32[1, k, rows(j), :] = x32[0, k, pl.ds(j, SEGS, stride=STEPS), :]

    project(0)
    weight_hold(1, 0, 1, 2)
    weight_relay(1, 0)

    sent = []

    def send(slot, quarter, tp):
        k = len(sent)
        copy = remote(
            mid.at[slot, quarter], mid.at[slot, quarter], ags.at[k], agr.at[slot, quarter], c, tp
        )
        copy.start()
        sent.append(copy)

    zp, zm, zz = ztp(1, xl), ztp(3, xl), ztp(2, xl)
    xp, xm, xz = ztp(1, 1 - xl), ztp(3, 1 - xl), ztp(2, 1 - xl)
    for part in range(2):
        project_wait(0, part)

        @pl.loop(0, 16)
        def _(i, part=part):
            here = pl.ds(pl.multiple_of(part * HALF + i * 16, 16), 16)
            before = jnp.concatenate([x32[1, k, here, :] for k in range(WIDTH // LANES)], axis=1)
            value = (before + arrivals(0, part, i)).astype(BF16)
            mid[t, part * 2 + i // 8, pl.ds(pl.multiple_of((i % 8) * 16, 16), 16), :] = value

        for quarter in (2 * part, 2 * part + 1):
            send(t, quarter, xn)
            send(t, quarter, zp)
            send(t, quarter, zm)

    def have(slot, *quarters):
        for quarter in quarters:
            arrived(mid.at[slot, quarter], agr.at[slot, quarter])

    load_win.wait()

    def absorb(*slots, fresh=False):
        count = len(slots)
        scales = [gain[:, pl.ds(pl.multiple_of(slot * WIDTH, WIDTH), WIDTH)] for slot in slots]

        @pl.loop(0, 16)
        def _(i):
            here = pl.ds(pl.multiple_of((i % 4) * 32, 32), 32)
            there = pl.ds(pl.multiple_of(i * 32, 32), 32)
            total = 0.0 if fresh else ssq[there, :]
            for k, slot in enumerate(slots):
                values = mid[slot, i // 4, here, :].astype(F32)
                square = values * values
                total += square[:, 0:128] + square[:, 128:256] + square[:, 256:384] + square[:, 384:512]
                scaled[there, WIDTH * k : WIDTH * (k + 1)] = (values * scales[k]).astype(BF16)
            ssq[there, :] = total

        @pl.loop(0, 6)
        def _(i):
            cols = pl.ds(pl.multiple_of((i % 2) * 256, 256), 256)
            weights = [win[i // 2, pl.ds(pl.multiple_of(slot * WIDTH, WIDTH), WIDTH), cols] for slot in slots]
            product = jnp.dot(
                scaled[:, 0 : WIDTH * count], jnp.concatenate(weights, axis=0), preferred_element_type=F32
            )
            acc[i // 2, :, cols] = product if fresh else acc[i // 2, :, cols] + product

    absorb(t, fresh=True)
    weight_hold(1, 3)
    weight_relay(1, 1)
    have(xn, 0, 1)
    for quarter in range(2):
        send(xn, quarter, zp)
        send(xn, quarter, zm)
    have(zm, 0, 1, 2, 3)
    send(zm, 0, zp)
    send(zm, 2, zp)
    send(zm, 2, xn)
    send(zm, 3, xn)
    have(zp, 0, 1, 2, 3)
    send(zp, 1, zm)
    send(zp, 3, zm)
    send(zp, 2, xn)
    send(zp, 3, xn)
    absorb(zm, zp)
    weight_relay(1, 2)
    have(xm, 0, 1)
    send(xm, 0, zp)
    have(xp, 0, 1)
    send(xp, 1, zm)
    have(zz, 0, 1, 2, 3)
    send(zz, 2, xn)
    send(zz, 3, xn)
    have(xn, 2, 3)
    absorb(xn, zz)
    weight_relay(1, 3)
    have(xm, 2, 3)
    have(xp, 2, 3)
    absorb(xm, xp)
    have(xz, 0, 1, 2, 3)
    absorb(xz)
    weight_late(1, 0, 1, 2, 3)

    def finish(i):
        here = pl.ds(i * 16 if isinstance(i, int) else pl.multiple_of(i * 16, 16), 16)
        meansq = jnp.sum(ssq[here, :], axis=1, keepdims=True) * (1.0 / 4096.0)
        factor = lax.rsqrt(meansq + 1e-6)
        values = [(acc[p, here, :] * factor).astype(BF16) for p in range(3)]
        for p in range(3):
            acc[p, here, :] = values[p].astype(F32)
        return values

    tails = finish(31)
    for p in range(3):
        ltail_s[p] = tails[p]
    l_copy = remote(ltail_s, ltail, hs.at[2], hr.at[2], (c + 1) % 16, t)
    l_copy.start()

    @pl.loop(0, 31)
    def _(i):
        finish(i)

    def longer(j, now, before, before2):
        mixed = [tap(sw2, 0, p) * now[p] + tap(sw2, 1, p) * before[p] + tap(sw2, 2, p) * before2[p] for p in range(3)]
        q32[rows(j), :] = mixed[0]
        uext[rows(j), :] = mixed[1] * mixed[2]

    @pl.loop(2, STEPS)
    def _(j):
        longer(
            j,
            [acc[p, rows(j), :] for p in range(3)],
            [acc[p, rows(j - 1), :] for p in range(3)],
            [acc[p, rows(j - 2), :] for p in range(3)],
        )

    arrived(ltail, hr.at[2])
    edge1, edge2 = [], []
    for p in range(3):
        got = ltail[p].astype(F32) * live
        edge2.append(jnp.where(first, pltpu.roll(got[:SEGS], 5, 0), pltpu.roll(acc[p, rows(62), :], 1, 0)))
        edge1.append(jnp.where(first, pltpu.roll(got[SEGS:], 5, 0), pltpu.roll(acc[p, rows(63), :], 1, 0)))
    y0 = [acc[p, rows(0), :] for p in range(3)]
    y1 = [acc[p, rows(1), :] for p in range(3)]
    longer(0, y0, edge1, edge2)
    longer(1, y1, y0, edge1)

    def row_of(ref, n, lane):
        return jnp.broadcast_to(ref[n : n + 1, lane], (SEGS, LANES))

    @pl.loop(0, WIDTH // LANES)
    def _(lt):
        lane = lanes(lt)
        decay = [jnp.exp(-row_of(rate, n, lane)) for n in range(POLES)]

        def step(i, states):
            for k in range(4):
                u = uext[rows(4 * i + k), lane]
                states = [decay[n] * states[n] + u for n in range(POLES)]
            return tuple(states)

        states = lax.fori_loop(0, STEPS // 4, step, tuple(jnp.zeros((SEGS, LANES), F32) for _ in range(POLES)))
        for n in range(POLES):
            est[rows(n), lane] = states[n]
            decays[rows(n), lane] = decay[n]

    place = seg1 % 4

    @pl.loop(0, WIDTH // LANES)
    def _(lt):
        lane = lanes(lt)
        for g in range(2):
            packed = []
            for h in range(2):
                total = jnp.zeros((SEGS, LANES), F32)
                for r in range(4):
                    n = g * 8 + h * 4 + r
                    span = jnp.exp(-float(STEPS) * row_of(rate, n, lane))
                    value = est[rows(n), lane]
                    value = value + span * jnp.where(place >= 1, pltpu.roll(value, 1, 0), 0.0)
                    value = value + span * span * jnp.where(place >= 2, pltpu.roll(value, 2, 0), 0.0)
                    est[rows(n), lane] = jnp.where(place >= 1, pltpu.roll(value, 1, 0), 0.0)
                    end = value if r == 3 else pltpu.roll(value, (r - 3) % 8, 0)
                    total = jnp.where(place == r, end, total)
                packed.append(total)
            st_s[pl.ds(g * 16, 16), lane] = jnp.concatenate(packed, axis=0).astype(BF16)

    def state_copy(d):
        return remote(st_s, st_r.at[d - 1], sts.at[d - 1], strv.at[d - 1], c + d, t)

    for d in range(15, 0, -1):

        @pl.when(c + d < 16)
        def _(d=d):
            state_copy(d).start()

    @pl.loop(0, WIDTH // LANES)
    def _(lt):
        lane = lanes(lt)
        for n in range(POLES):
            weights[rows(n), lane] = row_of(resid, n, lane) * jnp.sqrt(1.0 - jnp.exp(-2.0 * row_of(rate, n, lane)))

    packs = []
    for g in range(4):
        total = jnp.zeros((SEGS, WIDTH), F32)
        for r in range(4):
            n = g * 4 + r
            total = jnp.where(seg % 4 == r, jnp.broadcast_to(rate[n : n + 1, :], (SEGS, WIDTH)), total)
        packs.append(total)
    pack = jnp.concatenate(packs, axis=0)
    hin[...] = jnp.zeros((4 * SEGS, WIDTH), F32)
    for d in range(1, 16):

        @pl.when(c - d >= 0)
        def _(d=d):
            arrived(st_r.at[d - 1], strv.at[d - 1])
            hin[...] += jnp.exp(pack * (-256.0 * (d - 1))) * st_r[d - 1].astype(F32)

    for part in range(2):

        @pl.loop(0, WIDTH // LANES)
        def _(lt, part=part):
            lane = lanes(lt)
            decay, weight, states = [], [], []
            for n in range(POLES):
                decay.append(decays[rows(n), lane])
                weight.append(weights[rows(n), lane])
                state = est[rows(n), lane]
                if part == 0:
                    r = row_of(rate, n, lane)
                    k = (n // 4) * SEGS + n % 4
                    enter = jnp.where(
                        seg1 < 4,
                        jnp.broadcast_to(hin[k : k + 1, lane], (SEGS, LANES)),
                        jnp.broadcast_to(hin[k + 4 : k + 5, lane], (SEGS, LANES)),
                    )
                    state = state + jnp.exp(r * (place.astype(F32) * (-float(STEPS)))) * enter
                states.append(state)
            skip = jnp.broadcast_to(skip2[:, lane], (SEGS, LANES))

            def step(i, states):
                values = []
                for k in range(4):
                    j = part * (STEPS // 2) + 4 * i + k
                    u = uext[rows(j), lane]
                    states = [decay[n] * states[n] + u for n in range(POLES)]
                    terms = [weight[n] * states[n] for n in range(POLES)]
                    while len(terms) > 1:
                        terms = [terms[a] + terms[a + 1] for a in range(0, len(terms), 2)]
                    values.append(q32[rows(j), lane] * (terms[0] + skip * u))
                zo[1, part, pl.ds(pl.multiple_of(i * 32, 32), 32), lane] = jnp.concatenate(values, axis=0).astype(BF16)
                return tuple(states)

            states = lax.fori_loop(0, STEPS // 8, step, tuple(states))
            if part == 0:
                for n in range(POLES):
                    est[rows(n), lane] = states[n]

        z_copy(1, part).start()

    project(1)
    for part in range(2):
        project_wait(1, part)

        @pl.loop(0, 16)
        def _(i, part=part):
            base = mid[t, part * 2 + i // 8, pl.ds(pl.multiple_of((i % 8) * 16, 16), 16), :].astype(F32)
            value = base + arrivals(1, part, i)
            j = part * (STEPS // 2) + 2 * i
            for k in range(WIDTH // LANES):
                piece = value[:, LANES * k : LANES * (k + 1)]
                x32[2, k, pl.ds(j, SEGS, stride=STEPS), :] = piece[:SEGS]
                x32[2, k, pl.ds(j + 1, SEGS, stride=STEPS), :] = piece[SEGS:]

        @pl.loop(0, 8)
        def _(i, part=part):
            here = pl.ds(pl.multiple_of(i * STEPS + part * 32, 32), 32)
            there = pl.ds(pl.multiple_of(i % 4 * STEPS + part * 32, 32), 32)
            value = jnp.concatenate([x32[2, k, here, :] for k in range(WIDTH // LANES)], axis=1)
            obf[i // 4, there, :] = value.astype(BF16)

    store = pltpu.make_async_copy(obf, out_h, loc.at[3])
    store.start()

    tail_copy.wait_send()
    u_copy.wait_send()
    l_copy.wait_send()
    weight_drain(0, wo1_h)
    weight_drain(1, wo2_h)
    project_drain(0)
    project_drain(1)
    for copy in sent:
        copy.wait_send()
    for d in range(1, 16):

        @pl.when(c + d < 16)
        def _(d=d):
            state_copy(d).wait_send()

    store.wait()


def local(
    residual_in, mr_qkv, mr_short_w, mr_filter, mr_skip, mr_out_w, lr_gain,
    lr_in_w, lr_short_w, lr_rate, lr_res, lr_skip, lr_out_w,
):
    vmem = pl.BlockSpec(memory_space=pltpu.VMEM)
    hbm = pl.BlockSpec(memory_space=pl.ANY)
    dma = pltpu.SemaphoreType.DMA
    scratch = [
        pltpu.VMEM((2, 3, 256, WIDTH), BF16),
        pltpu.VMEM((2, 3, 8, WIDTH), BF16),
        pltpu.VMEM((3, WIDTH // LANES, ROWS, LANES), F32),
        pltpu.VMEM((ROWS, WIDTH), F32),
        pltpu.VMEM((192 * SEGS, WIDTH), F32),
        pltpu.VMEM((TAPS * SEGS, WIDTH), F32),
        pltpu.VMEM((256, WIDTH), BF16),
        pltpu.VMEM((256, WIDTH), BF16),
        pltpu.VMEM((2, 2, ROWS // 2, WIDTH), BF16),
        pltpu.VMEM((2, 2, ROWS // 2, WIDTH), BF16),
        pltpu.VMEM((2, 8, 2, WIDTH, 256), BF16),
        pltpu.VMEM((3, 4096, WIDTH), BF16),
        pltpu.VMEM((2, 2, 6, ROWS // 2, 256), BF16),
        pltpu.VMEM((2, 2, 6, ROWS // 2, 256), BF16),
        pltpu.VMEM((ROWS, WIDTH), F32),
        pltpu.VMEM((8, 4, 128, WIDTH), BF16),
        pltpu.VMEM((ROWS, 2 * WIDTH), BF16),
        pltpu.VMEM((3, ROWS, WIDTH), F32),
        pltpu.VMEM((ROWS, LANES), F32),
        pltpu.VMEM((3, 16, WIDTH), BF16),
        pltpu.VMEM((3, 16, WIDTH), BF16),
        pltpu.VMEM((POLES * SEGS, WIDTH), F32),
        pltpu.VMEM((POLES * SEGS, WIDTH), F32),
        pltpu.VMEM((POLES * SEGS, WIDTH), F32),
        pltpu.VMEM((4 * SEGS, WIDTH), BF16),
        pltpu.VMEM((15, 4 * SEGS, WIDTH), BF16),
        pltpu.VMEM((4 * SEGS, WIDTH), F32),
        pltpu.VMEM((2, 256, WIDTH), BF16),
        pltpu.VMEM((2, 256, WIDTH), BF16),
        dma((4,)),
        dma((3,)),
        dma((3,)),
        dma((2, 3)),
        dma((2, 2, 4)),
        dma((2, 8)),
        dma((2, 8, 2)),
        dma((2, 2)),
        dma((2, 2)),
        dma((2, 2, 6)),
        dma((2, 2, 6)),
        dma((32,)),
        dma((8, 4)),
        dma((15,)),
        dma((15,)),
    ]
    return pl.pallas_call(
        kernel,
        out_shape=jax.ShapeDtypeStruct((2, 256, WIDTH), BF16),
        in_specs=[hbm, hbm, vmem, vmem, vmem, hbm, vmem, hbm, vmem, vmem, vmem, vmem, hbm],
        out_specs=hbm,
        scratch_shapes=scratch,
        compiler_params=pltpu.CompilerParams(
            collective_id=0, has_side_effects=True, vmem_limit_bytes=62 * 1024 * 1024
        ),
    )(
        residual_in,
        jnp.transpose(mr_qkv, (0, 2, 1, 3)),
        mr_short_w,
        mr_filter,
        mr_skip.reshape(1, WIDTH),
        mr_out_w,
        lr_gain.reshape(1, 8 * WIDTH),
        jnp.transpose(lr_in_w, (1, 0, 2)),
        lr_short_w,
        lr_rate,
        lr_res,
        lr_skip.reshape(1, WIDTH),
        lr_out_w,
    )


def solution(mesh):
    in_specs = (
        P(None, "ctx", "tp"),
        P(None, "ctx", None, "tp"),
        P(None, None, "tp"),
        P(None, "tp"),
        P("tp"),
        P("tp", "ctx"),
        P(),
        P(None, None, "tp"),
        P(None, None, "tp"),
        P(None, "tp"),
        P(None, "tp"),
        P("tp"),
        P("tp", "ctx"),
    )
    return jax.shard_map(local, mesh=mesh, in_specs=in_specs, out_specs=P(None, "ctx", "tp"), check_vma=False)
```
